256 devices in a mesh: gz: 8 (over z_lo, x), gy: 8 (over z_hi, core), gx: 4 (over y).
Axes of the slice: x: 4, y: 4, z: 8 (z_hi: 4, z_lo: 2; z = z_hi * 2 + z_lo), core: 2. Of those that a mesh axis runs over, the one named last changes fastest.
Arguments:
- images: bfloat16 [8, 1280, 640], P('gz', 'gy', 'gx'), may hold values from -6 to 6
- tissue_mask: int32 [8, 32, 16], P('gz', 'gy', 'gx'), may hold values 0 or 1
Outputs:
- flow_fields: float32 [4, 8, 32, 16], P(None, 'gz', 'gy', 'gx')
- mesh_offsets: float32 [2, 8, 32, 16], P(None, 'gz', 'gy', 'gx')
The draws below stay inside these ranges and needn't reach their ends.
Inputs may be any that keep to these rules, and one draw needn't show every extreme that they name: `tissue_mask`: 0 or 1 for each patch.
All inputs are finite; a program needn't handle non-finite values. No bound on the sum of `tissue_mask` on one device may be relied on, other than what follows from the above.
Results may differ from the reference program's by a relative error of at most 0.0003.
Values may be sent and summed in bfloat16 or wider, within the bound.
A program may use at most 128 MiB of HBM per device.

```python
import jax
import jax.numpy as jnp
from jax import lax

PATCH = 160
STRIDE = 40
RELAX = 4
SECTIONS = 8
HEIGHT = 1280
WIDTH = 640
NODES_Y = 32
NODES_X = 16


def plant(result, rng, least, top_value):
    index_at = [jax.random.randint(jax.random.fold_in(rng, axis), (), 0, length) for axis, length in enumerate(result.shape)]
    main_axis = result.shape.index(max(result.shape))
    beside = index_at[:main_axis] + [(index_at[main_axis] + 1) % result.shape[main_axis]] + index_at[main_axis + 1:]
    return result.at[tuple(index_at)].set(least).at[tuple(beside)].set(top_value)


def level_of(key, dims, cuts, least, largest):
    level = 1.0
    for dim, blocks in cuts:
        draws = jax.random.uniform(jax.random.fold_in(jax.random.fold_in(key, 6), dim), (blocks,), jnp.float32, least / len(cuts), largest / len(cuts))
        level = level * jnp.repeat(jnp.exp(draws), dims[dim] // blocks).reshape((-1,) + (1,) * (len(dims) - 1 - dim))
    return level


def normal_values(key, shape, width, limit, shards=(), held_as=jnp.bfloat16):
    values = width * jax.random.normal(key, shape, jnp.float32)
    if shards:
        values = values * level_of(key, shape, shards, -0.22, 0.18)
    return jnp.clip(values, -limit, limit).astype(held_as)


def setup_inputs(seed: int = 0) -> dict:
    keys = jax.random.split(jax.random.key(seed), 3)
    return {
        "images": normal_values(keys[0], (SECTIONS, HEIGHT, WIDTH), 1.0, 6.0, ((0, 8), (1, 8), (2, 4))),
        "tissue_mask": plant((jax.random.randint(keys[1], (SECTIONS, NODES_Y, NODES_X), 0, 4) < 3).astype(jnp.int32), jax.random.fold_in(keys[1], 1), 0, 1),
    }


EPSILON = 1e-6
STIFFNESS = 0.5
STEP_SIZE = 0.2


def windows(section):
    repeats = PATCH // STRIDE
    count_y = section.shape[0] // STRIDE - repeats + 1
    count_x = section.shape[1] // STRIDE - repeats + 1
    blocks = section.reshape(section.shape[0] // STRIDE, STRIDE, section.shape[1] // STRIDE, STRIDE)
    pieces = []
    for first in range(repeats):
        row_pieces = [blocks[first:first + count_y, :, second:second + count_x, :] for second in range(repeats)]
        pieces.append(jnp.stack(row_pieces, 0))
    stacked = jnp.stack(pieces, 0)
    stacked = jnp.transpose(stacked, (2, 4, 0, 3, 1, 5))
    return stacked.reshape(count_y * count_x, PATCH, PATCH)


def centroid(correl):
    squared = correl * correl
    weights = squared * squared
    totals = jnp.sum(weights, axis=(1, 2)) + EPSILON
    shifts = ((jnp.arange(PATCH, dtype=jnp.int32) + PATCH // 2) % PATCH - PATCH // 2).astype(jnp.float32)
    flow_y = jnp.sum(weights * shifts[None, :, None], axis=(1, 2)) / totals
    flow_x = jnp.sum(weights * shifts[None, None, :], axis=(1, 2)) / totals
    return flow_y, flow_x


def upward(fields, distance):
    return jnp.pad(fields[:, distance:], ((0, 0), (0, distance), (0, 0), (0, 0)))


def downward(fields, distance):
    return jnp.pad(fields[:, :SECTIONS - distance], ((0, 0), (distance, 0), (0, 0), (0, 0)))


def reference(images, tissue_mask):
    margin = (PATCH - STRIDE) // 2
    nodes_y = HEIGHT // STRIDE
    nodes_x = WIDTH // STRIDE
    padded = jnp.pad(images.astype(jnp.float32), ((0, 2), (margin, margin), (margin, margin)))

    def spectra_of(position):
        section = lax.dynamic_index_in_dim(padded, position, 0, keepdims=False)
        return jnp.fft.fft2(windows(section))

    def section_flows(position):
        own_spec = spectra_of(position)
        results = []
        for distance in (1, 2):
            others = spectra_of(position + distance)
            correl = jnp.real(jnp.fft.ifft2(others * jnp.conj(own_spec))).astype(jnp.float32)
            flow_y, flow_x = centroid(correl)
            results.append(flow_y)
            results.append(flow_x)
        return jnp.stack(results, 0)

    flow_all = lax.map(section_flows, jnp.arange(SECTIONS, dtype=jnp.int32))
    flow_fields = jnp.transpose(flow_all, (1, 0, 2)).reshape(4, SECTIONS, nodes_y, nodes_x)
    mask_float = tissue_mask.astype(jnp.float32)
    mask_padded = jnp.pad(mask_float, ((0, 2), (0, 0), (0, 0)))
    weight_one = (mask_float * mask_padded[1:SECTIONS + 1])[None]
    weight_two = (mask_float * mask_padded[2:SECTIONS + 2])[None]
    flow_one = flow_fields[0:2]
    flow_two = flow_fields[2:4]
    low_weight_one = downward(weight_one, 1)
    low_weight_two = downward(weight_two, 2)
    low_flow_one = downward(flow_one, 1)
    low_flow_two = downward(flow_two, 2)
    offsets = jnp.zeros((2, SECTIONS, nodes_y, nodes_x), jnp.float32)
    for _ in range(RELAX):
        widened = jnp.pad(offsets, ((0, 0), (0, 0), (1, 1), (1, 1)))
        laplace = (widened[:, :, :-2, 1:-1] + widened[:, :, 2:, 1:-1] + widened[:, :, 1:-1, :-2]
                   + widened[:, :, 1:-1, 2:] - 4.0 * offsets)
        forces = STIFFNESS * laplace
        forces = forces + weight_one * (upward(offsets, 1) - offsets - flow_one)
        forces = forces + weight_two * (upward(offsets, 2) - offsets - flow_two)
        forces = forces - low_weight_one * (offsets - downward(offsets, 1) - low_flow_one)
        forces = forces - low_weight_two * (offsets - downward(offsets, 2) - low_flow_two)
        offsets = offsets + STEP_SIZE * forces
    return flow_fields, offsets
```

```python
import functools
import math

import jax
import jax.numpy as jnp
import numpy as np
from jax import lax
from jax.experimental import pallas as pl
from jax.experimental.pallas import tpu as pltpu
from jax.sharding import PartitionSpec as P

PATCH = 160
STRIDE = 40
RELAX = 4
EPSILON = 1e-06
STIFFNESS = 0.5
STEP_SIZE = 0.2

TILE = 160
HALO = 64
ROWS = TILE + 2 * HALO
LANES = 128
SIN_ROW = 88
FREQ = 168
MESH = pl.DeviceIdType.MESH
DIRECTIONS = [(dy, dx) for dy in (-1, 0, 1) for dx in (-1, 0, 1) if (dy, dx) != (0, 0)]


def split(table):
    table = jnp.asarray(table, jnp.float32)
    high = table.astype(jnp.bfloat16)
    low = (table - high.astype(jnp.float32)).astype(jnp.bfloat16)
    return high, low


def split_np(table):
    bf16 = jnp.bfloat16
    high = np.asarray(table, np.float32).astype(bf16)
    low = (np.asarray(table, np.float64) - high.astype(np.float64)).astype(np.float32).astype(bf16)
    return high, low


def cosine(product):
    return np.cos(2.0 * np.pi * (product % PATCH) / PATCH)


def sine(product):
    phase = product % (PATCH // 2)
    return np.where(phase == 0, 0.0, np.sin(2.0 * np.pi * (product % PATCH) / PATCH))


def column_tables():
    freq = np.arange(81)
    out = []
    for j in range(4):
        lane = np.arange(256)
        if j == 0:
            column = lane - 128
            good = lane >= 0
        elif j == 1:
            column = np.where(lane < 108, 32 + lane, lane - 128)
            good = lane >= 96
        elif j == 2:
            column = np.where(lane < 128, 32 + lane, np.where(lane < 148, 32 + lane, lane - 128))
            good = lane < 160
        else:
            column = 32 + lane
            good = lane >= 0
        m = column - (40 * j - 60)
        good = good & (m >= 0) & (m < PATCH)
        product = m[:, None] * freq[None, :]
        table = np.zeros((256, 256))
        table[:, 0:81] = cosine(product) * good[:, None]
        table[:, 128:209] = sine(product) * good[:, None]
        high, low = split_np(table)
        out.append(np.concatenate([high, low], 0))
    return np.stack(out)


def row_table(i, base):
    row = np.arange(256) + base
    n = row - 4 - 40 * i
    good = (n >= 0) & (n < PATCH)
    table = np.zeros((FREQ, 256))
    table[0:81] = cosine(np.arange(81)[:, None] * n[None]) * good[None]
    table[SIN_ROW : SIN_ROW + 80] = sine(np.arange(80)[:, None] * n[None]) * good[None]
    high, low = split_np(table)
    return np.concatenate([high, low, high], 1)


def inverse_tables():
    freq = np.arange(81)
    scale = np.where((freq == 0) | (freq == 80), 1.0, 2.0) / PATCH
    n = np.arange(PATCH)
    product = n[:, None] * freq[None, :]
    cos_part, sin_part = cosine(product) * scale[None], sine(product) * scale[None]
    left = np.zeros((PATCH, FREQ))
    left[:, 0:81] = cos_part
    left[:, SIN_ROW : SIN_ROW + 80] = sin_part[:, :80]
    high, low = split_np(left)
    pad = np.zeros((PATCH, 512 - 3 * FREQ), high.dtype)
    left_table = np.concatenate([high, high, low, pad], 1)
    right = np.zeros((256, 256))
    right[0:81, 0:PATCH] = cos_part.T
    right[128:209, 0:PATCH] = sin_part.T
    high, low = split_np(right)
    right_table = np.concatenate([high, high, low], 0)
    return left_table, right_table


def place_tables():
    lane = np.arange(128)[None]
    p = np.arange(16)[:, None]
    position = (p // 4) * 16 + p % 4
    return (lane == position).astype(np.float32)


def when(condition):
    return pl.when(condition)


def kernel(
    sizes,
    image_ref,
    mask_ref,
    column_hbm,
    row_hbm,
    last_hbm,
    left_hbm,
    right_hbm,
    flow_ref,
    offset_ref,
    buf,
    work,
    column_table,
    row_tab,
    last_tab,
    left_tab,
    right_tab,
    y_high,
    y_low,
    spec,
    red,
    tile_scr,
    colb,
    plane,
    table_sem,
    halo_send,
    halo_recv,
    tile_send,
    tile_recv,
    col_send,
    col_recv,
    plane_send,
    plane_recv,
):
    nz, ny, nx = sizes
    gz, gy, gx = lax.axis_index("gz"), lax.axis_index("gy"), lax.axis_index("gx")
    f32, bf16 = jnp.float32, jnp.bfloat16

    tables = [
        pltpu.make_async_copy(source, target, table_sem.at[k])
        for k, (source, target) in enumerate(
            (
                (column_hbm, column_table),
                (row_hbm, row_tab),
                (last_hbm, last_tab),
                (left_hbm, left_tab),
                (right_hbm, right_tab),
            )
        )
    ]
    for copy in tables:
        copy.start()

    def exists(dy, dx):
        ok = None
        for step, position, count in ((dy, gy, ny), (dx, gx, nx)):
            term = None
            if step < 0:
                term = position > 0
            elif step > 0:
                term = position < count - 1
            if term is not None:
                ok = term if ok is None else ok & term
        return ok

    barrier = pltpu.get_barrier_semaphore()
    for dz in range(1, nz):
        pl.semaphore_signal(
            barrier, inc=1, device_id={"gz": lax.rem(gz + dz, nz)}, device_id_type=MESH
        )
    for dy, dx in DIRECTIONS:

        @when(exists(dy, dx))
        def _():
            pl.semaphore_signal(
                barrier, inc=1, device_id={"gy": gy + dy, "gx": gx + dx}, device_id_type=MESH
            )

    image = image_ref[0]
    buf[0, 1, HALO : HALO + TILE, :] = image[:, 0:128]
    buf[0, 2, HALO : HALO + TILE, :] = image[:, 32:160]
    zeros = jnp.zeros((HALO, LANES), bf16)

    @when(gy == 0)
    def _():
        for s in range(3):
            for t in range(4):
                buf[s, t, 0:HALO, :] = zeros

    @when(gy == ny - 1)
    def _():
        for s in range(3):
            for t in range(4):
                buf[s, t, HALO + TILE : ROWS, :] = zeros

    @when(gx == 0)
    def _():
        for s in range(3):
            buf[s, 0] = jnp.zeros((ROWS, LANES), bf16)

    @when(gx == nx - 1)
    def _():
        for s in range(3):
            buf[s, 3] = jnp.zeros((ROWS, LANES), bf16)

    for d, (dy, dx) in enumerate(DIRECTIONS):

        @when(jnp.logical_not(exists(-dy, -dx)))
        def _():
            plane[d] = jnp.zeros((8, 1, 384), f32)

    if nz < 8:
        colb[...] = jnp.zeros((8, 1, 384), f32)

    tile_scr[...] = jnp.zeros((8, LANES), f32)
    tile_scr[0:4, 0:4] = mask_ref[0].astype(f32)
    mask_tile = tile_scr[...]
    mask_row = mask_tile[0:1]
    for y in range(1, 4):
        mask_row = mask_row + pltpu.roll(mask_tile[y : y + 1], 16 * y, 1)
    mask_row = mask_row + pltpu.roll(mask_row, 64, 1)
    colb[gz, 0:1, 256:384] = mask_row

    neighbours = (nz - 1) + 8
    missing = (
        3 * (gy == 0).astype(jnp.int32)
        + 3 * (gy == ny - 1).astype(jnp.int32)
        + 3 * (gx == 0).astype(jnp.int32)
        + 3 * (gx == nx - 1).astype(jnp.int32)
        - ((gy == 0) & (gx == 0)).astype(jnp.int32)
        - ((gy == 0) & (gx == nx - 1)).astype(jnp.int32)
        - ((gy == ny - 1) & (gx == 0)).astype(jnp.int32)
        - ((gy == ny - 1) & (gx == nx - 1)).astype(jnp.int32)
    )
    pl.semaphore_wait(barrier, neighbours - missing)

    top, middle, bottom = (0, HALO), (HALO, TILE), (HALO + TILE, HALO)

    def halo_copy(s, d):
        dy, dx = DIRECTIONS[d]
        source_rows = {-1: (HALO, HALO), 0: middle, 1: (TILE, HALO)}[dy]
        target_rows = {-1: bottom, 0: middle, 1: top}[dy]
        source_tiles = {-1: (1, 1), 0: (1, 2), 1: (2, 1)}[dx]
        target_tiles = {-1: (3, 1), 0: (1, 2), 1: (0, 1)}[dx]
        return pltpu.make_async_remote_copy(
            src_ref=buf.at[s, pl.ds(*source_tiles), pl.ds(*source_rows)],
            dst_ref=buf.at[s, pl.ds(*target_tiles), pl.ds(*target_rows)],
            send_sem=halo_send.at[s, d],
            recv_sem=halo_recv.at[s, d],
            device_id={"gy": gy + dy, "gx": gx + dx},
            device_id_type=MESH,
        )

    def tile_copy(s):
        return pltpu.make_async_remote_copy(
            src_ref=buf.at[0, pl.ds(1, 2), pl.ds(*middle)],
            dst_ref=buf.at[s, pl.ds(1, 2), pl.ds(*middle)],
            send_sem=tile_send.at[s - 1],
            recv_sem=tile_recv.at[s - 1],
            device_id={"gz": gz - s},
            device_id_type=MESH,
        )

    def send_halos(s):
        for d, (dy, dx) in enumerate(DIRECTIONS):

            @when(exists(dy, dx))
            def _():
                halo_copy(s, d).start()

    def forward(s):
        for d, (dy, dx) in enumerate(DIRECTIONS):

            @when(exists(-dy, -dx))
            def _():
                halo_copy(s, d).wait_recv()

    send_halos(0)
    for s in (1, 2):

        @when(gz >= s)
        def _():
            tile_copy(s).start()

    def relay(s):
        @when(gz + s < nz)
        def _():
            tile_copy(s).wait_recv()
            send_halos(s)

    lane = lax.broadcasted_iota(jnp.int32, (ROWS, LANES), 1)

    def spectra(s, slot):
        left, tile_a, tile_b, right = buf[s, 0], buf[s, 1], buf[s, 2], buf[s, 3]
        work[0, :, 0:128] = left
        work[0, :, 128:256] = tile_a
        work[1, :, 0:128] = jnp.where(lane < 108, tile_b, left)
        work[1, :, 128:256] = tile_a
        work[2, :, 0:128] = tile_b
        work[2, :, 128:256] = jnp.where(lane < 20, right, tile_a)
        work[3, :, 0:128] = tile_b
        work[3, :, 128:256] = right

        def per_column(j, carry):
            @when((s == 0) & (j == 1))
            def _():
                relay(1)

            @when((s == 0) & (j == 3))
            def _():
                relay(2)

            a = work[j]
            y = jnp.dot(
                jnp.concatenate([a, a], 1), column_table[j], preferred_element_type=f32
            )
            high = y.astype(bf16)
            y_high[...] = high
            y_low[...] = (y - high.astype(f32)).astype(bf16)
            first_high, first_low = y_high[0:256], y_low[0:256]
            out = jnp.dot(
                row_tab[...],
                jnp.concatenate([first_high, first_high, first_low], 0),
                preferred_element_type=f32,
            )
            for i in range(3):
                spec[slot, j * 4 + i] = out[i * FREQ : (i + 1) * FREQ]
            last_high, last_low = y_high[32:288], y_low[32:288]
            spec[slot, j * 4 + 3] = jnp.dot(
                last_tab[...],
                jnp.concatenate([last_high, last_high, last_low], 0),
                preferred_element_type=f32,
            )
            return carry

        lax.fori_loop(0, 4, per_column, 0)

    shift_lane = lax.broadcasted_iota(jnp.int32, (8, LANES), 1)
    shift_low = (lax.rem(shift_lane + 80, PATCH) - 80).astype(f32)
    sub = lax.broadcasted_iota(jnp.int32, (8, LANES), 0).astype(f32)
    shift_high = (shift_lane - 32).astype(f32)

    def cross(a, b):
        ccs, css = a[0:80, 0:128], a[0:80, 128:256]
        scs, sss = a[88:168, 0:128], a[88:168, 128:256]
        cct, cst = b[0:80, 0:128], b[0:80, 128:256]
        sct, sst = b[88:168, 0:128], b[88:168, 128:256]
        q_cc = cct * ccs + sst * sss + cst * css + sct * scs
        q_ss = cct * sss + sst * ccs - cst * scs - sct * css
        q_cs = cst * ccs + sst * scs - cct * css - sct * sss
        q_sc = sct * ccs + sst * css - cct * scs - cst * sss
        cce, cse = a[80:88, 0:128], a[80:88, 128:256]
        cct, cst = b[80:88, 0:128], b[80:88, 128:256]
        e_cc = cct * cce + cst * cse
        e_cs = cst * cce - cct * cse
        cos_half = jnp.concatenate([q_cc, e_cc, q_sc], 0)
        sin_half = jnp.concatenate([q_cs, e_cs, q_ss], 0)
        return jnp.concatenate([cos_half, sin_half], 1)

    def correlate(index):
        def per_group(g, carry):
            rows = []
            for k in range(4):
                q = cross(spec[0, g * 4 + k], spec[1, g * 4 + k])
                high = q.astype(bf16).astype(f32)
                stacked = jnp.concatenate(
                    [high, q - high, high, jnp.zeros((8, 256), f32)], 0
                ).astype(bf16)
                v = jnp.dot(left_tab[...], stacked, preferred_element_type=f32)
                high = v.astype(bf16)
                low = (v - high.astype(f32)).astype(bf16)
                rows.append(jnp.concatenate([high, low, high], 1))
            c = jnp.dot(
                jnp.concatenate(rows, 0), right_tab[...], preferred_element_type=f32
            )
            for k in range(4):
                totals = [None, None]
                moment = None
                for r in range(20):
                    base = float(8 * r if r < 10 else 8 * r - PATCH)
                    for half in range(2):
                        value = c[
                            k * 160 + 8 * r : k * 160 + 8 * r + 8, 128 * half : 128 * half + 128
                        ]
                        square = value * value
                        weight = square * square
                        totals[half] = weight if totals[half] is None else totals[half] + weight
                        if base != 0.0:
                            term = weight * base
                            moment = term if moment is None else moment + term
                both = totals[0] + totals[1]
                red[0, index, g * 4 + k] = both
                red[1, index, g * 4 + k] = moment + both * sub
                red[2, index, g * 4 + k] = totals[0] * shift_low + totals[1] * shift_high
            return carry

        lax.fori_loop(0, 4, per_group, 0)

    for copy in tables:
        copy.wait()

    def per_section(s, carry):
        @when(gz + s < nz)
        def _():
            forward(s)

        spectra(s, lax.min(s, 1))

        @when(s > 0)
        def _():
            correlate(s - 1)

        return carry

    lax.fori_loop(0, 3, per_section, 0)

    place_lane = lax.broadcasted_iota(jnp.int32, (16, LANES), 1)
    place_node = lax.broadcasted_iota(jnp.int32, (16, LANES), 0)
    target = lax.rem(place_node, 4) * 16 + place_node // 4
    flow_rows = []
    for a in range(2):
        parts = [
            jnp.sum(jnp.sum(red[q, a], axis=1), axis=1, keepdims=True) for q in range(3)
        ]
        total = parts[0] + EPSILON
        flow_y = jnp.broadcast_to(parts[1] / total, (16, LANES))
        flow_x = jnp.broadcast_to(parts[2] / total, (16, LANES))
        placed = jnp.where(place_lane == target, flow_y, 0.0) + jnp.where(
            place_lane == target + 64, flow_x, 0.0
        )
        row = jnp.sum(placed, axis=0, keepdims=True)
        row = jnp.where(gz + a + 1 < nz, row, 0.0)
        colb[gz, 0:1, 128 * a : 128 * a + 128] = row
        flow_rows.append(row)

    def write(ref, index, row, lane_base):
        for y in range(4):
            start = lane_base + 16 * y
            moved = pltpu.roll(row, (128 - start) % 128, 1) if start % 128 else row
            ref[index, 0, y : y + 1, :] = moved[:, 0:4]

    for a in range(2):
        for comp in range(2):
            write(flow_ref, 2 * a + comp, flow_rows[a], 64 * comp)

    def col_copy(dz, slot):
        return pltpu.make_async_remote_copy(
            src_ref=colb.at[gz],
            dst_ref=colb.at[slot],
            send_sem=col_send.at[dz - 1],
            recv_sem=col_recv.at[dz - 1],
            device_id={"gz": lax.rem(gz + dz, nz)},
            device_id_type=MESH,
        )

    for dz in range(1, nz):
        col_copy(dz, gz).start()
    for dz in range(1, nz):
        col_copy(dz, lax.rem(gz + nz - dz, nz)).wait_recv()

    def plane_copy(d):
        dy, dx = DIRECTIONS[d]
        return pltpu.make_async_remote_copy(
            src_ref=colb,
            dst_ref=plane.at[d],
            send_sem=plane_send.at[d],
            recv_sem=plane_recv.at[d],
            device_id={"gy": gy + dy, "gx": gx + dx},
            device_id_type=MESH,
        )

    for d, (dy, dx) in enumerate(DIRECTIONS):

        @when(exists(dy, dx))
        def _():
            plane_copy(d).start()

    for d, (dy, dx) in enumerate(DIRECTIONS):

        @when(exists(-dy, -dx))
        def _():
            plane_copy(d).wait_recv()

    def block(by, bx):
        if (by, bx) == (0, 0):
            return colb[:, 0, :]
        return plane[DIRECTIONS.index((-by, -bx)), :, 0, :]

    flow_one, flow_two, masks = [], [], []
    for by in (-1, 0, 1):
        joined = None
        for bx in (-1, 0, 1):
            value = block(by, bx)
            pieces = [value[:, 128 * q : 128 * q + 128] for q in range(3)]
            if bx > -1:
                pieces = [pltpu.roll(piece, 4 * (bx + 1), 1) for piece in pieces]
            joined = pieces if joined is None else [x + y for x, y in zip(joined, pieces)]
        flow_one.append(joined[0])
        flow_two.append(joined[1])
        masks.append(joined[2])

    lanes8 = lax.broadcasted_iota(jnp.int32, (8, LANES), 1)
    depth = lax.broadcasted_iota(jnp.int32, (8, LANES), 0)
    x_in = lax.rem(lanes8, 16)
    y_in = lax.rem(lanes8 // 16, 4)
    not_first_x = (gx > 0).astype(jnp.int32)
    not_last_x = (gx < nx - 1).astype(jnp.int32)
    inside_x = jnp.where(
        x_in < 4, not_first_x, jnp.where(x_in < 8, 1, jnp.where(x_in < 12, not_last_x, 0))
    ).astype(f32)
    row_valid = [(gy > 0).astype(jnp.int32), 1, (gy < ny - 1).astype(jnp.int32)]
    inside = [inside_x * jnp.asarray(v, jnp.int32).astype(f32) for v in row_valid]

    def up(value, steps):
        return pltpu.roll(value, 8 - steps, 0)

    def down(value, steps):
        return pltpu.roll(value, steps, 0)

    steady, weights = [], []
    for b in range(3):
        w1 = jnp.where(depth + 1 < nz, masks[b] * up(masks[b], 1), 0.0)
        w2 = jnp.where(depth + 2 < nz, masks[b] * up(masks[b], 2), 0.0)
        l1, l2 = down(w1, 1), down(w2, 2)
        pull = (
            l1 * down(flow_one[b], 1)
            + l2 * down(flow_two[b], 2)
            - w1 * flow_one[b]
            - w2 * flow_two[b]
        )
        steady.append(pull)
        weights.append((w1, w2, l1, l2, w1 + w2 + l1 + l2))

    u = [STEP_SIZE * steady[b] * inside[b] for b in range(3)]
    for _ in range(RELAX - 1):
        fresh = []
        for b in range(3):
            value = u[b]
            below = pltpu.roll(value, 128 - 16, 1)
            above = pltpu.roll(value, 16, 1)
            edge_below = pltpu.roll(u[b + 1], 48, 1) if b < 2 else jnp.zeros_like(value)
            edge_above = pltpu.roll(u[b - 1], 128 - 48, 1) if b > 0 else jnp.zeros_like(value)
            below = jnp.where(y_in == 3, edge_below, below)
            above = jnp.where(y_in == 0, edge_above, above)
            laplace = (
                below + above + pltpu.roll(value, 1, 1) + pltpu.roll(value, 127, 1) - 4.0 * value
            )
            w1, w2, l1, l2, total = weights[b]
            forces = STIFFNESS * laplace + steady[b] - total * value
            forces = forces + w1 * up(value, 1) + w2 * up(value, 2)
            forces = forces + l1 * down(value, 1) + l2 * down(value, 2)
            fresh.append((value + STEP_SIZE * forces) * inside[b])
        u = fresh

    row = jnp.sum(jnp.where(depth == gz, u[1], 0.0), axis=0, keepdims=True)
    for comp in range(2):
        write(offset_ref, comp, row, 64 * comp + 4)

    for s in range(3):
        for d, (dy, dx) in enumerate(DIRECTIONS):

            @when(exists(dy, dx) & (gz + s < nz))
            def _():
                halo_copy(s, d).wait_send()

    for s in (1, 2):

        @when(gz >= s)
        def _():
            tile_copy(s).wait_send()

    for dz in range(1, nz):
        col_copy(dz, gz).wait_send()
    for d, (dy, dx) in enumerate(DIRECTIONS):

        @when(exists(dy, dx))
        def _():
            plane_copy(d).wait_send()


def solution(mesh):
    sizes = tuple(mesh.shape[name] for name in ("gz", "gy", "gx"))
    f32, bf16 = jnp.float32, jnp.bfloat16
    column_table = column_tables()
    row_tab = np.concatenate([row_table(i, 0) for i in range(3)], 0)
    last_tab = row_table(3, 32)
    left_tab, right_tab = inverse_tables()
    constants = (column_table, row_tab, last_tab, left_tab, right_tab)

    def body(images, tissue_mask):
        vmem = pl.BlockSpec(memory_space=pltpu.VMEM)
        anywhere = pl.BlockSpec(memory_space=pl.ANY)
        dma = pltpu.SemaphoreType.DMA
        return pl.pallas_call(
            functools.partial(kernel, sizes),
            out_shape=(
                jax.ShapeDtypeStruct((4, 1, 4, 4), f32),
                jax.ShapeDtypeStruct((2, 1, 4, 4), f32),
            ),
            in_specs=[vmem, vmem] + [anywhere] * 5,
            out_specs=(vmem, vmem),
            scratch_shapes=[
                pltpu.VMEM((3, 4, ROWS, LANES), bf16),
                pltpu.VMEM((4, ROWS, 256), bf16),
                pltpu.VMEM(column_table.shape, bf16),
                pltpu.VMEM(row_tab.shape, bf16),
                pltpu.VMEM(last_tab.shape, bf16),
                pltpu.VMEM(left_tab.shape, bf16),
                pltpu.VMEM(right_tab.shape, bf16),
                pltpu.VMEM((ROWS, 256), bf16),
                pltpu.VMEM((ROWS, 256), bf16),
                pltpu.VMEM((2, 16, FREQ, 256), f32),
                pltpu.VMEM((3, 2, 16, 8, LANES), f32),
                pltpu.VMEM((8, LANES), f32),
                pltpu.VMEM((8, 1, 384), f32),
                pltpu.VMEM((8, 8, 1, 384), f32),
                dma((5,)),
                dma((3, 8)),
                dma((3, 8)),
                dma((2,)),
                dma((2,)),
                dma((7,)),
                dma((7,)),
                dma((8,)),
                dma((8,)),
            ],
            compiler_params=pltpu.CompilerParams(
                collective_id=0, has_side_effects=True, vmem_limit_bytes=48 * 1024 * 1024
            ),
        )(images, tissue_mask, *[jnp.asarray(x) for x in constants])

    return jax.shard_map(
        body,
        mesh=mesh,
        in_specs=(P("gz", "gy", "gx"), P("gz", "gy", "gx")),
        out_specs=(P(None, "gz", "gy", "gx"), P(None, "gz", "gy", "gx")),
        check_vma=False,
    )
```

```python
import functools
import math

import jax
import jax.numpy as jnp
import numpy as np
from jax import lax
from jax.experimental import pallas as pl
from jax.experimental.pallas import tpu as pltpu
from jax.sharding import PartitionSpec as P

PATCH = 160
STRIDE = 40
RELAX = 4
EPSILON = 1e-06
STIFFNESS = 0.5
STEP_SIZE = 0.2

TILE = 160
HALO = 64
ROWS = TILE + 2 * HALO
LANES = 128
FIRST = 208
SECOND = ROWS - FIRST
MESH = pl.DeviceIdType.MESH
DIRECTIONS = [(dy, dx) for dy in (-1, 0, 1) for dx in (-1, 0, 1) if (dy, dx) != (0, 0)]


def split_np(table):
    bf16 = jnp.bfloat16
    high = np.asarray(table, np.float32).astype(bf16)
    low = (np.asarray(table, np.float64) - high.astype(np.float64)).astype(np.float32).astype(bf16)
    return high, low


def cosine(product):
    return np.cos(2.0 * np.pi * (product % PATCH) / PATCH)


def sine(product):
    phase = product % (PATCH // 2)
    return np.where(phase == 0, 0.0, np.sin(2.0 * np.pi * (product % PATCH) / PATCH))


def column_tables():
    freq = np.arange(81)
    out = []
    for j in range(4):
        lane = np.arange(256)
        if j == 0:
            column = lane - 128
            good = lane >= 0
        elif j == 1:
            column = np.where(lane < 108, 32 + lane, lane - 128)
            good = lane >= 96
        elif j == 2:
            column = np.where(lane < 128, 32 + lane, np.where(lane < 148, 32 + lane, lane - 128))
            good = lane < 160
        else:
            column = 32 + lane
            good = lane >= 0
        m = column - (40 * j - 60)
        good = good & (m >= 0) & (m < PATCH)
        product = m[:, None] * freq[None, :]
        table = np.zeros((256, 256))
        table[:, 0:81] = cosine(product) * good[:, None]
        table[:, 128:209] = sine(product) * good[:, None]
        high, low = split_np(table)
        out.append(np.concatenate([high, low], 0))
    return np.stack(out)


def parity_tables():
    low = np.arange(40)
    forward, inverse = [], []
    scale = np.where(low == 0, 1.0, 2.0) / PATCH
    for parity in range(2):
        n = 2 * np.arange(80) + parity
        product = low[:, None] * n[None]
        cos_part, sin_part = cosine(product), sine(product)
        sin_part[0] = cosine(40 * n) if parity == 0 else sine(40 * n)
        sin_scale = np.where(low == 0, 2.0, 2.0) / PATCH
        table = np.concatenate([cos_part, sin_part], 0)
        high, part = split_np(table)
        forward.append(np.concatenate([high, part, high], 1))
        table = np.concatenate([cos_part * scale[:, None], sin_part * sin_scale[:, None]], 0).T
        high, part = split_np(table)
        inverse.append(np.concatenate([high, high, part], 1))
    return np.stack(forward), np.stack(inverse)


def right_inverse():
    freq = np.arange(81)
    scale = np.where((freq == 0) | (freq == 80), 1.0, 2.0) / PATCH
    product = freq[:, None] * np.arange(PATCH)[None]
    right = np.zeros((256, 256))
    right[0:81, 0:PATCH] = cosine(product) * scale[:, None]
    right[128:209, 0:PATCH] = sine(product) * scale[:, None]
    high, low = split_np(right)
    return np.concatenate([high, high, low], 0)


def kernel(
    sizes,
    image_hbm,
    mask_hbm,
    column_hbm,
    row_hbm,
    left_hbm,
    right_hbm,
    flow_ref,
    offset_ref,
    buf,
    column_table,
    row_tab,
    left_tab,
    right_tab,
    y_a,
    y_b,
    y_c,
    y_d,
    rows_a,
    rows_b,
    spec,
    red,
    tile_scr,
    colb,
    plane,
    image_ref,
    mask_ref,
    table_sem,
    halo_send,
    halo_recv,
    tile_send,
    tile_recv,
    col_send,
    col_recv,
    plane_send,
    plane_recv,
    near_sem,
    far_sem,
):
    nz, ny, nx = sizes
    gz, gy, gx = lax.axis_index("gz"), lax.axis_index("gy"), lax.axis_index("gx")
    f32, bf16 = jnp.float32, jnp.bfloat16
    y_parts, rows_buf = (y_a, y_b, y_c, y_d), (rows_a, rows_b)

    tables = [
        pltpu.make_async_copy(source, target, table_sem.at[k])
        for k, (source, target) in enumerate(
            (
                (image_hbm, image_ref),
                (mask_hbm, mask_ref),
                (column_hbm, column_table),
                (row_hbm, row_tab),
                (left_hbm, left_tab),
                (right_hbm, right_tab),
            )
        )
    ]
    for copy in tables:
        copy.start()

    def exists(dy, dx):
        ok = None
        for step, position, count in ((dy, gy, ny), (dx, gx, nx)):
            term = None
            if step < 0:
                term = position > 0
            elif step > 0:
                term = position < count - 1
            if term is not None:
                ok = term if ok is None else ok & term
        return ok

    core = lax.rem(gy, 2)
    first_core, second_core = core == 0, core == 1
    base_gy = gy - core
    layer = gy // 2
    layers = ny // 2

    def count(*conditions):
        return sum(jnp.asarray(c).astype(jnp.int32) for c in conditions)

    barrier = pltpu.get_barrier_semaphore()

    @pl.when(second_core)
    def _():
        pl.semaphore_signal(barrier, inc=1, device_id={"gy": base_gy}, device_id_type=MESH)

    for dx in (-1, 1):

        @pl.when(exists(0, dx))
        def _():
            pl.semaphore_signal(
                barrier, inc=1, device_id={"gy": base_gy, "gx": gx + dx}, device_id_type=MESH
            )

    for dz in range(1, nz):
        pl.semaphore_signal(
            barrier,
            inc=1,
            device_id={"gz": lax.rem(gz + dz, nz), "gy": base_gy},
            device_id_type=MESH,
        )
    for dx in (-1, 0, 1):
        inside_x = True if dx == 0 else exists(0, dx)

        @pl.when(second_core & (layer < layers - 1) & inside_x)
        def _():
            pl.semaphore_signal(
                barrier, inc=1, device_id={"gy": gy + 2, "gx": gx + dx}, device_id_type=MESH
            )

        @pl.when(first_core & (layer > 0) & inside_x)
        def _():
            pl.semaphore_signal(
                barrier, inc=1, device_id={"gy": gy - 1, "gx": gx + dx}, device_id_type=MESH
            )

    tables[0].wait()
    image = image_ref[0]
    buf[0, 1, HALO : HALO + TILE, :] = image[:, 0:128]
    buf[0, 2, HALO : HALO + TILE, :] = image[:, 32:160]
    zeros = jnp.zeros((HALO, LANES), bf16)

    @pl.when(gy == 0)
    def _():
        for s in range(3):
            for t in range(4):
                buf[s, t, 0:HALO, :] = zeros

    @pl.when(gy == ny - 1)
    def _():
        for s in range(3):
            for t in range(4):
                buf[s, t, HALO + TILE : ROWS, :] = zeros

    @pl.when(gx == 0)
    def _():
        for s in range(3):
            buf[s, 0] = jnp.zeros((ROWS, LANES), bf16)

    @pl.when(gx == nx - 1)
    def _():
        for s in range(3):
            buf[s, 3] = jnp.zeros((ROWS, LANES), bf16)

    for d, (dy, dx) in enumerate(DIRECTIONS):

        @pl.when(jnp.logical_not(exists(-dy, -dx)))
        def _():
            plane[d] = jnp.zeros((8, 1, LANES), f32)

    if nz < 8:
        colb[...] = jnp.zeros((8, 1, LANES), f32)

    tables[1].wait()
    tile_scr[...] = jnp.zeros((8, LANES), f32)
    tile_scr[0:4, 0:4] = mask_ref[0].astype(f32)
    mask_tile = tile_scr[...]
    mask_row = mask_tile[0:1]
    for y in range(1, 4):
        mask_row = mask_row + pltpu.roll(mask_tile[y : y + 1], 16 * y, 1)
    mask_row = pltpu.roll(mask_row, 8, 1) + pltpu.roll(mask_row, 72, 1)

    beside = count(gx > 0, gx < nx - 1)

    @pl.when(first_core)
    def _():
        pl.semaphore_wait(barrier, 1 + 2 * (nz - 1) + 2 * beside)
        pl.semaphore_signal(near_sem, inc=1, device_id={"gy": gy + 1}, device_id_type=MESH)

    @pl.when(second_core)
    def _():
        pl.semaphore_wait(near_sem, 1)

    def far_barrier():
        @pl.when(second_core)
        def _():
            pl.semaphore_wait(
                barrier, (1 + beside) * count(layer > 0, layer < layers - 1)
            )
            pl.semaphore_signal(far_sem, inc=1, device_id={"gy": gy - 1}, device_id_type=MESH)

        @pl.when(first_core)
        def _():
            pl.semaphore_wait(far_sem, 1)

    top, middle, bottom = (0, HALO), (HALO, TILE), (HALO + TILE, HALO)

    def halo_copy(s, d):
        dy, dx = DIRECTIONS[d]
        source_rows = {-1: (HALO, HALO), 0: middle, 1: (TILE, HALO)}[dy]
        target_rows = {-1: bottom, 0: middle, 1: top}[dy]
        source_tiles = {-1: (1, 1), 0: (1, 2), 1: (2, 1)}[dx]
        target_tiles = {-1: (3, 1), 0: (1, 2), 1: (0, 1)}[dx]
        return pltpu.make_async_remote_copy(
            src_ref=buf.at[s, pl.ds(*source_tiles), pl.ds(*source_rows)],
            dst_ref=buf.at[s, pl.ds(*target_tiles), pl.ds(*target_rows)],
            send_sem=halo_send.at[s, d],
            recv_sem=halo_recv.at[s, d],
            device_id={"gy": gy + dy, "gx": gx + dx},
            device_id_type=MESH,
        )

    def tile_copy(s):
        return pltpu.make_async_remote_copy(
            src_ref=buf.at[s - 1, pl.ds(1, 2), pl.ds(*middle)],
            dst_ref=buf.at[s, pl.ds(1, 2), pl.ds(*middle)],
            send_sem=tile_send.at[s - 1],
            recv_sem=tile_recv.at[s - 1],
            device_id={"gz": gz - 1},
            device_id_type=MESH,
        )

    def is_near(dy):
        if dy == 0:
            return True
        return first_core if dy > 0 else second_core

    def send_halos(s, near):
        for d, (dy, dx) in enumerate(DIRECTIONS):
            if dy == 0 and not near:
                continue
            side = is_near(dy) if near else jnp.logical_not(is_near(dy))

            @pl.when(exists(dy, dx) & side)
            def _():
                halo_copy(s, d).start()

    def receive_halos(s, near):
        for d, (dy, dx) in enumerate(DIRECTIONS):
            if dy == 0 and not near:
                continue
            side = is_near(-dy) if near else jnp.logical_not(is_near(-dy))

            @pl.when(exists(-dy, -dx) & side)
            def _():
                halo_copy(s, d).wait_recv()

    @pl.when(gz > 0)
    def _():
        tile_copy(1).start()

    send_halos(0, True)

    def relay(s):
        @pl.when(gz + s < nz)
        def _():
            tile_copy(s).wait_recv()
            if s == 1:

                @pl.when(gz > 0)
                def _():
                    tile_copy(2).start()

            send_halos(s, True)

    first_row = lax.broadcasted_iota(jnp.int32, (8, 256), 0) == 0

    def spectra(s, slot, base, rows, top, between):
        area = pl.ds(base, rows)
        lane = lax.broadcasted_iota(jnp.int32, (rows, LANES), 1)
        left, tile_a, tile_b, right = (buf[s, t, area, :] for t in range(4))
        windows = (
            (left, tile_a),
            (jnp.where(lane < 108, tile_b, left), tile_a),
            (tile_b, jnp.where(lane < 20, right, tile_a)),
            (tile_b, right),
        )
        for j, (first, second) in enumerate(windows):
            y = jnp.dot(
                jnp.concatenate([first, second, first, second], 1),
                column_table[j],
                preferred_element_type=f32,
            )
            high = y.astype(bf16).astype(f32)
            low = y - high
            for t in range(2):
                cut = slice(128 * t, 128 * t + 128)
                y_parts[j][s, t, area, :] = high[:, cut]
                y_parts[j][s, 2 + t, area, :] = low[:, cut]
        between()
        for j in range(4):
            for k in range(2):
                start = 4 + 40 * (top + k)
                both = []
                for parity in range(2):
                    window = pl.ds(start + parity, 80, 2)
                    high, low = (
                        jnp.concatenate(
                            [y_parts[j][s, q + t, window, :].astype(bf16) for t in range(2)], 1
                        )
                        for q in (0, 2)
                    )
                    both.append(
                        jnp.dot(
                            row_tab[parity],
                            jnp.concatenate([high, high, low], 0),
                            preferred_element_type=f32,
                        )
                    )
                even, odd = both
                n = j * 2 + k
                spec[slot, n, 0:40] = even[0:40] + odd[0:40]
                spec[slot, n, 40:80] = even[0:40] - odd[0:40]
                total, rest = even[40:80] + odd[40:80], odd[40:80] - even[40:80]
                spec[slot, n, 80:88] = jnp.where(first_row, 0.0, total[0:8])
                spec[slot, n, 88:120] = total[8:40]
                spec[slot, n, 120:128] = jnp.where(first_row, 0.0, rest[0:8])
                spec[slot, n, 128:160] = rest[8:40]
                spec[slot, n, 160:168] = jnp.where(first_row, even[40:48], 0.0)
                spec[slot, n, 168:176] = jnp.where(first_row, odd[40:48], 0.0)

    shift_lane = lax.broadcasted_iota(jnp.int32, (8, LANES), 1)
    shift_low = (lax.rem(shift_lane + 80, PATCH) - 80).astype(f32)
    twice_sub = (2 * lax.broadcasted_iota(jnp.int32, (8, LANES), 0)).astype(f32)
    shift_high = (shift_lane - 32).astype(f32)

    def cross(n, cos_rows, sin_rows):
        cos_lanes, sin_lanes = slice(0, 128), slice(128, 256)
        ccs, css = spec[0, n, cos_rows, cos_lanes], spec[0, n, cos_rows, sin_lanes]
        scs, sss = spec[0, n, sin_rows, cos_lanes], spec[0, n, sin_rows, sin_lanes]
        cct, cst = spec[1, n, cos_rows, cos_lanes], spec[1, n, cos_rows, sin_lanes]
        sct, sst = spec[1, n, sin_rows, cos_lanes], spec[1, n, sin_rows, sin_lanes]
        q_cc = cct * ccs + sst * sss + cst * css + sct * scs
        q_ss = cct * sss + sst * ccs - cst * scs - sct * css
        q_cs = cst * ccs + sst * scs - cct * css - sct * sss
        q_sc = sct * ccs + sst * css - cct * scs - cst * sss
        return jnp.concatenate([q_cc, q_cs], 1), jnp.concatenate([q_sc, q_ss], 1)

    def transform_rows(n, target, m):
        cos_low, sin_low = cross(n, slice(0, 40), slice(80, 120))
        cos_high, sin_high = cross(n, slice(40, 80), slice(120, 160))
        cos_mid, sin_mid = cross(n, slice(160, 168), slice(168, 176))
        parts = (
            (cos_low + cos_high, sin_low - sin_high, cos_mid),
            (cos_low - cos_high, sin_low + sin_high, sin_mid),
        )
        for parity, (cos_part, sin_part, mid) in enumerate(parts):
            q = jnp.concatenate([cos_part, sin_part[0:8] + mid, sin_part[8:40]], 0)
            high = q.astype(bf16)
            low = (q - high.astype(f32)).astype(bf16)
            v = jnp.dot(
                left_tab[parity],
                jnp.concatenate([high, low, high], 0),
                preferred_element_type=f32,
            )
            high = v.astype(bf16)
            low = (v - high.astype(f32)).astype(bf16)
            place = slice(160 * m + 80 * parity, 160 * m + 80 * parity + 80)
            target[place, 0:256] = high
            target[place, 256:512] = low

    def moments(c, index, node):
        tail, total, weighted = None, None, []
        for parity in range(2):
            running = ramp = None
            for block in range(9, -1, -1):
                start = 80 * parity + 8 * block
                value = c[start : start + 8]
                square = value * value
                weight = square * square
                near, far = weight[:, 0:128], weight[:, 128:256]
                tail = far if tail is None else tail + far
                joined = near + far
                running = joined if running is None else running + joined
                if block > 0:
                    ramp = running if ramp is None else ramp + running
                if block == 5:
                    wrapped = running
            weighted.append(16.0 * ramp - float(PATCH) * wrapped)
            total = running if total is None else total + running
        red[0, index, node] = total
        red[1, index, node] = weighted[0] + weighted[1] + running + total * twice_sub
        red[2, index, node] = total * shift_low + tail * (shift_high - shift_low)

    def correlate(index, top):
        def columns(g):
            high, low = rows_buf[g][:, 0:256], rows_buf[g][:, 256:512]
            c = jnp.dot(
                jnp.concatenate([high, low, high], 1), right_tab[...], preferred_element_type=f32
            )
            for m in range(4):
                node = (2 * g + m // 2) * 4 + top + m % 2
                moments(c[160 * m : 160 * m + 160], index, node)

        for m in range(4):
            transform_rows(m, rows_buf[0], m)
        for m in range(4):
            transform_rows(4 + m, rows_buf[1], m)
        columns(0)
        columns(1)

    for copy in tables[2:]:
        copy.wait()

    halves = (
        (pl.multiple_of(jnp.where(first_core, SECOND, 0), 16), FIRST, jnp.where(first_core, 2, 0)),
        (pl.multiple_of(jnp.where(first_core, 0, FIRST), 16), SECOND, jnp.where(first_core, 0, 2)),
    )
    for half, (base, rows, top_patch) in enumerate(halves):

        def per_section(s, carry):
            @pl.when(gz + s < nz)
            def _():
                receive_halos(s, half == 0)

            def between():
                if half == 0:

                    @pl.when(s == 0)
                    def _():
                        relay(1)

            spectra(s, lax.min(s, 1), base, rows, top_patch, between)
            if half == 0:

                @pl.when(s == 0)
                def _():
                    far_barrier()
                    send_halos(0, False)

                    @pl.when(gz + 1 < nz)
                    def _():
                        send_halos(1, False)

                @pl.when(s == 1)
                def _():
                    relay(2)

                    @pl.when(gz + 2 < nz)
                    def _():
                        send_halos(2, False)

            @pl.when(s > 0)
            def _():
                correlate(s - 1, top_patch)

            return carry

        lax.fori_loop(0, 3, per_section, 0)

    place_lane = lax.broadcasted_iota(jnp.int32, (16, LANES), 1)
    place_node = lax.broadcasted_iota(jnp.int32, (16, LANES), 0)
    target = lax.rem(place_node, 4) * 16 + place_node // 4
    flow_rows = []
    for a in range(2):
        parts = [
            jnp.sum(jnp.sum(red[q, a], axis=1), axis=1, keepdims=True) for q in range(3)
        ]
        total = parts[0] + EPSILON
        flow_y = jnp.broadcast_to(parts[1] / total, (16, LANES))
        flow_x = jnp.broadcast_to(parts[2] / total, (16, LANES))
        placed = jnp.where(place_lane == target, flow_y, 0.0) + jnp.where(
            place_lane == target + 64, flow_x, 0.0
        )
        row = jnp.sum(placed, axis=0, keepdims=True)
        row = jnp.where(gz + a + 1 < nz, row, 0.0)
        flow_rows.append(row)
    colb[gz] = flow_rows[0] + pltpu.roll(flow_rows[1], 4, 1) + mask_row

    def write(ref, index, row, lane_base):
        for y in range(4):
            start = lane_base + 16 * y
            moved = pltpu.roll(row, (128 - start) % 128, 1) if start % 128 else row
            ref[index, 0, y : y + 1, :] = moved[:, 0:4]

    for a in range(2):
        for comp in range(2):
            write(flow_ref, 2 * a + comp, flow_rows[a], 64 * comp)

    def col_copy(dz, slot):
        return pltpu.make_async_remote_copy(
            src_ref=colb.at[gz],
            dst_ref=colb.at[slot],
            send_sem=col_send.at[dz - 1],
            recv_sem=col_recv.at[dz - 1],
            device_id={"gz": lax.rem(gz + dz, nz)},
            device_id_type=MESH,
        )

    for dz in range(1, nz):
        col_copy(dz, gz).start()
    for dz in range(1, nz):
        col_copy(dz, lax.rem(gz + nz - dz, nz)).wait_recv()

    def plane_copy(d):
        dy, dx = DIRECTIONS[d]
        return pltpu.make_async_remote_copy(
            src_ref=colb,
            dst_ref=plane.at[d],
            send_sem=plane_send.at[d],
            recv_sem=plane_recv.at[d],
            device_id={"gy": gy + dy, "gx": gx + dx},
            device_id_type=MESH,
        )

    for d, (dy, dx) in enumerate(DIRECTIONS):

        @pl.when(exists(dy, dx))
        def _():
            plane_copy(d).start()

    for d, (dy, dx) in enumerate(DIRECTIONS):

        @pl.when(exists(-dy, -dx))
        def _():
            plane_copy(d).wait_recv()

    def block(by, bx):
        if (by, bx) == (0, 0):
            return colb[:, 0, :]
        return plane[DIRECTIONS.index((-by, -bx)), :, 0, :]

    lanes8 = lax.broadcasted_iota(jnp.int32, (8, LANES), 1)
    depth = lax.broadcasted_iota(jnp.int32, (8, LANES), 0)
    x_in = lax.rem(lanes8, 16)
    y_in = lax.rem(lanes8 // 16, 4)
    flow_one, flow_two, masks = [], [], []
    for by in (-1, 0, 1):
        joined = None
        for bx in (-1, 0, 1):
            value = block(by, bx)
            pieces = []
            for q in range(3):
                piece = jnp.where(x_in // 4 == q, value, 0.0)
                moved = (4 * (bx + 1 - q)) % 128
                pieces.append(pltpu.roll(piece, moved, 1) if moved else piece)
            joined = pieces if joined is None else [x + y for x, y in zip(joined, pieces)]
        flow_one.append(joined[0])
        flow_two.append(joined[1])
        masks.append(joined[2])

    not_first_x = (gx > 0).astype(jnp.int32)
    not_last_x = (gx < nx - 1).astype(jnp.int32)
    inside_x = jnp.where(
        x_in < 4, not_first_x, jnp.where(x_in < 8, 1, jnp.where(x_in < 12, not_last_x, 0))
    ).astype(f32)
    row_valid = [(gy > 0).astype(jnp.int32), 1, (gy < ny - 1).astype(jnp.int32)]
    inside = [inside_x * jnp.asarray(v, jnp.int32).astype(f32) for v in row_valid]

    def up(value, steps):
        return pltpu.roll(value, 8 - steps, 0)

    def down(value, steps):
        return pltpu.roll(value, steps, 0)

    steady, weights = [], []
    for b in range(3):
        w1 = jnp.where(depth + 1 < nz, masks[b] * up(masks[b], 1), 0.0)
        w2 = jnp.where(depth + 2 < nz, masks[b] * up(masks[b], 2), 0.0)
        l1, l2 = down(w1, 1), down(w2, 2)
        pull = (
            l1 * down(flow_one[b], 1)
            + l2 * down(flow_two[b], 2)
            - w1 * flow_one[b]
            - w2 * flow_two[b]
        )
        steady.append(pull)
        weights.append((w1, w2, l1, l2, w1 + w2 + l1 + l2))

    u = [STEP_SIZE * steady[b] * inside[b] for b in range(3)]
    for _ in range(RELAX - 1):
        fresh = []
        for b in range(3):
            value = u[b]
            below = pltpu.roll(value, 128 - 16, 1)
            above = pltpu.roll(value, 16, 1)
            edge_below = pltpu.roll(u[b + 1], 48, 1) if b < 2 else jnp.zeros_like(value)
            edge_above = pltpu.roll(u[b - 1], 128 - 48, 1) if b > 0 else jnp.zeros_like(value)
            below = jnp.where(y_in == 3, edge_below, below)
            above = jnp.where(y_in == 0, edge_above, above)
            laplace = (
                below + above + pltpu.roll(value, 1, 1) + pltpu.roll(value, 127, 1) - 4.0 * value
            )
            w1, w2, l1, l2, total = weights[b]
            forces = STIFFNESS * laplace + steady[b] - total * value
            forces = forces + w1 * up(value, 1) + w2 * up(value, 2)
            forces = forces + l1 * down(value, 1) + l2 * down(value, 2)
            fresh.append((value + STEP_SIZE * forces) * inside[b])
        u = fresh

    row = jnp.sum(jnp.where(depth == gz, u[1], 0.0), axis=0, keepdims=True)
    for comp in range(2):
        write(offset_ref, comp, row, 64 * comp + 4)

    for s in range(3):
        for d, (dy, dx) in enumerate(DIRECTIONS):

            @pl.when(exists(dy, dx) & (gz + s < nz))
            def _():
                halo_copy(s, d).wait_send()

    for s in (1, 2):

        @pl.when((gz > 0) & (gz + s - 1 < nz))
        def _():
            tile_copy(s).wait_send()

    for dz in range(1, nz):
        col_copy(dz, gz).wait_send()
    for d, (dy, dx) in enumerate(DIRECTIONS):

        @pl.when(exists(dy, dx))
        def _():
            plane_copy(d).wait_send()


def solution(mesh):
    sizes = tuple(mesh.shape[name] for name in ("gz", "gy", "gx"))
    f32, bf16 = jnp.float32, jnp.bfloat16
    column_table = column_tables()
    row_tab, left_tab = parity_tables()
    right_tab = right_inverse()
    constants = (column_table, row_tab, left_tab, right_tab)

    def body(images, tissue_mask):
        vmem = pl.BlockSpec(memory_space=pltpu.VMEM)
        anywhere = pl.BlockSpec(memory_space=pl.ANY)
        dma = pltpu.SemaphoreType.DMA
        return pl.pallas_call(
            functools.partial(kernel, sizes),
            out_shape=(
                jax.ShapeDtypeStruct((4, 1, 4, 4), f32),
                jax.ShapeDtypeStruct((2, 1, 4, 4), f32),
            ),
            in_specs=[anywhere] * 6,
            out_specs=(vmem, vmem),
            scratch_shapes=[
                pltpu.VMEM((3, 4, ROWS, LANES), bf16),
                pltpu.VMEM(column_table.shape, bf16),
                pltpu.VMEM(row_tab.shape, bf16),
                pltpu.VMEM(left_tab.shape, bf16),
                pltpu.VMEM(right_tab.shape, bf16),
                pltpu.VMEM((3, 4, ROWS, LANES), f32),
                pltpu.VMEM((3, 4, ROWS, LANES), f32),
                pltpu.VMEM((3, 4, ROWS, LANES), f32),
                pltpu.VMEM((3, 4, ROWS, LANES), f32),
                pltpu.VMEM((4 * PATCH, 512), bf16),
                pltpu.VMEM((4 * PATCH, 512), bf16),
                pltpu.VMEM((2, 8, 176, 256), f32),
                pltpu.VMEM((3, 2, 16, 8, LANES), f32),
                pltpu.VMEM((8, LANES), f32),
                pltpu.VMEM((8, 1, LANES), f32),
                pltpu.VMEM((8, 8, 1, LANES), f32),
                pltpu.VMEM((1, TILE, TILE), bf16),
                pltpu.VMEM((1, 4, 4), jnp.int32),
                dma((6,)),
                dma((3, 8)),
                dma((3, 8)),
                dma((2,)),
                dma((2,)),
                dma((7,)),
                dma((7,)),
                dma((8,)),
                dma((8,)),
                pltpu.SemaphoreType.REGULAR,
                pltpu.SemaphoreType.REGULAR,
            ],
            compiler_params=pltpu.CompilerParams(
                collective_id=0, has_side_effects=True, vmem_limit_bytes=67043328
            ),
        )(images, tissue_mask, *[jnp.asarray(x) for x in constants])

    return jax.shard_map(
        body,
        mesh=mesh,
        in_specs=(P("gz", "gy", "gx"), P("gz", "gy", "gx")),
        out_specs=(P(None, "gz", "gy", "gx"), P(None, "gz", "gy", "gx")),
        check_vma=False,
    )
```

```python
import functools
import math

import jax
import jax.numpy as jnp
import numpy as np
from jax import lax
from jax.experimental import pallas as pl
from jax.experimental.pallas import tpu as pltpu
from jax.sharding import PartitionSpec as P

PATCH = 160
STRIDE = 40
RELAX = 4
EPSILON = 1e-06
STIFFNESS = 0.5
STEP_SIZE = 0.2

TILE = 160
HALO = 64
ROWS = TILE + 2 * HALO
LANES = 128
FIRST = 208
SECOND = ROWS - FIRST
MESH = pl.DeviceIdType.MESH
DIRECTIONS = [(dy, dx) for dy in (-1, 0, 1) for dx in (-1, 0, 1) if (dy, dx) != (0, 0)]


def split_np(table):
    bf16 = jnp.bfloat16
    high = np.asarray(table, np.float32).astype(bf16)
    low = (np.asarray(table, np.float64) - high.astype(np.float64)).astype(np.float32).astype(bf16)
    return high, low


def cosine(product):
    return np.cos(2.0 * np.pi * (product % PATCH) / PATCH)


def sine(product):
    phase = product % (PATCH // 2)
    return np.where(phase == 0, 0.0, np.sin(2.0 * np.pi * (product % PATCH) / PATCH))


def column_tables():
    freq = np.arange(81)
    out = []
    for j in range(4):
        lane = np.arange(256)
        if j == 0:
            column = lane - 128
            good = lane >= 0
        elif j == 1:
            column = np.where(lane < 108, 32 + lane, lane - 128)
            good = lane >= 96
        elif j == 2:
            column = np.where(lane < 128, 32 + lane, np.where(lane < 148, 32 + lane, lane - 128))
            good = lane < 160
        else:
            column = 32 + lane
            good = lane >= 0
        m = column - (40 * j - 60)
        good = good & (m >= 0) & (m < PATCH)
        product = m[:, None] * freq[None, :]
        table = np.zeros((256, 256))
        table[:, 0:81] = cosine(product) * good[:, None]
        table[:, 128:209] = sine(product) * good[:, None]
        high, low = split_np(table)
        out.append(np.concatenate([high, low], 0))
    return np.stack(out)


def parity_tables():
    low = np.arange(40)
    forward, inverse = [], []
    scale = np.where(low == 0, 1.0, 2.0) / PATCH
    for parity in range(2):
        n = 2 * np.arange(80) + parity
        product = low[:, None] * n[None]
        cos_part, sin_part = cosine(product), sine(product)
        sin_part[0] = cosine(40 * n) if parity == 0 else sine(40 * n)
        sin_scale = np.where(low == 0, 2.0, 2.0) / PATCH
        table = np.concatenate([cos_part, sin_part], 0)
        high, part = split_np(table)
        forward.append(np.concatenate([high, part, high], 1))
        table = np.concatenate([cos_part * scale[:, None], sin_part * sin_scale[:, None]], 0).T
        high, part = split_np(table)
        inverse.append(np.concatenate([high, high, part], 1))
    return np.stack(forward), np.stack(inverse)


def right_inverse():
    freq = np.arange(81)
    scale = np.where((freq == 0) | (freq == 80), 1.0, 2.0) / PATCH
    product = freq[:, None] * np.arange(PATCH)[None]
    right = np.zeros((256, 256))
    right[0:81, 0:PATCH] = cosine(product) * scale[:, None]
    right[128:209, 0:PATCH] = sine(product) * scale[:, None]
    high, low = split_np(right)
    return np.concatenate([high, high, low], 0)


def kernel(
    sizes,
    image_hbm,
    mask_hbm,
    column_hbm,
    row_hbm,
    left_hbm,
    right_hbm,
    flow_ref,
    offset_ref,
    buf,
    column_table,
    row_tab,
    left_tab,
    right_tab,
    y_a,
    y_b,
    y_c,
    y_d,
    rows_a,
    rows_b,
    spec,
    red,
    tile_scr,
    colb,
    plane,
    image_ref,
    mask_ref,
    table_sem,
    halo_send,
    halo_recv,
    tile_send,
    tile_recv,
    col_send,
    col_recv,
    plane_send,
    plane_recv,
    near_sem,
    far_sem,
):
    nz, ny, nx = sizes
    gz, gy, gx = lax.axis_index("gz"), lax.axis_index("gy"), lax.axis_index("gx")
    f32, bf16 = jnp.float32, jnp.bfloat16
    y_parts, rows_buf = (y_a, y_b, y_c, y_d), (rows_a, rows_b)

    tables = [
        pltpu.make_async_copy(source, target, table_sem.at[k])
        for k, (source, target) in enumerate(
            (
                (image_hbm, image_ref),
                (mask_hbm, mask_ref),
                (column_hbm, column_table),
                (row_hbm, row_tab),
                (left_hbm, left_tab),
                (right_hbm, right_tab),
            )
        )
    ]
    for copy in tables:
        copy.start()

    def exists(dy, dx):
        ok = None
        for step, position, count in ((dy, gy, ny), (dx, gx, nx)):
            term = None
            if step < 0:
                term = position > 0
            elif step > 0:
                term = position < count - 1
            if term is not None:
                ok = term if ok is None else ok & term
        return ok

    core = lax.rem(gy, 2)
    first_core, second_core = core == 0, core == 1
    base_gy = gy - core
    layer = gy // 2
    layers = ny // 2

    def count(*conditions):
        return sum(jnp.asarray(c).astype(jnp.int32) for c in conditions)

    barrier = pltpu.get_barrier_semaphore()

    @pl.when(second_core)
    def _():
        pl.semaphore_signal(barrier, inc=1, device_id={"gy": base_gy}, device_id_type=MESH)

    for dx in (-1, 1):

        @pl.when(exists(0, dx))
        def _():
            pl.semaphore_signal(
                barrier, inc=1, device_id={"gy": base_gy, "gx": gx + dx}, device_id_type=MESH
            )

    for step, present in ((-1, gz > 0), (1, gz < nz - 1)):

        @pl.when(present)
        def _():
            pl.semaphore_signal(
                barrier, inc=1, device_id={"gz": gz + step, "gy": base_gy}, device_id_type=MESH
            )

    for dz in range(1, nz):
        other = lax.rem(gz + dz, nz)

        @pl.when((other != gz - 1) & (other != gz + 1))
        def _():
            pl.semaphore_signal(
                barrier,
                inc=1,
                device_id={"gz": other, "gy": base_gy + 1},
                device_id_type=MESH,
            )

    for dx in (-1, 0, 1):
        inside_x = True if dx == 0 else exists(0, dx)

        @pl.when(second_core & (layer < layers - 1) & inside_x)
        def _():
            pl.semaphore_signal(
                barrier, inc=1, device_id={"gy": gy + 2, "gx": gx + dx}, device_id_type=MESH
            )

        @pl.when(first_core & (layer > 0) & inside_x)
        def _():
            pl.semaphore_signal(
                barrier, inc=1, device_id={"gy": gy - 1, "gx": gx + dx}, device_id_type=MESH
            )

    tables[0].wait()
    image = image_ref[0]
    buf[0, 1, HALO : HALO + TILE, :] = image[:, 0:128]
    buf[0, 2, HALO : HALO + TILE, :] = image[:, 32:160]
    zeros = jnp.zeros((HALO, LANES), bf16)

    @pl.when(gy == 0)
    def _():
        for s in range(3):
            for t in range(4):
                buf[s, t, 0:HALO, :] = zeros

    @pl.when(gy == ny - 1)
    def _():
        for s in range(3):
            for t in range(4):
                buf[s, t, HALO + TILE : ROWS, :] = zeros

    @pl.when(gx == 0)
    def _():
        for s in range(3):
            buf[s, 0] = jnp.zeros((ROWS, LANES), bf16)

    @pl.when(gx == nx - 1)
    def _():
        for s in range(3):
            buf[s, 3] = jnp.zeros((ROWS, LANES), bf16)

    for d, (dy, dx) in enumerate(DIRECTIONS):

        @pl.when(jnp.logical_not(exists(-dy, -dx)))
        def _():
            plane[d] = jnp.zeros((8, 1, LANES), f32)

    if nz < 8:
        colb[...] = jnp.zeros((8, 1, LANES), f32)

    tables[1].wait()
    tile_scr[...] = jnp.zeros((8, LANES), f32)
    tile_scr[0:4, 0:4] = mask_ref[0].astype(f32)
    mask_tile = tile_scr[...]
    mask_row = mask_tile[0:1]
    for y in range(1, 4):
        mask_row = mask_row + pltpu.roll(mask_tile[y : y + 1], 16 * y, 1)
    mask_row = pltpu.roll(mask_row, 8, 1) + pltpu.roll(mask_row, 72, 1)

    beside = count(gx > 0, gx < nx - 1)
    adjacent = count(gz > 0, gz < nz - 1)

    @pl.when(first_core)
    def _():
        pl.semaphore_wait(barrier, 1 + 2 * adjacent + 2 * beside)
        pl.semaphore_signal(near_sem, inc=1, device_id={"gy": gy + 1}, device_id_type=MESH)

    @pl.when(second_core)
    def _():
        pl.semaphore_wait(near_sem, 1)

    def far_barrier():
        @pl.when(second_core)
        def _():
            pl.semaphore_wait(
                barrier,
                (1 + beside) * count(layer > 0, layer < layers - 1)
                + 2 * (nz - 1 - adjacent),
            )
            pl.semaphore_signal(far_sem, inc=1, device_id={"gy": gy - 1}, device_id_type=MESH)

        @pl.when(first_core)
        def _():
            pl.semaphore_wait(far_sem, 1)

    top, middle, bottom = (0, HALO), (HALO, TILE), (HALO + TILE, HALO)

    def halo_copy(s, d):
        dy, dx = DIRECTIONS[d]
        source_rows = {-1: (HALO, HALO), 0: middle, 1: (TILE, HALO)}[dy]
        target_rows = {-1: bottom, 0: middle, 1: top}[dy]
        source_tiles = {-1: (1, 1), 0: (1, 2), 1: (2, 1)}[dx]
        target_tiles = {-1: (3, 1), 0: (1, 2), 1: (0, 1)}[dx]
        return pltpu.make_async_remote_copy(
            src_ref=buf.at[s, pl.ds(*source_tiles), pl.ds(*source_rows)],
            dst_ref=buf.at[s, pl.ds(*target_tiles), pl.ds(*target_rows)],
            send_sem=halo_send.at[s, d],
            recv_sem=halo_recv.at[s, d],
            device_id={"gy": gy + dy, "gx": gx + dx},
            device_id_type=MESH,
        )

    def tile_copy(s):
        return pltpu.make_async_remote_copy(
            src_ref=buf.at[s - 1, pl.ds(1, 2), pl.ds(*middle)],
            dst_ref=buf.at[s, pl.ds(1, 2), pl.ds(*middle)],
            send_sem=tile_send.at[s - 1],
            recv_sem=tile_recv.at[s - 1],
            device_id={"gz": gz - 1},
            device_id_type=MESH,
        )

    def is_near(dy):
        if dy == 0:
            return True
        return first_core if dy > 0 else second_core

    def send_halos(s, near):
        for d, (dy, dx) in enumerate(DIRECTIONS):
            if dy == 0 and not near:
                continue
            side = is_near(dy) if near else jnp.logical_not(is_near(dy))

            @pl.when(exists(dy, dx) & side)
            def _():
                halo_copy(s, d).start()

    def receive_halos(s, near):
        for d, (dy, dx) in enumerate(DIRECTIONS):
            if dy == 0 and not near:
                continue
            side = is_near(-dy) if near else jnp.logical_not(is_near(-dy))

            @pl.when(exists(-dy, -dx) & side)
            def _():
                halo_copy(s, d).wait_recv()

    @pl.when(gz > 0)
    def _():
        tile_copy(1).start()

    send_halos(0, True)

    def relay(s):
        @pl.when(gz + s < nz)
        def _():
            tile_copy(s).wait_recv()
            if s == 1:

                @pl.when(gz > 0)
                def _():
                    tile_copy(2).start()

            send_halos(s, True)

    first_row = lax.broadcasted_iota(jnp.int32, (8, 256), 0) == 0

    def spectra(s, slot, base, rows, top, between):
        area = pl.ds(base, rows)
        lane = lax.broadcasted_iota(jnp.int32, (rows, LANES), 1)
        left, tile_a, tile_b, right = (buf[s, t, area, :] for t in range(4))
        windows = (
            (left, tile_a),
            (jnp.where(lane < 108, tile_b, left), tile_a),
            (tile_b, jnp.where(lane < 20, right, tile_a)),
            (tile_b, right),
        )
        for j, (first, second) in enumerate(windows):
            y = jnp.dot(
                jnp.concatenate([first, second, first, second], 1),
                column_table[j],
                preferred_element_type=f32,
            )
            high = y.astype(bf16).astype(f32)
            low = y - high
            for t in range(2):
                cut = slice(128 * t, 128 * t + 128)
                y_parts[j][s, t, area, :] = high[:, cut]
                y_parts[j][s, 2 + t, area, :] = low[:, cut]
        between()
        for j in range(4):
            for k in range(2):
                start = 4 + 40 * (top + k)
                both = []
                for parity in range(2):
                    window = pl.ds(start + parity, 80, 2)
                    high, low = (
                        jnp.concatenate(
                            [y_parts[j][s, q + t, window, :].astype(bf16) for t in range(2)], 1
                        )
                        for q in (0, 2)
                    )
                    both.append(
                        jnp.dot(
                            row_tab[parity],
                            jnp.concatenate([high, high, low], 0),
                            preferred_element_type=f32,
                        )
                    )
                even, odd = both
                n = j * 2 + k
                spec[slot, n, 0:40] = even[0:40] + odd[0:40]
                spec[slot, n, 40:80] = even[0:40] - odd[0:40]
                total, rest = even[40:80] + odd[40:80], odd[40:80] - even[40:80]
                spec[slot, n, 80:88] = jnp.where(first_row, 0.0, total[0:8])
                spec[slot, n, 88:120] = total[8:40]
                spec[slot, n, 120:128] = jnp.where(first_row, 0.0, rest[0:8])
                spec[slot, n, 128:160] = rest[8:40]
                spec[slot, n, 160:168] = jnp.where(first_row, even[40:48], 0.0)
                spec[slot, n, 168:176] = jnp.where(first_row, odd[40:48], 0.0)

    shift_lane = lax.broadcasted_iota(jnp.int32, (8, LANES), 1)
    shift_low = (lax.rem(shift_lane + 80, PATCH) - 80).astype(f32)
    twice_sub = (2 * lax.broadcasted_iota(jnp.int32, (8, LANES), 0)).astype(f32)
    shift_high = (shift_lane - 32).astype(f32)

    def cross(own, n, cos_rows, sin_rows):
        cos_lanes, sin_lanes = slice(0, 128), slice(128, 256)
        ccs, css = spec[own, n, cos_rows, cos_lanes], spec[own, n, cos_rows, sin_lanes]
        scs, sss = spec[own, n, sin_rows, cos_lanes], spec[own, n, sin_rows, sin_lanes]
        cct, cst = spec[2, n, cos_rows, cos_lanes], spec[2, n, cos_rows, sin_lanes]
        sct, sst = spec[2, n, sin_rows, cos_lanes], spec[2, n, sin_rows, sin_lanes]
        q_cc = cct * ccs + sst * sss + cst * css + sct * scs
        q_ss = cct * sss + sst * ccs - cst * scs - sct * css
        q_cs = cst * ccs + sst * scs - cct * css - sct * sss
        q_sc = sct * ccs + sst * css - cct * scs - cst * sss
        return jnp.concatenate([q_cc, q_cs], 1), jnp.concatenate([q_sc, q_ss], 1)

    def transform_rows(own, n, target, m):
        cos_low, sin_low = cross(own, n, slice(0, 40), slice(80, 120))
        cos_high, sin_high = cross(own, n, slice(40, 80), slice(120, 160))
        cos_mid, sin_mid = cross(own, n, slice(160, 168), slice(168, 176))
        parts = (
            (cos_low + cos_high, sin_low - sin_high, cos_mid),
            (cos_low - cos_high, sin_low + sin_high, sin_mid),
        )
        for parity, (cos_part, sin_part, mid) in enumerate(parts):
            q = jnp.concatenate([cos_part, sin_part[0:8] + mid, sin_part[8:40]], 0)
            high = q.astype(bf16)
            low = (q - high.astype(f32)).astype(bf16)
            v = jnp.dot(
                left_tab[parity],
                jnp.concatenate([high, low, high], 0),
                preferred_element_type=f32,
            )
            high = v.astype(bf16)
            low = (v - high.astype(f32)).astype(bf16)
            place = slice(160 * m + 80 * parity, 160 * m + 80 * parity + 80)
            target[place, 0:256] = high
            target[place, 256:512] = low

    def moments(c, index, node):
        tail, total, weighted = None, None, []
        for parity in range(2):
            running = ramp = None
            for block in range(9, -1, -1):
                start = 80 * parity + 8 * block
                value = c[start : start + 8]
                square = value * value
                weight = square * square
                near, far = weight[:, 0:128], weight[:, 128:256]
                tail = far if tail is None else tail + far
                joined = near + far
                running = joined if running is None else running + joined
                if block > 0:
                    ramp = running if ramp is None else ramp + running
                if block == 5:
                    wrapped = running
            weighted.append(16.0 * ramp - float(PATCH) * wrapped)
            total = running if total is None else total + running
        red[0, index, node] = total
        red[1, index, node] = weighted[0] + weighted[1] + running + total * twice_sub
        red[2, index, node] = total * shift_low + tail * (shift_high - shift_low)

    def correlate(own, index, top):
        def columns(g):
            high, low = rows_buf[g][:, 0:256], rows_buf[g][:, 256:512]
            c = jnp.dot(
                jnp.concatenate([high, low, high], 1), right_tab[...], preferred_element_type=f32
            )
            for m in range(4):
                node = (2 * g + m // 2) * 4 + top + m % 2
                moments(c[160 * m : 160 * m + 160], index, node)

        for m in range(4):
            transform_rows(own, m, rows_buf[0], m)
        for m in range(4):
            transform_rows(own, 4 + m, rows_buf[1], m)
        columns(0)
        columns(1)

    for copy in tables[2:]:
        copy.wait()

    halves = (
        (pl.multiple_of(jnp.where(first_core, SECOND, 0), 16), FIRST, jnp.where(first_core, 2, 0)),
        (pl.multiple_of(jnp.where(first_core, 0, FIRST), 16), SECOND, jnp.where(first_core, 0, 2)),
    )

    def run(half, first, last):
        base, rows, top_patch = halves[half]

        def per_section(s, carry):
            @pl.when(gz + s < nz)
            def _():
                receive_halos(s, half == 0)

            def between():
                if half == 0 and first == 0:

                    @pl.when(s == 0)
                    def _():
                        relay(1)

            spectra(s, jnp.where(s == 0, half, 2), base, rows, top_patch, between)
            if half == 0 and first == 0:

                @pl.when(s == 0)
                def _():
                    far_barrier()
                    send_halos(0, False)

                    @pl.when(gz + 1 < nz)
                    def _():
                        send_halos(1, False)

            if last > 0:

                @pl.when(s > 0)
                def _():
                    correlate(half, s - 1, top_patch)

            return carry

        lax.fori_loop(first, last + 1, per_section, 0)

    run(0, 0, 1)
    relay(2)

    @pl.when(gz + 2 < nz)
    def _():
        send_halos(2, False)

    run(1, 0, 1)
    run(0, 2, 2)
    run(1, 2, 2)

    place_lane = lax.broadcasted_iota(jnp.int32, (16, LANES), 1)
    place_node = lax.broadcasted_iota(jnp.int32, (16, LANES), 0)
    target = lax.rem(place_node, 4) * 16 + place_node // 4
    flow_rows = []
    for a in range(2):
        parts = [
            jnp.sum(jnp.sum(red[q, a], axis=1), axis=1, keepdims=True) for q in range(3)
        ]
        total = parts[0] + EPSILON
        flow_y = jnp.broadcast_to(parts[1] / total, (16, LANES))
        flow_x = jnp.broadcast_to(parts[2] / total, (16, LANES))
        placed = jnp.where(place_lane == target, flow_y, 0.0) + jnp.where(
            place_lane == target + 64, flow_x, 0.0
        )
        row = jnp.sum(placed, axis=0, keepdims=True)
        row = jnp.where(gz + a + 1 < nz, row, 0.0)
        flow_rows.append(row)
    colb[gz] = flow_rows[0] + pltpu.roll(flow_rows[1], 4, 1) + mask_row

    def write(ref, index, row, lane_base):
        for y in range(4):
            start = lane_base + 16 * y
            moved = pltpu.roll(row, (128 - start) % 128, 1) if start % 128 else row
            ref[index, 0, y : y + 1, :] = moved[:, 0:4]

    for a in range(2):
        for comp in range(2):
            write(flow_ref, 2 * a + comp, flow_rows[a], 64 * comp)

    def col_copy(dz, slot):
        return pltpu.make_async_remote_copy(
            src_ref=colb.at[gz],
            dst_ref=colb.at[slot],
            send_sem=col_send.at[dz - 1],
            recv_sem=col_recv.at[dz - 1],
            device_id={"gz": lax.rem(gz + dz, nz)},
            device_id_type=MESH,
        )

    for dz in range(1, nz):
        col_copy(dz, gz).start()
    for dz in range(1, nz):
        col_copy(dz, lax.rem(gz + nz - dz, nz)).wait_recv()

    def plane_copy(d):
        dy, dx = DIRECTIONS[d]
        return pltpu.make_async_remote_copy(
            src_ref=colb,
            dst_ref=plane.at[d],
            send_sem=plane_send.at[d],
            recv_sem=plane_recv.at[d],
            device_id={"gy": gy + dy, "gx": gx + dx},
            device_id_type=MESH,
        )

    for d, (dy, dx) in enumerate(DIRECTIONS):

        @pl.when(exists(dy, dx))
        def _():
            plane_copy(d).start()

    for d, (dy, dx) in enumerate(DIRECTIONS):

        @pl.when(exists(-dy, -dx))
        def _():
            plane_copy(d).wait_recv()

    def block(by, bx):
        if (by, bx) == (0, 0):
            return colb[:, 0, :]
        return plane[DIRECTIONS.index((-by, -bx)), :, 0, :]

    lanes8 = lax.broadcasted_iota(jnp.int32, (8, LANES), 1)
    depth = lax.broadcasted_iota(jnp.int32, (8, LANES), 0)
    x_in = lax.rem(lanes8, 16)
    y_in = lax.rem(lanes8 // 16, 4)
    flow_one, flow_two, masks = [], [], []
    for by in (-1, 0, 1):
        joined = None
        for bx in (-1, 0, 1):
            value = block(by, bx)
            pieces = []
            for q in range(3):
                piece = jnp.where(x_in // 4 == q, value, 0.0)
                moved = (4 * (bx + 1 - q)) % 128
                pieces.append(pltpu.roll(piece, moved, 1) if moved else piece)
            joined = pieces if joined is None else [x + y for x, y in zip(joined, pieces)]
        flow_one.append(joined[0])
        flow_two.append(joined[1])
        masks.append(joined[2])

    not_first_x = (gx > 0).astype(jnp.int32)
    not_last_x = (gx < nx - 1).astype(jnp.int32)
    inside_x = jnp.where(
        x_in < 4, not_first_x, jnp.where(x_in < 8, 1, jnp.where(x_in < 12, not_last_x, 0))
    ).astype(f32)
    row_valid = [(gy > 0).astype(jnp.int32), 1, (gy < ny - 1).astype(jnp.int32)]
    inside = [inside_x * jnp.asarray(v, jnp.int32).astype(f32) for v in row_valid]

    def up(value, steps):
        return pltpu.roll(value, 8 - steps, 0)

    def down(value, steps):
        return pltpu.roll(value, steps, 0)

    steady, weights = [], []
    for b in range(3):
        w1 = jnp.where(depth + 1 < nz, masks[b] * up(masks[b], 1), 0.0)
        w2 = jnp.where(depth + 2 < nz, masks[b] * up(masks[b], 2), 0.0)
        l1, l2 = down(w1, 1), down(w2, 2)
        pull = (
            l1 * down(flow_one[b], 1)
            + l2 * down(flow_two[b], 2)
            - w1 * flow_one[b]
            - w2 * flow_two[b]
        )
        steady.append(pull)
        weights.append((w1, w2, l1, l2, w1 + w2 + l1 + l2))

    u = [STEP_SIZE * steady[b] * inside[b] for b in range(3)]
    for _ in range(RELAX - 1):
        fresh = []
        for b in range(3):
            value = u[b]
            below = pltpu.roll(value, 128 - 16, 1)
            above = pltpu.roll(value, 16, 1)
            edge_below = pltpu.roll(u[b + 1], 48, 1) if b < 2 else jnp.zeros_like(value)
            edge_above = pltpu.roll(u[b - 1], 128 - 48, 1) if b > 0 else jnp.zeros_like(value)
            below = jnp.where(y_in == 3, edge_below, below)
            above = jnp.where(y_in == 0, edge_above, above)
            laplace = (
                below + above + pltpu.roll(value, 1, 1) + pltpu.roll(value, 127, 1) - 4.0 * value
            )
            w1, w2, l1, l2, total = weights[b]
            forces = STIFFNESS * laplace + steady[b] - total * value
            forces = forces + w1 * up(value, 1) + w2 * up(value, 2)
            forces = forces + l1 * down(value, 1) + l2 * down(value, 2)
            fresh.append((value + STEP_SIZE * forces) * inside[b])
        u = fresh

    row = jnp.sum(jnp.where(depth == gz, u[1], 0.0), axis=0, keepdims=True)
    for comp in range(2):
        write(offset_ref, comp, row, 64 * comp + 4)

    for s in range(3):
        for d, (dy, dx) in enumerate(DIRECTIONS):

            @pl.when(exists(dy, dx) & (gz + s < nz))
            def _():
                halo_copy(s, d).wait_send()

    for s in (1, 2):

        @pl.when((gz > 0) & (gz + s - 1 < nz))
        def _():
            tile_copy(s).wait_send()

    for dz in range(1, nz):
        col_copy(dz, gz).wait_send()
    for d, (dy, dx) in enumerate(DIRECTIONS):

        @pl.when(exists(dy, dx))
        def _():
            plane_copy(d).wait_send()


def solution(mesh):
    sizes = tuple(mesh.shape[name] for name in ("gz", "gy", "gx"))
    f32, bf16 = jnp.float32, jnp.bfloat16
    column_table = column_tables()
    row_tab, left_tab = parity_tables()
    right_tab = right_inverse()
    constants = (column_table, row_tab, left_tab, right_tab)

    def body(images, tissue_mask):
        vmem = pl.BlockSpec(memory_space=pltpu.VMEM)
        anywhere = pl.BlockSpec(memory_space=pltpu.HBM)
        dma = pltpu.SemaphoreType.DMA
        return pl.pallas_call(
            functools.partial(kernel, sizes),
            out_shape=(
                jax.ShapeDtypeStruct((4, 1, 4, 4), f32),
                jax.ShapeDtypeStruct((2, 1, 4, 4), f32),
            ),
            in_specs=[anywhere] * 6,
            out_specs=(vmem, vmem),
            scratch_shapes=[
                pltpu.VMEM((3, 4, ROWS, LANES), bf16),
                pltpu.VMEM(column_table.shape, bf16),
                pltpu.VMEM(row_tab.shape, bf16),
                pltpu.VMEM(left_tab.shape, bf16),
                pltpu.VMEM(right_tab.shape, bf16),
                pltpu.VMEM((3, 4, ROWS, LANES), f32),
                pltpu.VMEM((3, 4, ROWS, LANES), f32),
                pltpu.VMEM((3, 4, ROWS, LANES), f32),
                pltpu.VMEM((3, 4, ROWS, LANES), f32),
                pltpu.VMEM((4 * PATCH, 512), bf16),
                pltpu.VMEM((4 * PATCH, 512), bf16),
                pltpu.VMEM((3, 8, 176, 256), f32),
                pltpu.VMEM((3, 2, 16, 8, LANES), f32),
                pltpu.VMEM((8, LANES), f32),
                pltpu.VMEM((8, 1, LANES), f32),
                pltpu.VMEM((8, 8, 1, LANES), f32),
                pltpu.VMEM((1, TILE, TILE), bf16),
                pltpu.VMEM((1, 4, 4), jnp.int32),
                dma((6,)),
                dma((3, 8)),
                dma((3, 8)),
                dma((2,)),
                dma((2,)),
                dma((7,)),
                dma((7,)),
                dma((8,)),
                dma((8,)),
                pltpu.SemaphoreType.REGULAR,
                pltpu.SemaphoreType.REGULAR,
            ],
            compiler_params=pltpu.CompilerParams(
                collective_id=0, has_side_effects=True, vmem_limit_bytes=56 * 1024 * 1024
            ),
        )(images, tissue_mask, *[jnp.asarray(x) for x in constants])

    return jax.shard_map(
        body,
        mesh=mesh,
        in_specs=(P("gz", "gy", "gx"), P("gz", "gy", "gx")),
        out_specs=(P(None, "gz", "gy", "gx"), P(None, "gz", "gy", "gx")),
        check_vma=False,
    )
```

```python
import functools
import math

import jax
import jax.numpy as jnp
import numpy as np
from jax import lax
from jax.experimental import pallas as pl
from jax.experimental.pallas import tpu as pltpu
from jax.sharding import PartitionSpec as P

PATCH = 160
STRIDE = 40
RELAX = 4
EPSILON = 1e-06
STIFFNESS = 0.5
STEP_SIZE = 0.2

TILE = 160
HALO = 64
ROWS = TILE + 2 * HALO
LANES = 128
FIRST = 208
SECOND = ROWS - FIRST
MESH = pl.DeviceIdType.MESH
DIRECTIONS = [(dy, dx) for dy in (-1, 0, 1) for dx in (-1, 0, 1) if (dy, dx) != (0, 0)]


def split_np(table):
    bf16 = jnp.bfloat16
    high = np.asarray(table, np.float32).astype(bf16)
    low = (np.asarray(table, np.float64) - high.astype(np.float64)).astype(np.float32).astype(bf16)
    return high, low


def cosine(product):
    return np.cos(2.0 * np.pi * (product % PATCH) / PATCH)


def sine(product):
    phase = product % (PATCH // 2)
    return np.where(phase == 0, 0.0, np.sin(2.0 * np.pi * (product % PATCH) / PATCH))


def column_tables():
    freq = np.arange(81)
    out = []
    for j in range(4):
        lane = np.arange(256)
        if j == 0:
            column = lane - 128
            good = lane >= 0
        elif j == 1:
            column = np.where(lane < 108, 32 + lane, lane - 128)
            good = lane >= 96
        elif j == 2:
            column = np.where(lane < 128, 32 + lane, np.where(lane < 148, 32 + lane, lane - 128))
            good = lane < 160
        else:
            column = 32 + lane
            good = lane >= 0
        m = column - (40 * j - 60)
        good = good & (m >= 0) & (m < PATCH)
        product = m[:, None] * freq[None, :]
        table = np.zeros((256, 256))
        table[:, 0:81] = cosine(product) * good[:, None]
        table[:, 128:209] = sine(product) * good[:, None]
        high, low = split_np(table)
        out.append(np.concatenate([high, low], 0))
    return np.stack(out)


def parity_tables():
    low = np.arange(40)
    forward, inverse = [], []
    scale = np.where(low == 0, 1.0, 2.0) / PATCH
    for parity in range(2):
        n = 2 * np.arange(80) + parity
        product = low[:, None] * n[None]
        cos_part, sin_part = cosine(product), sine(product)
        sin_part[0] = cosine(40 * n) if parity == 0 else sine(40 * n)
        sin_scale = np.where(low == 0, 2.0, 2.0) / PATCH
        table = np.concatenate([cos_part, sin_part], 0)
        high, part = split_np(table)
        forward.append(np.concatenate([high, part, high], 1))
        table = np.concatenate([cos_part * scale[:, None], sin_part * sin_scale[:, None]], 0).T
        high, part = split_np(table)
        inverse.append(np.concatenate([high, high, part], 1))
    return np.stack(forward), np.stack(inverse)


def right_inverse():
    freq = np.arange(81)
    scale = np.where((freq == 0) | (freq == 80), 1.0, 2.0) / PATCH
    product = freq[:, None] * np.arange(PATCH)[None]
    right = np.zeros((256, 256))
    right[0:81, 0:PATCH] = cosine(product) * scale[:, None]
    right[128:209, 0:PATCH] = sine(product) * scale[:, None]
    high, low = split_np(right)
    return np.concatenate([high, high, low], 0)


def kernel(
    sizes,
    image_hbm,
    mask_hbm,
    column_hbm,
    row_hbm,
    left_hbm,
    right_hbm,
    flow_ref,
    offset_ref,
    buf,
    column_table,
    row_tab,
    left_tab,
    right_tab,
    y_a,
    y_b,
    y_c,
    y_d,
    rows_a,
    rows_b,
    spec,
    red,
    tile_scr,
    colb,
    plane,
    image_ref,
    mask_ref,
    table_sem,
    halo_send,
    halo_recv,
    tile_send,
    tile_recv,
    col_send,
    col_recv,
    plane_send,
    plane_recv,
    near_sem,
    far_sem,
    wide_sem,
):
    nz, ny, nx = sizes
    gz, gy, gx = lax.axis_index("gz"), lax.axis_index("gy"), lax.axis_index("gx")
    f32, bf16 = jnp.float32, jnp.bfloat16
    y_parts, rows_buf = (y_a, y_b, y_c, y_d), (rows_a, rows_b)

    tables = [
        pltpu.make_async_copy(source, target, table_sem.at[k])
        for k, (source, target) in enumerate(
            (
                (image_hbm, image_ref),
                (mask_hbm, mask_ref),
                (column_hbm, column_table),
                (row_hbm, row_tab),
                (left_hbm, left_tab),
                (right_hbm, right_tab),
            )
        )
    ]
    for copy in tables:
        copy.start()

    def exists(dy, dx):
        ok = None
        for step, position, count in ((dy, gy, ny), (dx, gx, nx)):
            term = None
            if step < 0:
                term = position > 0
            elif step > 0:
                term = position < count - 1
            if term is not None:
                ok = term if ok is None else ok & term
        return ok

    core = lax.rem(gy, 2)
    first_core, second_core = core == 0, core == 1
    base_gy = gy - core
    layer = gy // 2
    layers = ny // 2

    def count(*conditions):
        return sum(jnp.asarray(c).astype(jnp.int32) for c in conditions)

    barrier = pltpu.get_barrier_semaphore()

    @pl.when(second_core)
    def _():
        pl.semaphore_signal(barrier, inc=1, device_id={"gy": base_gy}, device_id_type=MESH)

    for dx in (-1, 1):

        @pl.when(exists(0, dx))
        def _():
            pl.semaphore_signal(
                barrier, inc=1, device_id={"gy": base_gy, "gx": gx + dx}, device_id_type=MESH
            )

    for step, present in ((-1, gz > 0), (1, gz < nz - 1)):

        @pl.when(present)
        def _():
            pl.semaphore_signal(
                barrier, inc=1, device_id={"gz": gz + step, "gy": base_gy}, device_id_type=MESH
            )

    for dz in range(1, nz):
        other = lax.rem(gz + dz, nz)

        @pl.when((other != gz - 1) & (other != gz + 1))
        def _():
            pl.semaphore_signal(
                barrier,
                inc=1,
                device_id={"gz": other, "gy": base_gy + 1},
                device_id_type=MESH,
            )

    for dx in (-1, 0, 1):
        inside_x = True if dx == 0 else exists(0, dx)

        @pl.when(second_core & (layer < layers - 1) & inside_x)
        def _():
            pl.semaphore_signal(
                barrier, inc=1, device_id={"gy": gy + 2, "gx": gx + dx}, device_id_type=MESH
            )

        @pl.when(first_core & (layer > 0) & inside_x)
        def _():
            pl.semaphore_signal(
                barrier, inc=1, device_id={"gy": gy - 1, "gx": gx + dx}, device_id_type=MESH
            )

    tables[0].wait()
    image = image_ref[0]
    buf[0, 1, HALO : HALO + TILE, :] = image[:, 0:128]
    buf[0, 2, HALO : HALO + TILE, :] = image[:, 32:160]
    zeros = jnp.zeros((HALO, LANES), bf16)

    @pl.when(gy == 0)
    def _():
        for s in range(3):
            for t in range(4):
                buf[s, t, 0:HALO, :] = zeros

    @pl.when(gy == ny - 1)
    def _():
        for s in range(3):
            for t in range(4):
                buf[s, t, HALO + TILE : ROWS, :] = zeros

    @pl.when(gx == 0)
    def _():
        for s in range(3):
            buf[s, 0] = jnp.zeros((ROWS, LANES), bf16)

    @pl.when(gx == nx - 1)
    def _():
        for s in range(3):
            buf[s, 3] = jnp.zeros((ROWS, LANES), bf16)

    for d, (dy, dx) in enumerate(DIRECTIONS):

        @pl.when(jnp.logical_not(exists(-dy, -dx)))
        def _():
            plane[d] = jnp.zeros((8, 1, LANES), f32)

    if nz < 8:
        colb[...] = jnp.zeros((8, 1, LANES), f32)
        for d in range(8):
            plane[d] = jnp.zeros((8, 1, LANES), f32)

    tables[1].wait()
    tile_scr[...] = jnp.zeros((8, LANES), f32)
    tile_scr[0:4, 0:4] = mask_ref[0].astype(f32)
    mask_tile = tile_scr[...]
    mask_row = mask_tile[0:1]
    for y in range(1, 4):
        mask_row = mask_row + pltpu.roll(mask_tile[y : y + 1], 16 * y, 1)
    mask_row = pltpu.roll(mask_row, 8, 1) + pltpu.roll(mask_row, 72, 1)

    beside = count(gx > 0, gx < nx - 1)
    adjacent = count(gz > 0, gz < nz - 1)

    @pl.when(first_core)
    def _():
        pl.semaphore_wait(barrier, 1 + 2 * adjacent + 2 * beside)
        pl.semaphore_signal(near_sem, inc=1, device_id={"gy": gy + 1}, device_id_type=MESH)

    @pl.when(second_core)
    def _():
        pl.semaphore_wait(near_sem, 1)

    def far_barrier():
        @pl.when(second_core)
        def _():
            pl.semaphore_wait(
                barrier,
                (1 + beside) * count(layer > 0, layer < layers - 1)
                + 2 * (nz - 1 - adjacent),
            )
            pl.semaphore_signal(far_sem, inc=1, device_id={"gy": gy - 1}, device_id_type=MESH)

        @pl.when(first_core)
        def _():
            pl.semaphore_wait(far_sem, 1)

        for dz in range(1, nz):
            pl.semaphore_signal(
                wide_sem, inc=1, device_id={"gz": lax.rem(gz + dz, nz)}, device_id_type=MESH
            )

    top, middle, bottom = (0, HALO), (HALO, TILE), (HALO + TILE, HALO)

    def halo_copy(s, d):
        dy, dx = DIRECTIONS[d]
        source_rows = {-1: (HALO, HALO), 0: middle, 1: (TILE, HALO)}[dy]
        target_rows = {-1: bottom, 0: middle, 1: top}[dy]
        source_tiles = {-1: (1, 1), 0: (1, 2), 1: (2, 1)}[dx]
        target_tiles = {-1: (3, 1), 0: (1, 2), 1: (0, 1)}[dx]
        return pltpu.make_async_remote_copy(
            src_ref=buf.at[s, pl.ds(*source_tiles), pl.ds(*source_rows)],
            dst_ref=buf.at[s, pl.ds(*target_tiles), pl.ds(*target_rows)],
            send_sem=halo_send.at[s, d],
            recv_sem=halo_recv.at[s, d],
            device_id={"gy": gy + dy, "gx": gx + dx},
            device_id_type=MESH,
        )

    def tile_copy(s):
        return pltpu.make_async_remote_copy(
            src_ref=buf.at[s - 1, pl.ds(1, 2), pl.ds(*middle)],
            dst_ref=buf.at[s, pl.ds(1, 2), pl.ds(*middle)],
            send_sem=tile_send.at[s - 1],
            recv_sem=tile_recv.at[s - 1],
            device_id={"gz": gz - 1},
            device_id_type=MESH,
        )

    def is_near(dy):
        if dy == 0:
            return True
        return first_core if dy > 0 else second_core

    def send_halos(s, near):
        for d, (dy, dx) in enumerate(DIRECTIONS):
            if dy == 0 and not near:
                continue
            side = is_near(dy) if near else jnp.logical_not(is_near(dy))

            @pl.when(exists(dy, dx) & side)
            def _():
                halo_copy(s, d).start()

    def receive_halos(s, near):
        for d, (dy, dx) in enumerate(DIRECTIONS):
            if dy == 0 and not near:
                continue
            side = is_near(-dy) if near else jnp.logical_not(is_near(-dy))

            @pl.when(exists(-dy, -dx) & side)
            def _():
                halo_copy(s, d).wait_recv()

    @pl.when(gz > 0)
    def _():
        tile_copy(1).start()

    send_halos(0, True)

    def relay(s):
        @pl.when(gz + s < nz)
        def _():
            tile_copy(s).wait_recv()
            if s == 1:

                @pl.when(gz > 0)
                def _():
                    tile_copy(2).start()

            send_halos(s, True)

    first_row = lax.broadcasted_iota(jnp.int32, (8, 256), 0) == 0

    def spectra(s, slot, base, rows, top, between):
        area = pl.ds(base, rows)
        lane = lax.broadcasted_iota(jnp.int32, (rows, LANES), 1)
        left, tile_a, tile_b, right = (buf[s, t, area, :] for t in range(4))
        windows = (
            (left, tile_a),
            (jnp.where(lane < 108, tile_b, left), tile_a),
            (tile_b, jnp.where(lane < 20, right, tile_a)),
            (tile_b, right),
        )
        for j, (first, second) in enumerate(windows):
            y = jnp.dot(
                jnp.concatenate([first, second, first, second], 1),
                column_table[j],
                preferred_element_type=f32,
            )
            high = y.astype(bf16).astype(f32)
            low = y - high
            for t in range(2):
                cut = slice(128 * t, 128 * t + 128)
                y_parts[j][s, t, area, :] = high[:, cut]
                y_parts[j][s, 2 + t, area, :] = low[:, cut]
        between()
        for j in range(4):
            for k in range(2):
                start = 4 + 40 * (top + k)
                both = []
                for parity in range(2):
                    window = pl.ds(start + parity, 80, 2)
                    high, low = (
                        jnp.concatenate(
                            [y_parts[j][s, q + t, window, :].astype(bf16) for t in range(2)], 1
                        )
                        for q in (0, 2)
                    )
                    both.append(
                        jnp.dot(
                            row_tab[parity],
                            jnp.concatenate([high, high, low], 0),
                            preferred_element_type=f32,
                        )
                    )
                even, odd = both
                n = j * 2 + k
                spec[slot, n, 0:40] = even[0:40] + odd[0:40]
                spec[slot, n, 40:80] = even[0:40] - odd[0:40]
                total, rest = even[40:80] + odd[40:80], odd[40:80] - even[40:80]
                spec[slot, n, 80:88] = jnp.where(first_row, 0.0, total[0:8])
                spec[slot, n, 88:120] = total[8:40]
                spec[slot, n, 120:128] = jnp.where(first_row, 0.0, rest[0:8])
                spec[slot, n, 128:160] = rest[8:40]
                spec[slot, n, 160:168] = jnp.where(first_row, even[40:48], 0.0)
                spec[slot, n, 168:176] = jnp.where(first_row, odd[40:48], 0.0)

    shift_lane = lax.broadcasted_iota(jnp.int32, (8, LANES), 1)
    shift_low = (lax.rem(shift_lane + 80, PATCH) - 80).astype(f32)
    twice_sub = (2 * lax.broadcasted_iota(jnp.int32, (8, LANES), 0)).astype(f32)
    shift_high = (shift_lane - 32).astype(f32)

    def cross(own, n, cos_rows, sin_rows):
        cos_lanes, sin_lanes = slice(0, 128), slice(128, 256)
        ccs, css = spec[own, n, cos_rows, cos_lanes], spec[own, n, cos_rows, sin_lanes]
        scs, sss = spec[own, n, sin_rows, cos_lanes], spec[own, n, sin_rows, sin_lanes]
        cct, cst = spec[2, n, cos_rows, cos_lanes], spec[2, n, cos_rows, sin_lanes]
        sct, sst = spec[2, n, sin_rows, cos_lanes], spec[2, n, sin_rows, sin_lanes]
        q_cc = cct * ccs + sst * sss + cst * css + sct * scs
        q_ss = cct * sss + sst * ccs - cst * scs - sct * css
        q_cs = cst * ccs + sst * scs - cct * css - sct * sss
        q_sc = sct * ccs + sst * css - cct * scs - cst * sss
        return jnp.concatenate([q_cc, q_cs], 1), jnp.concatenate([q_sc, q_ss], 1)

    def transform_rows(own, n, target, m):
        cos_low, sin_low = cross(own, n, slice(0, 40), slice(80, 120))
        cos_high, sin_high = cross(own, n, slice(40, 80), slice(120, 160))
        cos_mid, sin_mid = cross(own, n, slice(160, 168), slice(168, 176))
        parts = (
            (cos_low + cos_high, sin_low - sin_high, cos_mid),
            (cos_low - cos_high, sin_low + sin_high, sin_mid),
        )
        for parity, (cos_part, sin_part, mid) in enumerate(parts):
            q = jnp.concatenate([cos_part, sin_part[0:8] + mid, sin_part[8:40]], 0)
            high = q.astype(bf16)
            low = (q - high.astype(f32)).astype(bf16)
            v = jnp.dot(
                left_tab[parity],
                jnp.concatenate([high, low, high], 0),
                preferred_element_type=f32,
            )
            high = v.astype(bf16)
            low = (v - high.astype(f32)).astype(bf16)
            place = slice(160 * m + 80 * parity, 160 * m + 80 * parity + 80)
            target[place, 0:256] = high
            target[place, 256:512] = low

    def moments(c, index, node):
        tail, total, weighted = None, None, []
        for parity in range(2):
            running = ramp = None
            for block in range(9, -1, -1):
                start = 80 * parity + 8 * block
                value = c[start : start + 8]
                square = value * value
                weight = square * square
                near, far = weight[:, 0:128], weight[:, 128:256]
                tail = far if tail is None else tail + far
                joined = near + far
                running = joined if running is None else running + joined
                if block > 0:
                    ramp = running if ramp is None else ramp + running
                if block == 5:
                    wrapped = running
            weighted.append(16.0 * ramp - float(PATCH) * wrapped)
            total = running if total is None else total + running
        red[0, index, node] = total
        red[1, index, node] = weighted[0] + weighted[1] + running + total * twice_sub
        red[2, index, node] = total * shift_low + tail * (shift_high - shift_low)

    def correlate(own, index, top):
        def columns(g):
            high, low = rows_buf[g][:, 0:256], rows_buf[g][:, 256:512]
            c = jnp.dot(
                jnp.concatenate([high, low, high], 1), right_tab[...], preferred_element_type=f32
            )
            for m in range(4):
                node = (2 * g + m // 2) * 4 + top + m % 2
                moments(c[160 * m : 160 * m + 160], index, node)

        for m in range(4):
            transform_rows(own, m, rows_buf[0], m)
        for m in range(4):
            transform_rows(own, 4 + m, rows_buf[1], m)
        columns(0)
        columns(1)

    for copy in tables[2:]:
        copy.wait()

    halves = (
        (pl.multiple_of(jnp.where(first_core, SECOND, 0), 16), FIRST, jnp.where(first_core, 2, 0)),
        (pl.multiple_of(jnp.where(first_core, 0, FIRST), 16), SECOND, jnp.where(first_core, 0, 2)),
    )

    def run(half, first, last):
        base, rows, top_patch = halves[half]

        def per_section(s, carry):
            @pl.when(gz + s < nz)
            def _():
                receive_halos(s, half == 0)

            def between():
                if half == 0 and first == 0:

                    @pl.when(s == 0)
                    def _():
                        relay(1)

            spectra(s, jnp.where(s == 0, half, 2), base, rows, top_patch, between)
            if half == 0 and first == 0:

                @pl.when(s == 0)
                def _():
                    far_barrier()
                    send_halos(0, False)

                    @pl.when(gz + 1 < nz)
                    def _():
                        send_halos(1, False)

            if last > 0:

                @pl.when(s > 0)
                def _():
                    correlate(half, s - 1, top_patch)

            return carry

        lax.fori_loop(first, last + 1, per_section, 0)

    run(0, 0, 1)
    relay(2)

    @pl.when(gz + 2 < nz)
    def _():
        send_halos(2, False)

    run(1, 0, 1)
    run(0, 2, 2)
    run(1, 2, 2)

    place_lane = lax.broadcasted_iota(jnp.int32, (16, LANES), 1)
    place_node = lax.broadcasted_iota(jnp.int32, (16, LANES), 0)
    target = lax.rem(place_node, 4) * 16 + place_node // 4
    flow_rows = []
    for a in range(2):
        parts = [
            jnp.sum(jnp.sum(red[q, a], axis=1), axis=1, keepdims=True) for q in range(3)
        ]
        total = parts[0] + EPSILON
        flow_y = jnp.broadcast_to(parts[1] / total, (16, LANES))
        flow_x = jnp.broadcast_to(parts[2] / total, (16, LANES))
        placed = jnp.where(place_lane == target, flow_y, 0.0) + jnp.where(
            place_lane == target + 64, flow_x, 0.0
        )
        row = jnp.sum(placed, axis=0, keepdims=True)
        row = jnp.where(gz + a + 1 < nz, row, 0.0)
        flow_rows.append(row)
    colb[gz] = flow_rows[0] + pltpu.roll(flow_rows[1], 4, 1) + mask_row

    def write(ref, index, row, lane_base):
        for y in range(4):
            start = lane_base + 16 * y
            moved = pltpu.roll(row, (128 - start) % 128, 1) if start % 128 else row
            ref[index, 0, y : y + 1, :] = moved[:, 0:4]

    def col_copy(dz, slot):
        return pltpu.make_async_remote_copy(
            src_ref=colb.at[gz],
            dst_ref=colb.at[slot],
            send_sem=col_send.at[dz - 1],
            recv_sem=col_recv.at[dz - 1],
            device_id={"gz": lax.rem(gz + dz, nz)},
            device_id_type=MESH,
        )

    def plane_copy(d, dz):
        dy, dx = DIRECTIONS[d]
        return pltpu.make_async_remote_copy(
            src_ref=colb.at[gz],
            dst_ref=plane.at[d, gz],
            send_sem=plane_send.at[d],
            recv_sem=plane_recv.at[d],
            device_id={"gz": lax.rem(gz + dz, nz), "gy": gy + dy, "gx": gx + dx},
            device_id_type=MESH,
        )

    def plane_total(d):
        dy, dx = DIRECTIONS[d]
        return pltpu.make_async_remote_copy(
            src_ref=plane.at[d, pl.ds(0, nz)],
            dst_ref=plane.at[d, pl.ds(0, nz)],
            send_sem=plane_send.at[d],
            recv_sem=plane_recv.at[d],
            device_id={"gy": gy + dy, "gx": gx + dx},
            device_id_type=MESH,
        )

    pl.semaphore_wait(wide_sem, nz - 1)
    order = sorted(range(8), key=lambda d: -abs(DIRECTIONS[d][0]) - abs(DIRECTIONS[d][1]))
    for d in order:

        @pl.when(exists(*DIRECTIONS[d]))
        def _():
            for dz in range(nz):
                plane_copy(d, dz).start()

    for dz in range(1, nz):
        col_copy(dz, gz).start()

    for a in range(2):
        for comp in range(2):
            write(flow_ref, 2 * a + comp, flow_rows[a], 64 * comp)

    for dz in range(1, nz):
        col_copy(dz, lax.rem(gz + nz - dz, nz)).wait_recv()

    for d, (dy, dx) in enumerate(DIRECTIONS):

        @pl.when(exists(-dy, -dx))
        def _():
            plane_total(d).wait_recv()

    def block(by, bx):
        if (by, bx) == (0, 0):
            return colb[:, 0, :]
        return plane[DIRECTIONS.index((-by, -bx)), :, 0, :]

    lanes8 = lax.broadcasted_iota(jnp.int32, (8, LANES), 1)
    depth = lax.broadcasted_iota(jnp.int32, (8, LANES), 0)
    x_in = lax.rem(lanes8, 16)
    y_in = lax.rem(lanes8 // 16, 4)
    flow_one, flow_two, masks = [], [], []
    for by in (-1, 0, 1):
        joined = None
        for bx in (-1, 0, 1):
            value = block(by, bx)
            pieces = []
            for q in range(3):
                piece = jnp.where(x_in // 4 == q, value, 0.0)
                moved = (4 * (bx + 1 - q)) % 128
                pieces.append(pltpu.roll(piece, moved, 1) if moved else piece)
            joined = pieces if joined is None else [x + y for x, y in zip(joined, pieces)]
        flow_one.append(joined[0])
        flow_two.append(joined[1])
        masks.append(joined[2])

    not_first_x = (gx > 0).astype(jnp.int32)
    not_last_x = (gx < nx - 1).astype(jnp.int32)
    inside_x = jnp.where(
        x_in < 4, not_first_x, jnp.where(x_in < 8, 1, jnp.where(x_in < 12, not_last_x, 0))
    ).astype(f32)
    row_valid = [(gy > 0).astype(jnp.int32), 1, (gy < ny - 1).astype(jnp.int32)]
    inside = [inside_x * jnp.asarray(v, jnp.int32).astype(f32) for v in row_valid]

    def up(value, steps):
        return pltpu.roll(value, 8 - steps, 0)

    def down(value, steps):
        return pltpu.roll(value, steps, 0)

    steady, weights = [], []
    for b in range(3):
        w1 = jnp.where(depth + 1 < nz, masks[b] * up(masks[b], 1), 0.0)
        w2 = jnp.where(depth + 2 < nz, masks[b] * up(masks[b], 2), 0.0)
        l1, l2 = down(w1, 1), down(w2, 2)
        pull = (
            l1 * down(flow_one[b], 1)
            + l2 * down(flow_two[b], 2)
            - w1 * flow_one[b]
            - w2 * flow_two[b]
        )
        steady.append(pull)
        weights.append((w1, w2, l1, l2, w1 + w2 + l1 + l2))

    u = [STEP_SIZE * steady[b] * inside[b] for b in range(3)]
    for _ in range(RELAX - 1):
        fresh = []
        for b in range(3):
            value = u[b]
            below = pltpu.roll(value, 128 - 16, 1)
            above = pltpu.roll(value, 16, 1)
            edge_below = pltpu.roll(u[b + 1], 48, 1) if b < 2 else jnp.zeros_like(value)
            edge_above = pltpu.roll(u[b - 1], 128 - 48, 1) if b > 0 else jnp.zeros_like(value)
            below = jnp.where(y_in == 3, edge_below, below)
            above = jnp.where(y_in == 0, edge_above, above)
            laplace = (
                below + above + pltpu.roll(value, 1, 1) + pltpu.roll(value, 127, 1) - 4.0 * value
            )
            w1, w2, l1, l2, total = weights[b]
            forces = STIFFNESS * laplace + steady[b] - total * value
            forces = forces + w1 * up(value, 1) + w2 * up(value, 2)
            forces = forces + l1 * down(value, 1) + l2 * down(value, 2)
            fresh.append((value + STEP_SIZE * forces) * inside[b])
        u = fresh

    row = jnp.sum(jnp.where(depth == gz, u[1], 0.0), axis=0, keepdims=True)
    for comp in range(2):
        write(offset_ref, comp, row, 64 * comp + 4)

    for s in range(3):
        for d, (dy, dx) in enumerate(DIRECTIONS):

            @pl.when(exists(dy, dx) & (gz + s < nz))
            def _():
                halo_copy(s, d).wait_send()

    for s in (1, 2):

        @pl.when((gz > 0) & (gz + s - 1 < nz))
        def _():
            tile_copy(s).wait_send()

    for dz in range(1, nz):
        col_copy(dz, gz).wait_send()
    for d, (dy, dx) in enumerate(DIRECTIONS):

        @pl.when(exists(dy, dx))
        def _():
            plane_total(d).wait_send()


def solution(mesh):
    sizes = tuple(mesh.shape[name] for name in ("gz", "gy", "gx"))
    f32, bf16 = jnp.float32, jnp.bfloat16
    column_table = column_tables()
    row_tab, left_tab = parity_tables()
    right_tab = right_inverse()
    constants = (column_table, row_tab, left_tab, right_tab)

    def body(images, tissue_mask):
        vmem = pl.BlockSpec(memory_space=pltpu.VMEM)
        anywhere = pl.BlockSpec(memory_space=pltpu.HBM)
        dma = pltpu.SemaphoreType.DMA
        return pl.pallas_call(
            functools.partial(kernel, sizes),
            out_shape=(
                jax.ShapeDtypeStruct((4, 1, 4, 4), f32),
                jax.ShapeDtypeStruct((2, 1, 4, 4), f32),
            ),
            in_specs=[anywhere] * 6,
            out_specs=(vmem, vmem),
            scratch_shapes=[
                pltpu.VMEM((3, 4, ROWS, LANES), bf16),
                pltpu.VMEM(column_table.shape, bf16),
                pltpu.VMEM(row_tab.shape, bf16),
                pltpu.VMEM(left_tab.shape, bf16),
                pltpu.VMEM(right_tab.shape, bf16),
                pltpu.VMEM((3, 4, ROWS, LANES), f32),
                pltpu.VMEM((3, 4, ROWS, LANES), f32),
                pltpu.VMEM((3, 4, ROWS, LANES), f32),
                pltpu.VMEM((3, 4, ROWS, LANES), f32),
                pltpu.VMEM((4 * PATCH, 512), bf16),
                pltpu.VMEM((4 * PATCH, 512), bf16),
                pltpu.VMEM((3, 8, 176, 256), f32),
                pltpu.VMEM((3, 2, 16, 8, LANES), f32),
                pltpu.VMEM((8, LANES), f32),
                pltpu.VMEM((8, 1, LANES), f32),
                pltpu.VMEM((8, 8, 1, LANES), f32),
                pltpu.VMEM((1, TILE, TILE), bf16),
                pltpu.VMEM((1, 4, 4), jnp.int32),
                dma((6,)),
                dma((3, 8)),
                dma((3, 8)),
                dma((2,)),
                dma((2,)),
                dma((7,)),
                dma((7,)),
                dma((8,)),
                dma((8,)),
                pltpu.SemaphoreType.REGULAR,
                pltpu.SemaphoreType.REGULAR,
                pltpu.SemaphoreType.REGULAR,
            ],
            compiler_params=pltpu.CompilerParams(
                collective_id=0, has_side_effects=True, vmem_limit_bytes=56 * 1024 * 1024
            ),
        )(images, tissue_mask, *[jnp.asarray(x) for x in constants])

    return jax.shard_map(
        body,
        mesh=mesh,
        in_specs=(P("gz", "gy", "gx"), P("gz", "gy", "gx")),
        out_specs=(P(None, "gz", "gy", "gx"), P(None, "gz", "gy", "gx")),
        check_vma=False,
    )
```

```python
import functools
import math

import jax
import jax.numpy as jnp
import numpy as np
from jax import lax
from jax.experimental import pallas as pl
from jax.experimental.pallas import tpu as pltpu
from jax.sharding import PartitionSpec as P

PATCH = 160
STRIDE = 40
RELAX = 4
EPSILON = 1e-06
STIFFNESS = 0.5
STEP_SIZE = 0.2

TILE = 160
HALO = 64
ROWS = TILE + 2 * HALO
LANES = 128
FIRST = 208
SECOND = ROWS - FIRST
MESH = pl.DeviceIdType.MESH
DIRECTIONS = [(dy, dx) for dy in (-1, 0, 1) for dx in (-1, 0, 1) if (dy, dx) != (0, 0)]


def split_np(table):
    bf16 = jnp.bfloat16
    high = np.asarray(table, np.float32).astype(bf16)
    low = (np.asarray(table, np.float64) - high.astype(np.float64)).astype(np.float32).astype(bf16)
    return high, low


def cosine(product):
    return np.cos(2.0 * np.pi * (product % PATCH) / PATCH)


def sine(product):
    phase = product % (PATCH // 2)
    return np.where(phase == 0, 0.0, np.sin(2.0 * np.pi * (product % PATCH) / PATCH))


def column_tables():
    freq = np.arange(81)
    out = []
    for j in range(4):
        lane = np.arange(256)
        if j == 0:
            column = lane - 128
            good = lane >= 0
        elif j == 1:
            column = np.where(lane < 108, 32 + lane, lane - 128)
            good = lane >= 96
        elif j == 2:
            column = np.where(lane < 128, 32 + lane, np.where(lane < 148, 32 + lane, lane - 128))
            good = lane < 160
        else:
            column = 32 + lane
            good = lane >= 0
        m = column - (40 * j - 60)
        good = good & (m >= 0) & (m < PATCH)
        product = m[:, None] * freq[None, :]
        table = np.zeros((256, 256))
        table[:, 0:81] = cosine(product) * good[:, None]
        table[:, 128:209] = sine(product) * good[:, None]
        high, low = split_np(table)
        out.append(np.concatenate([high, low], 0))
    return np.stack(out)


def parity_tables():
    low = np.arange(40)
    forward, inverse = [], []
    scale = np.where(low == 0, 1.0, 2.0) / PATCH
    for parity in range(2):
        n = 2 * np.arange(80) + parity
        product = low[:, None] * n[None]
        cos_part, sin_part = cosine(product), sine(product)
        sin_part[0] = cosine(40 * n) if parity == 0 else sine(40 * n)
        sin_scale = np.where(low == 0, 2.0, 2.0) / PATCH
        table = np.concatenate([cos_part, sin_part], 0)
        high, part = split_np(table)
        forward.append(np.concatenate([high, part, high], 1))
        table = np.concatenate([cos_part * scale[:, None], sin_part * sin_scale[:, None]], 0).T
        high, part = split_np(table)
        inverse.append(np.concatenate([high, high, part], 1))
    return np.stack(forward), np.stack(inverse)


def right_inverse():
    freq = np.arange(81)
    scale = np.where((freq == 0) | (freq == 80), 1.0, 2.0) / PATCH
    product = freq[:, None] * np.arange(PATCH)[None]
    right = np.zeros((256, 256))
    right[0:81, 0:PATCH] = cosine(product) * scale[:, None]
    right[128:209, 0:PATCH] = sine(product) * scale[:, None]
    high, low = split_np(right)
    return np.concatenate([high, high, low], 0)


def kernel(
    sizes,
    image_hbm,
    mask_hbm,
    column_hbm,
    row_hbm,
    left_hbm,
    right_hbm,
    flow_ref,
    offset_ref,
    buf,
    column_table,
    row_tab,
    left_tab,
    right_tab,
    y_a,
    y_b,
    y_c,
    y_d,
    rows_a,
    rows_b,
    spec,
    red,
    tile_scr,
    colb,
    plane,
    image_ref,
    mask_ref,
    table_sem,
    halo_send,
    halo_recv,
    tile_send,
    tile_recv,
    col_send,
    col_recv,
    plane_send,
    plane_recv,
    near_sem,
    far_sem,
    wide_sem,
):
    nz, ny, nx = sizes
    gz, gy, gx = lax.axis_index("gz"), lax.axis_index("gy"), lax.axis_index("gx")
    f32, bf16 = jnp.float32, jnp.bfloat16
    y_parts, rows_buf = (y_a, y_b, y_c, y_d), (rows_a, rows_b)

    tables = [
        pltpu.make_async_copy(source, target, table_sem.at[k])
        for k, (source, target) in enumerate(
            (
                (image_hbm, image_ref),
                (mask_hbm, mask_ref),
                (column_hbm, column_table),
                (row_hbm, row_tab),
                (left_hbm, left_tab),
                (right_hbm, right_tab),
            )
        )
    ]
    for copy in tables:
        copy.start()

    def exists(dy, dx):
        ok = None
        for step, position, count in ((dy, gy, ny), (dx, gx, nx)):
            term = None
            if step < 0:
                term = position > 0
            elif step > 0:
                term = position < count - 1
            if term is not None:
                ok = term if ok is None else ok & term
        return ok

    core = lax.rem(gy, 2)
    first_core, second_core = core == 0, core == 1
    base_gy = gy - core
    layer = gy // 2
    layers = ny // 2

    def count(*conditions):
        return sum(jnp.asarray(c).astype(jnp.int32) for c in conditions)

    barrier = pltpu.get_barrier_semaphore()

    @pl.when(second_core)
    def _():
        pl.semaphore_signal(barrier, inc=1, device_id={"gy": base_gy}, device_id_type=MESH)

    for dx in (-1, 1):

        @pl.when(exists(0, dx))
        def _():
            pl.semaphore_signal(
                barrier, inc=1, device_id={"gy": base_gy, "gx": gx + dx}, device_id_type=MESH
            )

    for step, present in ((-1, gz > 0), (1, gz < nz - 1)):

        @pl.when(present)
        def _():
            pl.semaphore_signal(
                barrier, inc=1, device_id={"gz": gz + step, "gy": base_gy}, device_id_type=MESH
            )

    tables[0].wait()
    image = image_ref[0]
    buf[0, 1, HALO : HALO + TILE, :] = image[:, 0:128]
    buf[0, 2, HALO : HALO + TILE, :] = image[:, 32:160]
    beside = count(gx > 0, gx < nx - 1)
    adjacent = count(gz > 0, gz < nz - 1)

    @pl.when(first_core)
    def _():
        pl.semaphore_wait(barrier, 1 + 2 * adjacent + 2 * beside)
        pl.semaphore_signal(near_sem, inc=1, device_id={"gy": gy + 1}, device_id_type=MESH)

    @pl.when(second_core)
    def _():
        pl.semaphore_wait(near_sem, 1)

    def far_barrier():
        @pl.when(second_core)
        def _():
            pl.semaphore_wait(
                barrier,
                (1 + beside) * count(layer > 0, layer < layers - 1)
                + 2 * (nz - 1 - adjacent),
            )
            pl.semaphore_signal(far_sem, inc=1, device_id={"gy": gy - 1}, device_id_type=MESH)

        @pl.when(first_core)
        def _():
            pl.semaphore_wait(far_sem, 1)

        for dz in range(1, nz):
            pl.semaphore_signal(
                wide_sem, inc=1, device_id={"gz": lax.rem(gz + dz, nz)}, device_id_type=MESH
            )

    top, middle, bottom = (0, HALO), (HALO, TILE), (HALO + TILE, HALO)

    def halo_copy(s, d):
        dy, dx = DIRECTIONS[d]
        source_rows = {-1: (HALO, HALO), 0: middle, 1: (TILE, HALO)}[dy]
        target_rows = {-1: bottom, 0: middle, 1: top}[dy]
        source_tiles = {-1: (1, 1), 0: (1, 2), 1: (2, 1)}[dx]
        target_tiles = {-1: (3, 1), 0: (1, 2), 1: (0, 1)}[dx]
        return pltpu.make_async_remote_copy(
            src_ref=buf.at[s, pl.ds(*source_tiles), pl.ds(*source_rows)],
            dst_ref=buf.at[s, pl.ds(*target_tiles), pl.ds(*target_rows)],
            send_sem=halo_send.at[s, d],
            recv_sem=halo_recv.at[s, d],
            device_id={"gy": gy + dy, "gx": gx + dx},
            device_id_type=MESH,
        )

    def tile_copy(s, t):
        return pltpu.make_async_remote_copy(
            src_ref=buf.at[s - 1, t, pl.ds(*middle)],
            dst_ref=buf.at[s, t, pl.ds(*middle)],
            send_sem=tile_send.at[s - 1, t - 1],
            recv_sem=tile_recv.at[s - 1, t - 1],
            device_id={"gz": gz - 1},
            device_id_type=MESH,
        )

    def is_near(dy):
        if dy == 0:
            return True
        return first_core if dy > 0 else second_core

    def send_halos(s, near, steps=(-1, 0, 1)):
        for d, (dy, dx) in enumerate(DIRECTIONS):
            if (dy == 0 and not near) or dx not in steps:
                continue
            side = is_near(dy) if near else jnp.logical_not(is_near(dy))

            @pl.when(exists(dy, dx) & side)
            def _():
                halo_copy(s, d).start()

    def receive_halos(s, near):
        for d, (dy, dx) in enumerate(DIRECTIONS):
            if dy == 0 and not near:
                continue
            side = is_near(-dy) if near else jnp.logical_not(is_near(-dy))

            @pl.when(exists(-dy, -dx) & side)
            def _():
                halo_copy(s, d).wait_recv()

    @pl.when(gz > 0)
    def _():
        tile_copy(1, 1).start()
        tile_copy(1, 2).start()

    send_halos(0, True)

    for dz in range(1, nz):
        other = lax.rem(gz + dz, nz)

        @pl.when((other != gz - 1) & (other != gz + 1))
        def _():
            pl.semaphore_signal(
                barrier,
                inc=1,
                device_id={"gz": other, "gy": base_gy + 1},
                device_id_type=MESH,
            )

    for dx in (-1, 0, 1):
        inside_x = True if dx == 0 else exists(0, dx)

        @pl.when(second_core & (layer < layers - 1) & inside_x)
        def _():
            pl.semaphore_signal(
                barrier, inc=1, device_id={"gy": gy + 2, "gx": gx + dx}, device_id_type=MESH
            )

        @pl.when(first_core & (layer > 0) & inside_x)
        def _():
            pl.semaphore_signal(
                barrier, inc=1, device_id={"gy": gy - 1, "gx": gx + dx}, device_id_type=MESH
            )

    zeros = jnp.zeros((HALO, LANES), bf16)

    @pl.when(gy == 0)
    def _():
        for s in range(3):
            for t in range(4):
                buf[s, t, 0:HALO, :] = zeros

    @pl.when(gy == ny - 1)
    def _():
        for s in range(3):
            for t in range(4):
                buf[s, t, HALO + TILE : ROWS, :] = zeros

    @pl.when(gx == 0)
    def _():
        for s in range(3):
            buf[s, 0] = jnp.zeros((ROWS, LANES), bf16)

    @pl.when(gx == nx - 1)
    def _():
        for s in range(3):
            buf[s, 3] = jnp.zeros((ROWS, LANES), bf16)

    for d, (dy, dx) in enumerate(DIRECTIONS):

        @pl.when(jnp.logical_not(exists(-dy, -dx)))
        def _():
            plane[d] = jnp.zeros((8, 1, LANES), f32)

    if nz < 8:
        colb[...] = jnp.zeros((8, 1, LANES), f32)
        for d in range(8):
            plane[d] = jnp.zeros((8, 1, LANES), f32)

    tables[1].wait()
    tile_scr[...] = jnp.zeros((8, LANES), f32)
    tile_scr[0:4, 0:4] = mask_ref[0].astype(f32)
    mask_tile = tile_scr[...]
    mask_row = mask_tile[0:1]
    for y in range(1, 4):
        mask_row = mask_row + pltpu.roll(mask_tile[y : y + 1], 16 * y, 1)
    mask_row = pltpu.roll(mask_row, 8, 1) + pltpu.roll(mask_row, 72, 1)

    def relay(s):
        @pl.when(gz + s < nz)
        def _():
            for t in (1, 2):
                tile_copy(s, t).wait_recv()
                if s == 1:

                    @pl.when(gz > 0)
                    def _():
                        tile_copy(2, t).start()

                send_halos(s, True, (-1,) if t == 1 else (0, 1))

    first_row = lax.broadcasted_iota(jnp.int32, (8, 256), 0) == 0

    def spectra(s, slot, base, rows, top, between):
        area = pl.ds(base, rows)
        lane = lax.broadcasted_iota(jnp.int32, (rows, LANES), 1)
        left, tile_a, tile_b, right = (buf[s, t, area, :] for t in range(4))
        windows = (
            (left, tile_a),
            (jnp.where(lane < 108, tile_b, left), tile_a),
            (tile_b, jnp.where(lane < 20, right, tile_a)),
            (tile_b, right),
        )
        for j, (first, second) in enumerate(windows):
            y = jnp.dot(
                jnp.concatenate([first, second, first, second], 1),
                column_table[j],
                preferred_element_type=f32,
            )
            high = y.astype(bf16).astype(f32)
            low = y - high
            for t in range(2):
                cut = slice(128 * t, 128 * t + 128)
                y_parts[j][s, t, area, :] = high[:, cut]
                y_parts[j][s, 2 + t, area, :] = low[:, cut]
        between()
        for j in range(4):
            for k in range(2):
                start = 4 + 40 * (top + k)
                both = []
                for parity in range(2):
                    window = pl.ds(start + parity, 80, 2)
                    high, low = (
                        jnp.concatenate(
                            [y_parts[j][s, q + t, window, :].astype(bf16) for t in range(2)], 1
                        )
                        for q in (0, 2)
                    )
                    both.append(
                        jnp.dot(
                            row_tab[parity],
                            jnp.concatenate([high, high, low], 0),
                            preferred_element_type=f32,
                        )
                    )
                even, odd = both
                n = j * 2 + k
                spec[slot, n, 0:40] = even[0:40] + odd[0:40]
                spec[slot, n, 40:80] = even[0:40] - odd[0:40]
                total, rest = even[40:80] + odd[40:80], odd[40:80] - even[40:80]
                spec[slot, n, 80:88] = jnp.where(first_row, 0.0, total[0:8])
                spec[slot, n, 88:120] = total[8:40]
                spec[slot, n, 120:128] = jnp.where(first_row, 0.0, rest[0:8])
                spec[slot, n, 128:160] = rest[8:40]
                spec[slot, n, 160:168] = jnp.where(first_row, even[40:48], 0.0)
                spec[slot, n, 168:176] = jnp.where(first_row, odd[40:48], 0.0)

    shift_lane = lax.broadcasted_iota(jnp.int32, (8, LANES), 1)
    shift_low = (lax.rem(shift_lane + 80, PATCH) - 80).astype(f32)
    twice_sub = (2 * lax.broadcasted_iota(jnp.int32, (8, LANES), 0)).astype(f32)
    shift_high = (shift_lane - 32).astype(f32)

    def cross(own, n, cos_rows, sin_rows):
        cos_lanes, sin_lanes = slice(0, 128), slice(128, 256)
        ccs, css = spec[own, n, cos_rows, cos_lanes], spec[own, n, cos_rows, sin_lanes]
        scs, sss = spec[own, n, sin_rows, cos_lanes], spec[own, n, sin_rows, sin_lanes]
        cct, cst = spec[2, n, cos_rows, cos_lanes], spec[2, n, cos_rows, sin_lanes]
        sct, sst = spec[2, n, sin_rows, cos_lanes], spec[2, n, sin_rows, sin_lanes]
        q_cc = cct * ccs + sst * sss + cst * css + sct * scs
        q_ss = cct * sss + sst * ccs - cst * scs - sct * css
        q_cs = cst * ccs + sst * scs - cct * css - sct * sss
        q_sc = sct * ccs + sst * css - cct * scs - cst * sss
        return jnp.concatenate([q_cc, q_cs], 1), jnp.concatenate([q_sc, q_ss], 1)

    def transform_rows(own, n, target, m):
        cos_low, sin_low = cross(own, n, slice(0, 40), slice(80, 120))
        cos_high, sin_high = cross(own, n, slice(40, 80), slice(120, 160))
        cos_mid, sin_mid = cross(own, n, slice(160, 168), slice(168, 176))
        parts = (
            (cos_low + cos_high, sin_low - sin_high, cos_mid),
            (cos_low - cos_high, sin_low + sin_high, sin_mid),
        )
        for parity, (cos_part, sin_part, mid) in enumerate(parts):
            q = jnp.concatenate([cos_part, sin_part[0:8] + mid, sin_part[8:40]], 0)
            high = q.astype(bf16)
            low = (q - high.astype(f32)).astype(bf16)
            v = jnp.dot(
                left_tab[parity],
                jnp.concatenate([high, low, high], 0),
                preferred_element_type=f32,
            )
            high = v.astype(bf16)
            low = (v - high.astype(f32)).astype(bf16)
            place = slice(160 * m + 80 * parity, 160 * m + 80 * parity + 80)
            target[place, 0:256] = high
            target[place, 256:512] = low

    def moments(c, index, node):
        tail, total, weighted = None, None, []
        for parity in range(2):
            running = ramp = None
            for block in range(9, -1, -1):
                start = 80 * parity + 8 * block
                value = c[start : start + 8]
                square = value * value
                weight = square * square
                near, far = weight[:, 0:128], weight[:, 128:256]
                tail = far if tail is None else tail + far
                joined = near + far
                running = joined if running is None else running + joined
                if block > 0:
                    ramp = running if ramp is None else ramp + running
                if block == 5:
                    wrapped = running
            weighted.append(16.0 * ramp - float(PATCH) * wrapped)
            total = running if total is None else total + running
        red[0, index, node] = total
        red[1, index, node] = weighted[0] + weighted[1] + running + total * twice_sub
        red[2, index, node] = total * shift_low + tail * (shift_high - shift_low)

    def correlate(own, index, top):
        def columns(g):
            high, low = rows_buf[g][:, 0:256], rows_buf[g][:, 256:512]
            c = jnp.dot(
                jnp.concatenate([high, low, high], 1), right_tab[...], preferred_element_type=f32
            )
            for m in range(4):
                node = (2 * g + m // 2) * 4 + top + m % 2
                moments(c[160 * m : 160 * m + 160], index, node)

        for m in range(4):
            transform_rows(own, m, rows_buf[0], m)
        for m in range(4):
            transform_rows(own, 4 + m, rows_buf[1], m)
        columns(0)
        columns(1)

    for copy in tables[2:]:
        copy.wait()

    halves = (
        (pl.multiple_of(jnp.where(first_core, SECOND, 0), 16), FIRST, jnp.where(first_core, 2, 0)),
        (pl.multiple_of(jnp.where(first_core, 0, FIRST), 16), SECOND, jnp.where(first_core, 0, 2)),
    )

    def run(half, first, last):
        base, rows, top_patch = halves[half]

        def per_section(s, carry):
            @pl.when(gz + s < nz)
            def _():
                receive_halos(s, half == 0)

            def between():
                if half == 0 and first == 0:

                    @pl.when(s == 0)
                    def _():
                        relay(1)

            spectra(s, jnp.where(s == 0, half, 2), base, rows, top_patch, between)
            if half == 0 and first == 0:

                @pl.when(s == 0)
                def _():
                    far_barrier()
                    send_halos(0, False)

                    @pl.when(gz + 1 < nz)
                    def _():
                        send_halos(1, False)

            if last > 0:

                @pl.when(s > 0)
                def _():
                    correlate(half, s - 1, top_patch)

            return carry

        lax.fori_loop(first, last + 1, per_section, 0)

    run(0, 0, 1)
    relay(2)

    @pl.when(gz + 2 < nz)
    def _():
        send_halos(2, False)

    place_lane = lax.broadcasted_iota(jnp.int32, (16, LANES), 1)
    place_node = lax.broadcasted_iota(jnp.int32, (16, LANES), 0)
    target = lax.rem(place_node, 4) * 16 + place_node // 4

    def flow_row(a):
        parts = [
            jnp.sum(jnp.sum(red[q, a], axis=1), axis=1, keepdims=True) for q in range(3)
        ]
        total = parts[0] + EPSILON
        flow_y = jnp.broadcast_to(parts[1] / total, (16, LANES))
        flow_x = jnp.broadcast_to(parts[2] / total, (16, LANES))
        placed = jnp.where(place_lane == target, flow_y, 0.0) + jnp.where(
            place_lane == target + 64, flow_x, 0.0
        )
        row = jnp.sum(placed, axis=0, keepdims=True)
        return jnp.where(gz + a + 1 < nz, row, 0.0)

    run(1, 0, 1)
    flow_rows = [flow_row(0)]
    early = flow_rows[0] + mask_row
    run(0, 2, 2)
    run(1, 2, 2)
    flow_rows.append(flow_row(1))

    colb[gz] = early + pltpu.roll(flow_rows[1], 4, 1)

    def write(ref, index, row, lane_base):
        for y in range(4):
            start = lane_base + 16 * y
            moved = pltpu.roll(row, (128 - start) % 128, 1) if start % 128 else row
            ref[index, 0, y : y + 1, :] = moved[:, 0:4]

    def col_copy(dz, slot):
        return pltpu.make_async_remote_copy(
            src_ref=colb.at[gz],
            dst_ref=colb.at[slot],
            send_sem=col_send.at[dz - 1],
            recv_sem=col_recv.at[dz - 1],
            device_id={"gz": lax.rem(gz + dz, nz)},
            device_id_type=MESH,
        )

    def plane_copy(d, dz):
        dy, dx = DIRECTIONS[d]
        return pltpu.make_async_remote_copy(
            src_ref=colb.at[gz],
            dst_ref=plane.at[d, gz],
            send_sem=plane_send.at[d],
            recv_sem=plane_recv.at[d],
            device_id={"gz": lax.rem(gz + dz, nz), "gy": gy + dy, "gx": gx + dx},
            device_id_type=MESH,
        )

    def plane_total(d):
        dy, dx = DIRECTIONS[d]
        return pltpu.make_async_remote_copy(
            src_ref=plane.at[d, pl.ds(0, nz)],
            dst_ref=plane.at[d, pl.ds(0, nz)],
            send_sem=plane_send.at[d],
            recv_sem=plane_recv.at[d],
            device_id={"gy": gy + dy, "gx": gx + dx},
            device_id_type=MESH,
        )

    pl.semaphore_wait(wide_sem, nz - 1)
    order = sorted(range(8), key=lambda d: -abs(DIRECTIONS[d][0]) - abs(DIRECTIONS[d][1]))
    for d in order:

        @pl.when(exists(*DIRECTIONS[d]))
        def _():
            for dz in range(nz):
                plane_copy(d, dz).start()

    for dz in range(1, nz):
        col_copy(dz, gz).start()

    for a in range(2):
        for comp in range(2):
            write(flow_ref, 2 * a + comp, flow_rows[a], 64 * comp)

    for dz in range(1, nz):
        col_copy(dz, lax.rem(gz + nz - dz, nz)).wait_recv()

    for d, (dy, dx) in enumerate(DIRECTIONS):

        @pl.when(exists(-dy, -dx))
        def _():
            plane_total(d).wait_recv()

    def block(by, bx):
        if (by, bx) == (0, 0):
            return colb[:, 0, :]
        return plane[DIRECTIONS.index((-by, -bx)), :, 0, :]

    lanes8 = lax.broadcasted_iota(jnp.int32, (8, LANES), 1)
    depth = lax.broadcasted_iota(jnp.int32, (8, LANES), 0)
    x_in = lax.rem(lanes8, 16)
    y_in = lax.rem(lanes8 // 16, 4)
    flow_one, flow_two, masks = [], [], []
    for by in (-1, 0, 1):
        joined = None
        for bx in (-1, 0, 1):
            value = block(by, bx)
            pieces = []
            for q in range(3):
                piece = jnp.where(x_in // 4 == q, value, 0.0)
                moved = (4 * (bx + 1 - q)) % 128
                pieces.append(pltpu.roll(piece, moved, 1) if moved else piece)
            joined = pieces if joined is None else [x + y for x, y in zip(joined, pieces)]
        flow_one.append(joined[0])
        flow_two.append(joined[1])
        masks.append(joined[2])

    not_first_x = (gx > 0).astype(jnp.int32)
    not_last_x = (gx < nx - 1).astype(jnp.int32)
    inside_x = jnp.where(
        x_in < 4, not_first_x, jnp.where(x_in < 8, 1, jnp.where(x_in < 12, not_last_x, 0))
    ).astype(f32)
    row_valid = [(gy > 0).astype(jnp.int32), 1, (gy < ny - 1).astype(jnp.int32)]
    inside = [inside_x * jnp.asarray(v, jnp.int32).astype(f32) for v in row_valid]

    def up(value, steps):
        return pltpu.roll(value, 8 - steps, 0)

    def down(value, steps):
        return pltpu.roll(value, steps, 0)

    steady, weights = [], []
    for b in range(3):
        w1 = jnp.where(depth + 1 < nz, masks[b] * up(masks[b], 1), 0.0)
        w2 = jnp.where(depth + 2 < nz, masks[b] * up(masks[b], 2), 0.0)
        l1, l2 = down(w1, 1), down(w2, 2)
        pull = (
            l1 * down(flow_one[b], 1)
            + l2 * down(flow_two[b], 2)
            - w1 * flow_one[b]
            - w2 * flow_two[b]
        )
        steady.append(pull)
        weights.append((w1, w2, l1, l2, w1 + w2 + l1 + l2))

    u = [STEP_SIZE * steady[b] * inside[b] for b in range(3)]
    for _ in range(RELAX - 1):
        fresh = []
        for b in range(3):
            value = u[b]
            below = pltpu.roll(value, 128 - 16, 1)
            above = pltpu.roll(value, 16, 1)
            edge_below = pltpu.roll(u[b + 1], 48, 1) if b < 2 else jnp.zeros_like(value)
            edge_above = pltpu.roll(u[b - 1], 128 - 48, 1) if b > 0 else jnp.zeros_like(value)
            below = jnp.where(y_in == 3, edge_below, below)
            above = jnp.where(y_in == 0, edge_above, above)
            laplace = (
                below + above + pltpu.roll(value, 1, 1) + pltpu.roll(value, 127, 1) - 4.0 * value
            )
            w1, w2, l1, l2, total = weights[b]
            forces = STIFFNESS * laplace + steady[b] - total * value
            forces = forces + w1 * up(value, 1) + w2 * up(value, 2)
            forces = forces + l1 * down(value, 1) + l2 * down(value, 2)
            fresh.append((value + STEP_SIZE * forces) * inside[b])
        u = fresh

    row = jnp.sum(jnp.where(depth == gz, u[1], 0.0), axis=0, keepdims=True)
    for comp in range(2):
        write(offset_ref, comp, row, 64 * comp + 4)

    for s in range(3):
        for d, (dy, dx) in enumerate(DIRECTIONS):

            @pl.when(exists(dy, dx) & (gz + s < nz))
            def _():
                halo_copy(s, d).wait_send()

    for s in (1, 2):

        @pl.when((gz > 0) & (gz + s - 1 < nz))
        def _():
            tile_copy(s, 1).wait_send()
            tile_copy(s, 2).wait_send()

    for dz in range(1, nz):
        col_copy(dz, gz).wait_send()
    for d, (dy, dx) in enumerate(DIRECTIONS):

        @pl.when(exists(dy, dx))
        def _():
            plane_total(d).wait_send()


def solution(mesh):
    sizes = tuple(mesh.shape[name] for name in ("gz", "gy", "gx"))
    f32, bf16 = jnp.float32, jnp.bfloat16
    column_table = column_tables()
    row_tab, left_tab = parity_tables()
    right_tab = right_inverse()
    constants = (column_table, row_tab, left_tab, right_tab)

    def body(images, tissue_mask):
        vmem = pl.BlockSpec(memory_space=pltpu.VMEM)
        anywhere = pl.BlockSpec(memory_space=pltpu.HBM)
        dma = pltpu.SemaphoreType.DMA
        return pl.pallas_call(
            functools.partial(kernel, sizes),
            out_shape=(
                jax.ShapeDtypeStruct((4, 1, 4, 4), f32),
                jax.ShapeDtypeStruct((2, 1, 4, 4), f32),
            ),
            in_specs=[anywhere] * 6,
            out_specs=(vmem, vmem),
            scratch_shapes=[
                pltpu.VMEM((3, 4, ROWS, LANES), bf16),
                pltpu.VMEM(column_table.shape, bf16),
                pltpu.VMEM(row_tab.shape, bf16),
                pltpu.VMEM(left_tab.shape, bf16),
                pltpu.VMEM(right_tab.shape, bf16),
                pltpu.VMEM((3, 4, ROWS, LANES), f32),
                pltpu.VMEM((3, 4, ROWS, LANES), f32),
                pltpu.VMEM((3, 4, ROWS, LANES), f32),
                pltpu.VMEM((3, 4, ROWS, LANES), f32),
                pltpu.VMEM((4 * PATCH, 512), bf16),
                pltpu.VMEM((4 * PATCH, 512), bf16),
                pltpu.VMEM((3, 8, 176, 256), f32),
                pltpu.VMEM((3, 2, 16, 8, LANES), f32),
                pltpu.VMEM((8, LANES), f32),
                pltpu.VMEM((8, 1, LANES), f32),
                pltpu.VMEM((8, 8, 1, LANES), f32),
                pltpu.VMEM((1, TILE, TILE), bf16),
                pltpu.VMEM((1, 4, 4), jnp.int32),
                dma((6,)),
                dma((3, 8)),
                dma((3, 8)),
                dma((2, 2)),
                dma((2, 2)),
                dma((7,)),
                dma((7,)),
                dma((8,)),
                dma((8,)),
                pltpu.SemaphoreType.REGULAR,
                pltpu.SemaphoreType.REGULAR,
                pltpu.SemaphoreType.REGULAR,
            ],
            compiler_params=pltpu.CompilerParams(
                collective_id=0, has_side_effects=True, vmem_limit_bytes=32 * 1024 * 1024
            ),
        )(*[pltpu.with_memory_space_constraint(x, pltpu.HBM) for x in (images, tissue_mask, *[jnp.asarray(x) for x in constants])])

    return jax.shard_map(
        body,
        mesh=mesh,
        in_specs=(P("gz", "gy", "gx"), P("gz", "gy", "gx")),
        out_specs=(P(None, "gz", "gy", "gx"), P(None, "gz", "gy", "gx")),
        check_vma=False,
    )
```

```python
import functools
import math

import jax
import jax.numpy as jnp
import numpy as np
from jax import lax
from jax.experimental import pallas as pl
from jax.experimental.pallas import tpu as pltpu
from jax.sharding import PartitionSpec as P

PATCH = 160
STRIDE = 40
RELAX = 4
EPSILON = 1e-06
STIFFNESS = 0.5
STEP_SIZE = 0.2

TILE = 160
HALO = 64
ROWS = TILE + 2 * HALO
LANES = 128
FIRST = 208
SECOND = ROWS - FIRST
STRIP = 48
MESH = pl.DeviceIdType.MESH
DIRECTIONS = [(dy, dx) for dy in (-1, 0, 1) for dx in (-1, 0, 1) if (dy, dx) != (0, 0)]


def split_np(table):
    bf16 = jnp.bfloat16
    high = np.asarray(table, np.float32).astype(bf16)
    low = (np.asarray(table, np.float64) - high.astype(np.float64)).astype(np.float32).astype(bf16)
    return high, low


def cosine(product):
    return np.cos(2.0 * np.pi * (product % PATCH) / PATCH)


def sine(product):
    phase = product % (PATCH // 2)
    return np.where(phase == 0, 0.0, np.sin(2.0 * np.pi * (product % PATCH) / PATCH))


def column_tables():
    freq = np.arange(81)
    out = []
    for j in range(4):
        lane = np.arange(256)
        if j == 0:
            column = lane - 128
            good = lane >= 0
        elif j == 1:
            column = np.where(lane < 108, 32 + lane, lane - 128)
            good = lane >= 96
        elif j == 2:
            column = np.where(lane < 128, 32 + lane, np.where(lane < 148, 32 + lane, lane - 128))
            good = lane < 160
        else:
            column = 32 + lane
            good = lane >= 0
        m = column - (40 * j - 60)
        good = good & (m >= 0) & (m < PATCH)
        product = m[:, None] * freq[None, :]
        table = np.zeros((256, 256))
        table[:, 0:81] = cosine(product) * good[:, None]
        table[:, 128:209] = sine(product) * good[:, None]
        high, low = split_np(table)
        out.append(np.concatenate([high, low], 0))
    return np.stack(out)


def parity_tables():
    low = np.arange(40)
    forward, inverse = [], []
    scale = np.where(low == 0, 1.0, 2.0) / PATCH
    for parity in range(2):
        n = 2 * np.arange(80) + parity
        product = low[:, None] * n[None]
        cos_part, sin_part = cosine(product), sine(product)
        sin_part[0] = cosine(40 * n) if parity == 0 else sine(40 * n)
        sin_scale = np.where(low == 0, 2.0, 2.0) / PATCH
        table = np.concatenate([cos_part, sin_part], 0)
        high, part = split_np(table)
        forward.append(np.concatenate([high, part, high], 1))
        table = np.concatenate([cos_part * scale[:, None], sin_part * sin_scale[:, None]], 0).T
        high, part = split_np(table)
        inverse.append(np.concatenate([high, high, part], 1))
    return np.stack(forward), np.stack(inverse)


def right_inverse():
    freq = np.arange(81)
    scale = np.where((freq == 0) | (freq == 80), 1.0, 2.0) / PATCH
    product = freq[:, None] * np.arange(PATCH)[None]
    right = np.zeros((256, 256))
    right[0:81, 0:PATCH] = cosine(product) * scale[:, None]
    right[128:209, 0:PATCH] = sine(product) * scale[:, None]
    high, low = split_np(right)
    return np.concatenate([high, high, low], 0)


def kernel(
    sizes,
    image_hbm,
    mask_hbm,
    column_hbm,
    row_hbm,
    left_hbm,
    right_hbm,
    flow_ref,
    offset_ref,
    buf,
    strips,
    column_table,
    row_tab,
    left_tab,
    right_tab,
    y_a,
    y_b,
    y_c,
    y_d,
    rows_a,
    rows_b,
    spec,
    red,
    tile_scr,
    colb,
    plane,
    image_ref,
    mask_ref,
    table_sem,
    halo_send,
    halo_recv,
    tile_send,
    tile_recv,
    col_send,
    col_recv,
    plane_send,
    plane_recv,
    near_sem,
    far_sem,
    wide_sem,
):
    nz, ny, nx = sizes
    gz, gy, gx = lax.axis_index("gz"), lax.axis_index("gy"), lax.axis_index("gx")
    f32, bf16 = jnp.float32, jnp.bfloat16
    y_parts, rows_buf = (y_a, y_b, y_c, y_d), (rows_a, rows_b)

    tables = [
        pltpu.make_async_copy(source, target, table_sem.at[k])
        for k, (source, target) in enumerate(
            (
                (image_hbm, image_ref),
                (mask_hbm, mask_ref),
                (column_hbm, column_table),
                (row_hbm, row_tab),
                (left_hbm, left_tab),
                (right_hbm, right_tab),
            )
        )
    ]
    for copy in tables:
        copy.start()

    def exists(dy, dx):
        ok = None
        for step, position, count in ((dy, gy, ny), (dx, gx, nx)):
            term = None
            if step < 0:
                term = position > 0
            elif step > 0:
                term = position < count - 1
            if term is not None:
                ok = term if ok is None else ok & term
        return ok

    core = lax.rem(gy, 2)
    first_core, second_core = core == 0, core == 1
    base_gy = gy - core
    layer = gy // 2
    layers = ny // 2

    def count(*conditions):
        return sum(jnp.asarray(c).astype(jnp.int32) for c in conditions)

    barrier = pltpu.get_barrier_semaphore()

    @pl.when(second_core)
    def _():
        pl.semaphore_signal(barrier, inc=1, device_id={"gy": base_gy}, device_id_type=MESH)

    for dx in (-1, 1):

        @pl.when(exists(0, dx))
        def _():
            pl.semaphore_signal(
                barrier, inc=1, device_id={"gy": base_gy, "gx": gx + dx}, device_id_type=MESH
            )

    for step, present in ((-1, gz > 0), (1, gz < nz - 1)):

        @pl.when(present)
        def _():
            pl.semaphore_signal(
                barrier, inc=1, device_id={"gz": gz + step, "gy": base_gy}, device_id_type=MESH
            )

    tables[0].wait()
    image = image_ref[0]
    buf[0, 1, HALO : HALO + TILE, :] = image[:, 0:128]
    buf[0, 2, HALO : HALO + TILE, :] = image[:, 32:160]
    strip_lane = lax.broadcasted_iota(jnp.int32, (STRIP, LANES), 1)
    last_columns = buf[0, 2, HALO : HALO + TILE, :].astype(f32)
    strip = jnp.zeros((STRIP, LANES), f32)
    for q in range(4):
        count_q = min(STRIP, TILE - STRIP * q)
        piece = pltpu.roll(last_columns[STRIP * q : STRIP * q + count_q], (32 + 32 * q) % 128, 1)
        if count_q < STRIP:
            piece = jnp.concatenate([piece, jnp.zeros((STRIP - count_q, LANES), f32)], 0)
        strip = jnp.where(strip_lane // 32 == q, piece, strip)
    strips[0] = strip.astype(bf16)
    beside = count(gx > 0, gx < nx - 1)
    adjacent = count(gz > 0, gz < nz - 1)

    @pl.when(first_core)
    def _():
        pl.semaphore_wait(barrier, 1 + 2 * adjacent + 2 * beside)
        pl.semaphore_signal(near_sem, inc=1, device_id={"gy": gy + 1}, device_id_type=MESH)

    @pl.when(second_core)
    def _():
        pl.semaphore_wait(near_sem, 1)

    def far_barrier():
        @pl.when(second_core)
        def _():
            pl.semaphore_wait(
                barrier,
                (1 + beside) * count(layer > 0, layer < layers - 1)
                + 2 * (nz - 1 - adjacent),
            )
            pl.semaphore_signal(far_sem, inc=1, device_id={"gy": gy - 1}, device_id_type=MESH)

        @pl.when(first_core)
        def _():
            pl.semaphore_wait(far_sem, 1)

        for dz in range(1, nz):
            pl.semaphore_signal(
                wide_sem, inc=1, device_id={"gz": lax.rem(gz + dz, nz)}, device_id_type=MESH
            )

    top, middle, bottom = (0, HALO), (HALO, TILE), (HALO + TILE, HALO)

    def halo_copy(s, d):
        dy, dx = DIRECTIONS[d]
        source_rows = {-1: (HALO, HALO), 0: middle, 1: (TILE, HALO)}[dy]
        target_rows = {-1: bottom, 0: middle, 1: top}[dy]
        source_tiles = {-1: (1, 1), 0: (1, 2), 1: (2, 1)}[dx]
        target_tiles = {-1: (3, 1), 0: (1, 2), 1: (0, 1)}[dx]
        return pltpu.make_async_remote_copy(
            src_ref=buf.at[s, pl.ds(*source_tiles), pl.ds(*source_rows)],
            dst_ref=buf.at[s, pl.ds(*target_tiles), pl.ds(*target_rows)],
            send_sem=halo_send.at[s, d],
            recv_sem=halo_recv.at[s, d],
            device_id={"gy": gy + dy, "gx": gx + dx},
            device_id_type=MESH,
        )

    def tile_copy(s, t):
        if t == 1:
            source, target = buf.at[s - 1, 1, pl.ds(*middle)], buf.at[s, 1, pl.ds(*middle)]
        else:
            source, target = strips.at[s - 1], strips.at[s]
        return pltpu.make_async_remote_copy(
            src_ref=source,
            dst_ref=target,
            send_sem=tile_send.at[s - 1, t - 1],
            recv_sem=tile_recv.at[s - 1, t - 1],
            device_id={"gz": gz - 1},
            device_id_type=MESH,
        )

    def rebuild(s):
        moved = pltpu.roll(buf[s, 1, HALO : HALO + TILE, :].astype(f32), 96, 1)
        packed = strips[s].astype(f32)
        for q in range(4):
            count_q = min(STRIP, TILE - STRIP * q)
            rows = slice(STRIP * q, STRIP * q + count_q)
            piece = pltpu.roll(packed, (96 - 32 * q) % 128, 1) if q < 3 else packed
            lane_q = lax.broadcasted_iota(jnp.int32, (count_q, LANES), 1)
            buf[s, 2, HALO + STRIP * q : HALO + STRIP * q + count_q, :] = jnp.where(
                lane_q < 96, moved[rows], piece[0:count_q]
            ).astype(bf16)

    def is_near(dy):
        if dy == 0:
            return True
        return first_core if dy > 0 else second_core

    def send_halos(s, near, steps=(-1, 0, 1)):
        for d, (dy, dx) in enumerate(DIRECTIONS):
            if (dy == 0 and not near) or dx not in steps:
                continue
            side = is_near(dy) if near else jnp.logical_not(is_near(dy))

            @pl.when(exists(dy, dx) & side)
            def _():
                halo_copy(s, d).start()

    def receive_halos(s, near):
        for d, (dy, dx) in enumerate(DIRECTIONS):
            if dy == 0 and not near:
                continue
            side = is_near(-dy) if near else jnp.logical_not(is_near(-dy))

            @pl.when(exists(-dy, -dx) & side)
            def _():
                halo_copy(s, d).wait_recv()

    @pl.when(gz > 0)
    def _():
        tile_copy(1, 1).start()
        tile_copy(1, 2).start()

    send_halos(0, True)

    for dz in range(1, nz):
        other = lax.rem(gz + dz, nz)

        @pl.when((other != gz - 1) & (other != gz + 1))
        def _():
            pl.semaphore_signal(
                barrier,
                inc=1,
                device_id={"gz": other, "gy": base_gy + 1},
                device_id_type=MESH,
            )

    for dx in (-1, 0, 1):
        inside_x = True if dx == 0 else exists(0, dx)

        @pl.when(second_core & (layer < layers - 1) & inside_x)
        def _():
            pl.semaphore_signal(
                barrier, inc=1, device_id={"gy": gy + 2, "gx": gx + dx}, device_id_type=MESH
            )

        @pl.when(first_core & (layer > 0) & inside_x)
        def _():
            pl.semaphore_signal(
                barrier, inc=1, device_id={"gy": gy - 1, "gx": gx + dx}, device_id_type=MESH
            )

    zeros = jnp.zeros((HALO, LANES), bf16)

    @pl.when(gy == 0)
    def _():
        for s in range(3):
            for t in range(4):
                buf[s, t, 0:HALO, :] = zeros

    @pl.when(gy == ny - 1)
    def _():
        for s in range(3):
            for t in range(4):
                buf[s, t, HALO + TILE : ROWS, :] = zeros

    @pl.when(gx == 0)
    def _():
        for s in range(3):
            buf[s, 0] = jnp.zeros((ROWS, LANES), bf16)

    @pl.when(gx == nx - 1)
    def _():
        for s in range(3):
            buf[s, 3] = jnp.zeros((ROWS, LANES), bf16)

    for d, (dy, dx) in enumerate(DIRECTIONS):

        @pl.when(jnp.logical_not(exists(-dy, -dx)))
        def _():
            plane[d] = jnp.zeros((8, 1, LANES), f32)

    if nz < 8:
        colb[...] = jnp.zeros((8, 1, LANES), f32)
        for d in range(8):
            plane[d] = jnp.zeros((8, 1, LANES), f32)

    tables[1].wait()
    tile_scr[...] = jnp.zeros((8, LANES), f32)
    tile_scr[0:4, 0:4] = mask_ref[0].astype(f32)
    mask_tile = tile_scr[...]
    mask_row = mask_tile[0:1]
    for y in range(1, 4):
        mask_row = mask_row + pltpu.roll(mask_tile[y : y + 1], 16 * y, 1)
    mask_row = pltpu.roll(mask_row, 8, 1) + pltpu.roll(mask_row, 72, 1)

    def relay(s):
        @pl.when(gz + s < nz)
        def _():
            for t in (1, 2):
                tile_copy(s, t).wait_recv()
                if s == 1:

                    @pl.when(gz > 0)
                    def _():
                        tile_copy(2, t).start()

                if t == 2:
                    rebuild(s)
                send_halos(s, True, (-1,) if t == 1 else (0, 1))

    first_row = lax.broadcasted_iota(jnp.int32, (8, 256), 0) == 0

    def spectra(s, slot, base, rows, top):
        area = pl.ds(base, rows)
        lane = lax.broadcasted_iota(jnp.int32, (rows, LANES), 1)
        left, tile_a, tile_b, right = (buf[s, t, area, :] for t in range(4))
        windows = (
            (left, tile_a),
            (jnp.where(lane < 108, tile_b, left), tile_a),
            (tile_b, jnp.where(lane < 20, right, tile_a)),
            (tile_b, right),
        )
        for j, (first, second) in enumerate(windows):
            y = jnp.dot(
                jnp.concatenate([first, second, first, second], 1),
                column_table[j],
                preferred_element_type=f32,
            )
            high = y.astype(bf16).astype(f32)
            low = y - high
            for t in range(2):
                cut = slice(128 * t, 128 * t + 128)
                y_parts[j][s, t, area, :] = high[:, cut]
                y_parts[j][s, 2 + t, area, :] = low[:, cut]
        for j in range(4):
            for k in range(2):
                start = 4 + 40 * (top + k)
                both = []
                for parity in range(2):
                    window = pl.ds(start + parity, 80, 2)
                    high, low = (
                        jnp.concatenate(
                            [y_parts[j][s, q + t, window, :].astype(bf16) for t in range(2)], 1
                        )
                        for q in (0, 2)
                    )
                    both.append(
                        jnp.dot(
                            row_tab[parity],
                            jnp.concatenate([high, high, low], 0),
                            preferred_element_type=f32,
                        )
                    )
                even, odd = both
                n = j * 2 + k
                spec[slot, n, 0:40] = even[0:40] + odd[0:40]
                spec[slot, n, 40:80] = even[0:40] - odd[0:40]
                total, rest = even[40:80] + odd[40:80], odd[40:80] - even[40:80]
                spec[slot, n, 80:88] = jnp.where(first_row, 0.0, total[0:8])
                spec[slot, n, 88:120] = total[8:40]
                spec[slot, n, 120:128] = jnp.where(first_row, 0.0, rest[0:8])
                spec[slot, n, 128:160] = rest[8:40]
                spec[slot, n, 160:168] = jnp.where(first_row, even[40:48], 0.0)
                spec[slot, n, 168:176] = jnp.where(first_row, odd[40:48], 0.0)

    shift_lane = lax.broadcasted_iota(jnp.int32, (8, LANES), 1)
    shift_low = (lax.rem(shift_lane + 80, PATCH) - 80).astype(f32)
    twice_sub = (2 * lax.broadcasted_iota(jnp.int32, (8, LANES), 0)).astype(f32)
    shift_high = (shift_lane - 32).astype(f32)

    def cross(own, n, cos_rows, sin_rows):
        cos_lanes, sin_lanes = slice(0, 128), slice(128, 256)
        ccs, css = spec[own, n, cos_rows, cos_lanes], spec[own, n, cos_rows, sin_lanes]
        scs, sss = spec[own, n, sin_rows, cos_lanes], spec[own, n, sin_rows, sin_lanes]
        cct, cst = spec[2, n, cos_rows, cos_lanes], spec[2, n, cos_rows, sin_lanes]
        sct, sst = spec[2, n, sin_rows, cos_lanes], spec[2, n, sin_rows, sin_lanes]
        q_cc = cct * ccs + sst * sss + cst * css + sct * scs
        q_ss = cct * sss + sst * ccs - cst * scs - sct * css
        q_cs = cst * ccs + sst * scs - cct * css - sct * sss
        q_sc = sct * ccs + sst * css - cct * scs - cst * sss
        return jnp.concatenate([q_cc, q_cs], 1), jnp.concatenate([q_sc, q_ss], 1)

    def transform_rows(own, n, target, m):
        cos_low, sin_low = cross(own, n, slice(0, 40), slice(80, 120))
        cos_high, sin_high = cross(own, n, slice(40, 80), slice(120, 160))
        cos_mid, sin_mid = cross(own, n, slice(160, 168), slice(168, 176))
        parts = (
            (cos_low + cos_high, sin_low - sin_high, cos_mid),
            (cos_low - cos_high, sin_low + sin_high, sin_mid),
        )
        for parity, (cos_part, sin_part, mid) in enumerate(parts):
            q = jnp.concatenate([cos_part, sin_part[0:8] + mid, sin_part[8:40]], 0)
            high = q.astype(bf16)
            low = (q - high.astype(f32)).astype(bf16)
            v = jnp.dot(
                left_tab[parity],
                jnp.concatenate([high, low, high], 0),
                preferred_element_type=f32,
            )
            high = v.astype(bf16)
            low = (v - high.astype(f32)).astype(bf16)
            place = slice(160 * m + 80 * parity, 160 * m + 80 * parity + 80)
            target[place, 0:256] = high
            target[place, 256:512] = low

    def moments(c, index, node):
        tail, total, weighted = None, None, []
        for parity in range(2):
            running = ramp = None
            for block in range(9, -1, -1):
                start = 80 * parity + 8 * block
                value = c[start : start + 8]
                square = value * value
                weight = square * square
                near, far = weight[:, 0:128], weight[:, 128:256]
                tail = far if tail is None else tail + far
                joined = near + far
                running = joined if running is None else running + joined
                if block > 0:
                    ramp = running if ramp is None else ramp + running
                if block == 5:
                    wrapped = running
            weighted.append(16.0 * ramp - float(PATCH) * wrapped)
            total = running if total is None else total + running
        red[0, index, node] = total
        red[1, index, node] = weighted[0] + weighted[1] + running + total * twice_sub
        red[2, index, node] = total * shift_low + tail * (shift_high - shift_low)

    def correlate(own, index, top):
        def columns(g):
            high, low = rows_buf[g][:, 0:256], rows_buf[g][:, 256:512]
            c = jnp.dot(
                jnp.concatenate([high, low, high], 1), right_tab[...], preferred_element_type=f32
            )
            for m in range(4):
                node = (2 * g + m // 2) * 4 + top + m % 2
                moments(c[160 * m : 160 * m + 160], index, node)

        for m in range(4):
            transform_rows(own, m, rows_buf[0], m)
        for m in range(4):
            transform_rows(own, 4 + m, rows_buf[1], m)
        columns(0)
        columns(1)

    for copy in tables[2:]:
        copy.wait()

    halves = (
        (pl.multiple_of(jnp.where(first_core, SECOND, 0), 16), FIRST, jnp.where(first_core, 2, 0)),
        (pl.multiple_of(jnp.where(first_core, 0, FIRST), 16), SECOND, jnp.where(first_core, 0, 2)),
    )

    def run(half, first, last):
        base, rows, top_patch = halves[half]

        def per_section(s, carry):
            if half == 0 and first == 0:

                @pl.when(s == 0)
                def _():
                    relay(1)

            @pl.when(gz + s < nz)
            def _():
                receive_halos(s, half == 0)

            spectra(s, jnp.where(s == 0, half, 2), base, rows, top_patch)
            if half == 0 and first == 0:

                @pl.when(s == 0)
                def _():
                    far_barrier()
                    send_halos(0, False)

                    @pl.when(gz + 1 < nz)
                    def _():
                        send_halos(1, False)

            if last > 0:

                @pl.when(s > 0)
                def _():
                    correlate(half, s - 1, top_patch)

            return carry

        lax.fori_loop(first, last + 1, per_section, 0)

    run(0, 0, 1)
    relay(2)

    @pl.when(gz + 2 < nz)
    def _():
        send_halos(2, False)

    place_lane = lax.broadcasted_iota(jnp.int32, (16, LANES), 1)
    place_node = lax.broadcasted_iota(jnp.int32, (16, LANES), 0)
    target = lax.rem(place_node, 4) * 16 + place_node // 4

    def flow_row(a):
        parts = [
            jnp.sum(jnp.sum(red[q, a], axis=1), axis=1, keepdims=True) for q in range(3)
        ]
        total = parts[0] + EPSILON
        flow_y = jnp.broadcast_to(parts[1] / total, (16, LANES))
        flow_x = jnp.broadcast_to(parts[2] / total, (16, LANES))
        placed = jnp.where(place_lane == target, flow_y, 0.0) + jnp.where(
            place_lane == target + 64, flow_x, 0.0
        )
        row = jnp.sum(placed, axis=0, keepdims=True)
        return jnp.where(gz + a + 1 < nz, row, 0.0)

    run(1, 0, 1)
    flow_rows = [flow_row(0)]
    early = flow_rows[0] + mask_row
    run(0, 2, 2)
    run(1, 2, 2)
    flow_rows.append(flow_row(1))

    colb[gz] = early + pltpu.roll(flow_rows[1], 4, 1)

    def write(ref, index, row, lane_base):
        for y in range(4):
            start = lane_base + 16 * y
            moved = pltpu.roll(row, (128 - start) % 128, 1) if start % 128 else row
            ref[index, 0, y : y + 1, :] = moved[:, 0:4]

    def col_copy(dz, slot):
        return pltpu.make_async_remote_copy(
            src_ref=colb.at[gz],
            dst_ref=colb.at[slot],
            send_sem=col_send.at[dz - 1],
            recv_sem=col_recv.at[dz - 1],
            device_id={"gz": lax.rem(gz + dz, nz)},
            device_id_type=MESH,
        )

    def plane_copy(d, dz):
        dy, dx = DIRECTIONS[d]
        return pltpu.make_async_remote_copy(
            src_ref=colb.at[gz],
            dst_ref=plane.at[d, gz],
            send_sem=plane_send.at[d],
            recv_sem=plane_recv.at[d],
            device_id={"gz": lax.rem(gz + dz, nz), "gy": gy + dy, "gx": gx + dx},
            device_id_type=MESH,
        )

    def plane_total(d):
        dy, dx = DIRECTIONS[d]
        return pltpu.make_async_remote_copy(
            src_ref=plane.at[d, pl.ds(0, nz)],
            dst_ref=plane.at[d, pl.ds(0, nz)],
            send_sem=plane_send.at[d],
            recv_sem=plane_recv.at[d],
            device_id={"gy": gy + dy, "gx": gx + dx},
            device_id_type=MESH,
        )

    pl.semaphore_wait(wide_sem, nz - 1)
    order = sorted(range(8), key=lambda d: -abs(DIRECTIONS[d][0]) - abs(DIRECTIONS[d][1]))
    for d in order:

        @pl.when(exists(*DIRECTIONS[d]))
        def _():
            for dz in range(nz):
                plane_copy(d, dz).start()

    for dz in range(1, nz):
        col_copy(dz, gz).start()

    for a in range(2):
        for comp in range(2):
            write(flow_ref, 2 * a + comp, flow_rows[a], 64 * comp)

    for dz in range(1, nz):
        col_copy(dz, lax.rem(gz + nz - dz, nz)).wait_recv()

    for d, (dy, dx) in enumerate(DIRECTIONS):

        @pl.when(exists(-dy, -dx))
        def _():
            plane_total(d).wait_recv()

    def block(by, bx):
        if (by, bx) == (0, 0):
            return colb[:, 0, :]
        return plane[DIRECTIONS.index((-by, -bx)), :, 0, :]

    lanes8 = lax.broadcasted_iota(jnp.int32, (8, LANES), 1)
    depth = lax.broadcasted_iota(jnp.int32, (8, LANES), 0)
    x_in = lax.rem(lanes8, 16)
    y_in = lax.rem(lanes8 // 16, 4)
    flow_one, flow_two, masks = [], [], []
    for by in (-1, 0, 1):
        joined = None
        for bx in (-1, 0, 1):
            value = block(by, bx)
            pieces = []
            for q in range(3):
                piece = jnp.where(x_in // 4 == q, value, 0.0)
                moved = (4 * (bx + 1 - q)) % 128
                pieces.append(pltpu.roll(piece, moved, 1) if moved else piece)
            joined = pieces if joined is None else [x + y for x, y in zip(joined, pieces)]
        flow_one.append(joined[0])
        flow_two.append(joined[1])
        masks.append(joined[2])

    not_first_x = (gx > 0).astype(jnp.int32)
    not_last_x = (gx < nx - 1).astype(jnp.int32)
    inside_x = jnp.where(
        x_in < 4, not_first_x, jnp.where(x_in < 8, 1, jnp.where(x_in < 12, not_last_x, 0))
    ).astype(f32)
    row_valid = [(gy > 0).astype(jnp.int32), 1, (gy < ny - 1).astype(jnp.int32)]
    inside = [inside_x * jnp.asarray(v, jnp.int32).astype(f32) for v in row_valid]

    def up(value, steps):
        return pltpu.roll(value, 8 - steps, 0)

    def down(value, steps):
        return pltpu.roll(value, steps, 0)

    steady, weights = [], []
    for b in range(3):
        w1 = jnp.where(depth + 1 < nz, masks[b] * up(masks[b], 1), 0.0)
        w2 = jnp.where(depth + 2 < nz, masks[b] * up(masks[b], 2), 0.0)
        l1, l2 = down(w1, 1), down(w2, 2)
        pull = (
            l1 * down(flow_one[b], 1)
            + l2 * down(flow_two[b], 2)
            - w1 * flow_one[b]
            - w2 * flow_two[b]
        )
        steady.append(pull)
        weights.append((w1, w2, l1, l2, w1 + w2 + l1 + l2))

    u = [STEP_SIZE * steady[b] * inside[b] for b in range(3)]
    for _ in range(RELAX - 1):
        fresh = []
        for b in range(3):
            value = u[b]
            below = pltpu.roll(value, 128 - 16, 1)
            above = pltpu.roll(value, 16, 1)
            edge_below = pltpu.roll(u[b + 1], 48, 1) if b < 2 else jnp.zeros_like(value)
            edge_above = pltpu.roll(u[b - 1], 128 - 48, 1) if b > 0 else jnp.zeros_like(value)
            below = jnp.where(y_in == 3, edge_below, below)
            above = jnp.where(y_in == 0, edge_above, above)
            laplace = (
                below + above + pltpu.roll(value, 1, 1) + pltpu.roll(value, 127, 1) - 4.0 * value
            )
            w1, w2, l1, l2, total = weights[b]
            forces = STIFFNESS * laplace + steady[b] - total * value
            forces = forces + w1 * up(value, 1) + w2 * up(value, 2)
            forces = forces + l1 * down(value, 1) + l2 * down(value, 2)
            fresh.append((value + STEP_SIZE * forces) * inside[b])
        u = fresh

    row = jnp.sum(jnp.where(depth == gz, u[1], 0.0), axis=0, keepdims=True)
    for comp in range(2):
        write(offset_ref, comp, row, 64 * comp + 4)

    for s in range(3):
        for d, (dy, dx) in enumerate(DIRECTIONS):

            @pl.when(exists(dy, dx) & (gz + s < nz))
            def _():
                halo_copy(s, d).wait_send()

    for s in (1, 2):

        @pl.when((gz > 0) & (gz + s - 1 < nz))
        def _():
            tile_copy(s, 1).wait_send()
            tile_copy(s, 2).wait_send()

    for dz in range(1, nz):
        col_copy(dz, gz).wait_send()
    for d, (dy, dx) in enumerate(DIRECTIONS):

        @pl.when(exists(dy, dx))
        def _():
            plane_total(d).wait_send()


def solution(mesh):
    sizes = tuple(mesh.shape[name] for name in ("gz", "gy", "gx"))
    f32, bf16 = jnp.float32, jnp.bfloat16
    column_table = column_tables()
    row_tab, left_tab = parity_tables()
    right_tab = right_inverse()
    constants = (column_table, row_tab, left_tab, right_tab)

    def body(images, tissue_mask):
        vmem = pl.BlockSpec(memory_space=pltpu.VMEM)
        anywhere = pl.BlockSpec(memory_space=pltpu.HBM)
        dma = pltpu.SemaphoreType.DMA
        return pl.pallas_call(
            functools.partial(kernel, sizes),
            out_shape=(
                jax.ShapeDtypeStruct((4, 1, 4, 4), f32),
                jax.ShapeDtypeStruct((2, 1, 4, 4), f32),
            ),
            in_specs=[anywhere] * 6,
            out_specs=(vmem, vmem),
            scratch_shapes=[
                pltpu.VMEM((3, 4, ROWS, LANES), bf16),
                pltpu.VMEM((3, STRIP, LANES), bf16),
                pltpu.VMEM(column_table.shape, bf16),
                pltpu.VMEM(row_tab.shape, bf16),
                pltpu.VMEM(left_tab.shape, bf16),
                pltpu.VMEM(right_tab.shape, bf16),
                pltpu.VMEM((3, 4, ROWS, LANES), f32),
                pltpu.VMEM((3, 4, ROWS, LANES), f32),
                pltpu.VMEM((3, 4, ROWS, LANES), f32),
                pltpu.VMEM((3, 4, ROWS, LANES), f32),
                pltpu.VMEM((4 * PATCH, 512), bf16),
                pltpu.VMEM((4 * PATCH, 512), bf16),
                pltpu.VMEM((3, 8, 176, 256), f32),
                pltpu.VMEM((3, 2, 16, 8, LANES), f32),
                pltpu.VMEM((8, LANES), f32),
                pltpu.VMEM((8, 1, LANES), f32),
                pltpu.VMEM((8, 8, 1, LANES), f32),
                pltpu.VMEM((1, TILE, TILE), bf16),
                pltpu.VMEM((1, 4, 4), jnp.int32),
                dma((6,)),
                dma((3, 8)),
                dma((3, 8)),
                dma((2, 2)),
                dma((2, 2)),
                dma((7,)),
                dma((7,)),
                dma((8,)),
                dma((8,)),
                pltpu.SemaphoreType.REGULAR,
                pltpu.SemaphoreType.REGULAR,
                pltpu.SemaphoreType.REGULAR,
            ],
            compiler_params=pltpu.CompilerParams(
                collective_id=0, has_side_effects=True, vmem_limit_bytes=32 * 1024 * 1024
            ),
        )(*[pltpu.with_memory_space_constraint(x, pltpu.HBM) for x in (images, tissue_mask, *[jnp.asarray(x) for x in constants])])

    return jax.shard_map(
        body,
        mesh=mesh,
        in_specs=(P("gz", "gy", "gx"), P("gz", "gy", "gx")),
        out_specs=(P(None, "gz", "gy", "gx"), P(None, "gz", "gy", "gx")),
        check_vma=False,
    )
```

```python
import functools
import math

import jax
import jax.numpy as jnp
import numpy as np
from jax import lax
from jax.experimental import pallas as pl
from jax.experimental.pallas import tpu as pltpu
from jax.sharding import PartitionSpec as P

PATCH = 160
STRIDE = 40
RELAX = 4
EPSILON = 1e-06
STIFFNESS = 0.5
STEP_SIZE = 0.2

TILE = 160
HALO = 64
ROWS = TILE + 2 * HALO
LANES = 128
FIRST = 208
SECOND = ROWS - FIRST
STRIP = 48
MESH = pl.DeviceIdType.MESH
DIRECTIONS = [(dy, dx) for dy in (-1, 0, 1) for dx in (-1, 0, 1) if (dy, dx) != (0, 0)]


def split_np(table):
    bf16 = jnp.bfloat16
    high = np.asarray(table, np.float32).astype(bf16)
    low = (np.asarray(table, np.float64) - high.astype(np.float64)).astype(np.float32).astype(bf16)
    return high, low


def cosine(product):
    return np.cos(2.0 * np.pi * (product % PATCH) / PATCH)


def sine(product):
    phase = product % (PATCH // 2)
    return np.where(phase == 0, 0.0, np.sin(2.0 * np.pi * (product % PATCH) / PATCH))


def column_tables():
    freq = np.arange(81)
    out = []
    for j in range(4):
        lane = np.arange(256)
        if j == 0:
            column = lane - 128
            good = lane >= 0
        elif j == 1:
            column = np.where(lane < 108, 32 + lane, lane - 128)
            good = lane >= 96
        elif j == 2:
            column = np.where(lane < 128, 32 + lane, np.where(lane < 148, 32 + lane, lane - 128))
            good = lane < 160
        else:
            column = 32 + lane
            good = lane >= 0
        m = column - (40 * j - 60)
        good = good & (m >= 0) & (m < PATCH)
        product = m[:, None] * freq[None, :]
        table = np.zeros((256, 256))
        table[:, 0:81] = cosine(product) * good[:, None]
        table[:, 128:209] = sine(product) * good[:, None]
        high, low = split_np(table)
        out.append(np.concatenate([high, low], 0))
    return np.stack(out)


def parity_tables():
    low = np.arange(40)
    forward, inverse = [], []
    scale = np.where(low == 0, 1.0, 2.0) / PATCH
    for parity in range(2):
        n = 2 * np.arange(80) + parity
        product = low[:, None] * n[None]
        cos_part, sin_part = cosine(product), sine(product)
        sin_part[0] = cosine(40 * n) if parity == 0 else sine(40 * n)
        sin_scale = np.where(low == 0, 2.0, 2.0) / PATCH
        table = np.concatenate([cos_part, sin_part], 0)
        high, part = split_np(table)
        forward.append(np.concatenate([high, part, high], 1))
        table = np.concatenate([cos_part * scale[:, None], sin_part * sin_scale[:, None]], 0).T
        high, part = split_np(table)
        inverse.append(np.concatenate([high, high, part], 1))
    return np.stack(forward), np.stack(inverse)


def right_inverse():
    freq = np.arange(81)
    scale = np.where((freq == 0) | (freq == 80), 1.0, 2.0) / PATCH
    product = freq[:, None] * np.arange(PATCH)[None]
    right = np.zeros((256, 256))
    right[0:81, 0:PATCH] = cosine(product) * scale[:, None]
    right[128:209, 0:PATCH] = sine(product) * scale[:, None]
    high, low = split_np(right)
    return np.concatenate([high, high, low], 0)


def kernel(
    sizes,
    image_hbm,
    mask_hbm,
    column_hbm,
    row_hbm,
    left_hbm,
    right_hbm,
    flow_ref,
    offset_ref,
    buf,
    strips,
    column_table,
    row_tab,
    left_tab,
    right_tab,
    y_a,
    y_b,
    y_c,
    y_d,
    rows_a,
    rows_b,
    spec,
    red,
    tile_scr,
    colb,
    plane,
    image_ref,
    mask_ref,
    table_sem,
    halo_send,
    halo_recv,
    tile_send,
    tile_recv,
    col_send,
    col_recv,
    plane_send,
    plane_recv,
    near_sem,
    far_sem,
    wide_sem,
):
    nz, ny, nx = sizes
    gz, gy, gx = lax.axis_index("gz"), lax.axis_index("gy"), lax.axis_index("gx")
    f32, bf16 = jnp.float32, jnp.bfloat16
    y_parts, rows_buf = (y_a, y_b, y_c, y_d), (rows_a, rows_b)

    tables = [
        pltpu.make_async_copy(source, target, table_sem.at[k])
        for k, (source, target) in enumerate(
            (
                (image_hbm, image_ref),
                (mask_hbm, mask_ref),
                (column_hbm, column_table),
                (row_hbm, row_tab),
                (left_hbm, left_tab),
                (right_hbm, right_tab),
            )
        )
    ]
    for copy in tables[:2]:
        copy.start()

    def exists(dy, dx):
        ok = None
        for step, position, count in ((dy, gy, ny), (dx, gx, nx)):
            term = None
            if step < 0:
                term = position > 0
            elif step > 0:
                term = position < count - 1
            if term is not None:
                ok = term if ok is None else ok & term
        return ok

    core = lax.rem(gy, 2)
    first_core, second_core = core == 0, core == 1
    base_gy = gy - core
    layer = gy // 2
    layers = ny // 2

    def count(*conditions):
        return sum(jnp.asarray(c).astype(jnp.int32) for c in conditions)

    barrier = pltpu.get_barrier_semaphore()

    @pl.when(second_core)
    def _():
        pl.semaphore_signal(barrier, inc=1, device_id={"gy": base_gy}, device_id_type=MESH)

    for dx in (-1, 1):

        @pl.when(exists(0, dx))
        def _():
            pl.semaphore_signal(
                barrier, inc=1, device_id={"gy": base_gy, "gx": gx + dx}, device_id_type=MESH
            )

    for step, present in ((-1, gz > 0), (1, gz < nz - 1)):

        @pl.when(present)
        def _():
            pl.semaphore_signal(
                barrier, inc=1, device_id={"gz": gz + step, "gy": base_gy}, device_id_type=MESH
            )

    tables[0].wait()
    image = image_ref[0]
    buf[0, 1, HALO : HALO + TILE, :] = image[:, 0:128]
    buf[0, 2, HALO : HALO + TILE, :] = image[:, 32:160]
    strip_lane = lax.broadcasted_iota(jnp.int32, (STRIP, LANES), 1)
    last_columns = buf[0, 2, HALO : HALO + TILE, :].astype(f32)
    strip = jnp.zeros((STRIP, LANES), f32)
    for q in range(4):
        count_q = min(STRIP, TILE - STRIP * q)
        piece = pltpu.roll(last_columns[STRIP * q : STRIP * q + count_q], (32 + 32 * q) % 128, 1)
        if count_q < STRIP:
            piece = jnp.concatenate([piece, jnp.zeros((STRIP - count_q, LANES), f32)], 0)
        strip = jnp.where(strip_lane // 32 == q, piece, strip)
    strips[0] = strip.astype(bf16)
    beside = count(gx > 0, gx < nx - 1)
    adjacent = count(gz > 0, gz < nz - 1)

    @pl.when(first_core)
    def _():
        pl.semaphore_wait(barrier, 1 + 2 * adjacent + 2 * beside)
        pl.semaphore_signal(near_sem, inc=1, device_id={"gy": gy + 1}, device_id_type=MESH)

    @pl.when(second_core)
    def _():
        pl.semaphore_wait(near_sem, 1)

    def far_barrier():
        @pl.when(second_core)
        def _():
            pl.semaphore_wait(
                barrier,
                (1 + beside) * count(layer > 0, layer < layers - 1)
                + 2 * (nz - 1 - adjacent),
            )
            pl.semaphore_signal(far_sem, inc=1, device_id={"gy": gy - 1}, device_id_type=MESH)

        @pl.when(first_core)
        def _():
            pl.semaphore_wait(far_sem, 1)

        for dz in range(1, nz):
            pl.semaphore_signal(
                wide_sem, inc=1, device_id={"gz": lax.rem(gz + dz, nz)}, device_id_type=MESH
            )

    top, middle, bottom = (0, HALO), (HALO, TILE), (HALO + TILE, HALO)

    def halo_copy(s, d):
        dy, dx = DIRECTIONS[d]
        source_rows = {-1: (HALO, HALO), 0: middle, 1: (TILE, HALO)}[dy]
        target_rows = {-1: bottom, 0: middle, 1: top}[dy]
        source_tiles = {-1: (1, 1), 0: (1, 2), 1: (2, 1)}[dx]
        target_tiles = {-1: (3, 1), 0: (1, 2), 1: (0, 1)}[dx]
        return pltpu.make_async_remote_copy(
            src_ref=buf.at[s, pl.ds(*source_tiles), pl.ds(*source_rows)],
            dst_ref=buf.at[s, pl.ds(*target_tiles), pl.ds(*target_rows)],
            send_sem=halo_send.at[s, d],
            recv_sem=halo_recv.at[s, d],
            device_id={"gy": gy + dy, "gx": gx + dx},
            device_id_type=MESH,
        )

    def tile_copy(s, t):
        if t == 1:
            source, target = buf.at[s - 1, 1, pl.ds(*middle)], buf.at[s, 1, pl.ds(*middle)]
        else:
            source, target = strips.at[s - 1], strips.at[s]
        return pltpu.make_async_remote_copy(
            src_ref=source,
            dst_ref=target,
            send_sem=tile_send.at[s - 1, t - 1],
            recv_sem=tile_recv.at[s - 1, t - 1],
            device_id={"gz": gz - 1},
            device_id_type=MESH,
        )

    def rebuild(s):
        moved = pltpu.roll(buf[s, 1, HALO : HALO + TILE, :].astype(f32), 96, 1)
        packed = strips[s].astype(f32)
        for q in range(4):
            count_q = min(STRIP, TILE - STRIP * q)
            rows = slice(STRIP * q, STRIP * q + count_q)
            piece = pltpu.roll(packed, (96 - 32 * q) % 128, 1) if q < 3 else packed
            lane_q = lax.broadcasted_iota(jnp.int32, (count_q, LANES), 1)
            buf[s, 2, HALO + STRIP * q : HALO + STRIP * q + count_q, :] = jnp.where(
                lane_q < 96, moved[rows], piece[0:count_q]
            ).astype(bf16)

    def is_near(dy):
        if dy == 0:
            return True
        return first_core if dy > 0 else second_core

    def send_halos(s, near, steps=(-1, 0, 1)):
        for d, (dy, dx) in enumerate(DIRECTIONS):
            if (dy == 0 and not near) or dx not in steps:
                continue
            side = is_near(dy) if near else jnp.logical_not(is_near(dy))

            @pl.when(exists(dy, dx) & side)
            def _():
                halo_copy(s, d).start()

    def receive_halos(s, near):
        for d, (dy, dx) in enumerate(DIRECTIONS):
            if dy == 0 and not near:
                continue
            side = is_near(-dy) if near else jnp.logical_not(is_near(-dy))

            @pl.when(exists(-dy, -dx) & side)
            def _():
                halo_copy(s, d).wait_recv()

    @pl.when(gz > 0)
    def _():
        tile_copy(1, 1).start()
        tile_copy(1, 2).start()

    send_halos(0, True)
    for copy in tables[2:]:
        copy.start()

    for dz in range(1, nz):
        other = lax.rem(gz + dz, nz)

        @pl.when((other != gz - 1) & (other != gz + 1))
        def _():
            pl.semaphore_signal(
                barrier,
                inc=1,
                device_id={"gz": other, "gy": base_gy + 1},
                device_id_type=MESH,
            )

    for dx in (-1, 0, 1):
        inside_x = True if dx == 0 else exists(0, dx)

        @pl.when(second_core & (layer < layers - 1) & inside_x)
        def _():
            pl.semaphore_signal(
                barrier, inc=1, device_id={"gy": gy + 2, "gx": gx + dx}, device_id_type=MESH
            )

        @pl.when(first_core & (layer > 0) & inside_x)
        def _():
            pl.semaphore_signal(
                barrier, inc=1, device_id={"gy": gy - 1, "gx": gx + dx}, device_id_type=MESH
            )

    zeros = jnp.zeros((HALO, LANES), bf16)

    @pl.when(gy == 0)
    def _():
        for s in range(3):
            for t in range(4):
                buf[s, t, 0:HALO, :] = zeros

    @pl.when(gy == ny - 1)
    def _():
        for s in range(3):
            for t in range(4):
                buf[s, t, HALO + TILE : ROWS, :] = zeros

    @pl.when(gx == 0)
    def _():
        for s in range(3):
            buf[s, 0] = jnp.zeros((ROWS, LANES), bf16)

    @pl.when(gx == nx - 1)
    def _():
        for s in range(3):
            buf[s, 3] = jnp.zeros((ROWS, LANES), bf16)

    for d, (dy, dx) in enumerate(DIRECTIONS):

        @pl.when(jnp.logical_not(exists(-dy, -dx)))
        def _():
            plane[d] = jnp.zeros((8, 1, LANES), f32)

    if nz < 8:
        colb[...] = jnp.zeros((8, 1, LANES), f32)
        for d in range(8):
            plane[d] = jnp.zeros((8, 1, LANES), f32)

    tables[1].wait()
    tile_scr[...] = jnp.zeros((8, LANES), f32)
    tile_scr[0:4, 0:4] = mask_ref[0].astype(f32)
    mask_tile = tile_scr[...]
    mask_row = mask_tile[0:1]
    for y in range(1, 4):
        mask_row = mask_row + pltpu.roll(mask_tile[y : y + 1], 16 * y, 1)
    mask_row = pltpu.roll(mask_row, 8, 1) + pltpu.roll(mask_row, 72, 1)

    def relay(s):
        @pl.when(gz + s < nz)
        def _():
            for t in (1, 2):
                tile_copy(s, t).wait_recv()
                if s == 1:

                    @pl.when(gz > 0)
                    def _():
                        tile_copy(2, t).start()

                if t == 2:
                    rebuild(s)
                send_halos(s, True, (-1,) if t == 1 else (0, 1))

    first_row = lax.broadcasted_iota(jnp.int32, (8, 256), 0) == 0

    def spectra(s, slot, base, rows, top):
        area = pl.ds(base, rows)
        lane = lax.broadcasted_iota(jnp.int32, (rows, LANES), 1)
        left, tile_a, tile_b, right = (buf[s, t, area, :] for t in range(4))
        windows = (
            (left, tile_a),
            (jnp.where(lane < 108, tile_b, left), tile_a),
            (tile_b, jnp.where(lane < 20, right, tile_a)),
            (tile_b, right),
        )
        for j, (first, second) in enumerate(windows):
            y = jnp.dot(
                jnp.concatenate([first, second, first, second], 1),
                column_table[j],
                preferred_element_type=f32,
            )
            high = y.astype(bf16).astype(f32)
            low = y - high
            for t in range(2):
                cut = slice(128 * t, 128 * t + 128)
                y_parts[j][s, t, area, :] = high[:, cut]
                y_parts[j][s, 2 + t, area, :] = low[:, cut]
        for j in range(4):
            for k in range(2):
                start = 4 + 40 * (top + k)
                both = []
                for parity in range(2):
                    window = pl.ds(start + parity, 80, 2)
                    high, low = (
                        jnp.concatenate(
                            [y_parts[j][s, q + t, window, :].astype(bf16) for t in range(2)], 1
                        )
                        for q in (0, 2)
                    )
                    both.append(
                        jnp.dot(
                            row_tab[parity],
                            jnp.concatenate([high, high, low], 0),
                            preferred_element_type=f32,
                        )
                    )
                even, odd = both
                n = j * 2 + k
                spec[slot, n, 0:40] = even[0:40] + odd[0:40]
                spec[slot, n, 40:80] = even[0:40] - odd[0:40]
                total, rest = even[40:80] + odd[40:80], odd[40:80] - even[40:80]
                spec[slot, n, 80:88] = jnp.where(first_row, 0.0, total[0:8])
                spec[slot, n, 88:120] = total[8:40]
                spec[slot, n, 120:128] = jnp.where(first_row, 0.0, rest[0:8])
                spec[slot, n, 128:160] = rest[8:40]
                spec[slot, n, 160:168] = jnp.where(first_row, even[40:48], 0.0)
                spec[slot, n, 168:176] = jnp.where(first_row, odd[40:48], 0.0)

    shift_lane = lax.broadcasted_iota(jnp.int32, (8, LANES), 1)
    shift_low = (lax.rem(shift_lane + 80, PATCH) - 80).astype(f32)
    twice_sub = (2 * lax.broadcasted_iota(jnp.int32, (8, LANES), 0)).astype(f32)
    shift_high = (shift_lane - 32).astype(f32)

    def cross(own, n, cos_rows, sin_rows):
        cos_lanes, sin_lanes = slice(0, 128), slice(128, 256)
        ccs, css = spec[own, n, cos_rows, cos_lanes], spec[own, n, cos_rows, sin_lanes]
        scs, sss = spec[own, n, sin_rows, cos_lanes], spec[own, n, sin_rows, sin_lanes]
        cct, cst = spec[2, n, cos_rows, cos_lanes], spec[2, n, cos_rows, sin_lanes]
        sct, sst = spec[2, n, sin_rows, cos_lanes], spec[2, n, sin_rows, sin_lanes]
        q_cc = cct * ccs + sst * sss + cst * css + sct * scs
        q_ss = cct * sss + sst * ccs - cst * scs - sct * css
        q_cs = cst * ccs + sst * scs - cct * css - sct * sss
        q_sc = sct * ccs + sst * css - cct * scs - cst * sss
        return jnp.concatenate([q_cc, q_cs], 1), jnp.concatenate([q_sc, q_ss], 1)

    def transform_rows(own, n, target, m):
        cos_low, sin_low = cross(own, n, slice(0, 40), slice(80, 120))
        cos_high, sin_high = cross(own, n, slice(40, 80), slice(120, 160))
        cos_mid, sin_mid = cross(own, n, slice(160, 168), slice(168, 176))
        parts = (
            (cos_low + cos_high, sin_low - sin_high, cos_mid),
            (cos_low - cos_high, sin_low + sin_high, sin_mid),
        )
        for parity, (cos_part, sin_part, mid) in enumerate(parts):
            q = jnp.concatenate([cos_part, sin_part[0:8] + mid, sin_part[8:40]], 0)
            high = q.astype(bf16)
            low = (q - high.astype(f32)).astype(bf16)
            v = jnp.dot(
                left_tab[parity],
                jnp.concatenate([high, low, high], 0),
                preferred_element_type=f32,
            )
            high = v.astype(bf16)
            low = (v - high.astype(f32)).astype(bf16)
            place = slice(160 * m + 80 * parity, 160 * m + 80 * parity + 80)
            target[place, 0:256] = high
            target[place, 256:512] = low

    def moments(c, index, node):
        tail, total, weighted = None, None, []
        for parity in range(2):
            running = ramp = None
            for block in range(9, -1, -1):
                start = 80 * parity + 8 * block
                value = c[start : start + 8]
                square = value * value
                weight = square * square
                near, far = weight[:, 0:128], weight[:, 128:256]
                tail = far if tail is None else tail + far
                joined = near + far
                running = joined if running is None else running + joined
                if block > 0:
                    ramp = running if ramp is None else ramp + running
                if block == 5:
                    wrapped = running
            weighted.append(16.0 * ramp - float(PATCH) * wrapped)
            total = running if total is None else total + running
        red[0, index, node] = total
        red[1, index, node] = weighted[0] + weighted[1] + running + total * twice_sub
        red[2, index, node] = total * shift_low + tail * (shift_high - shift_low)

    def correlate(own, index, top):
        def columns(g):
            high, low = rows_buf[g][:, 0:256], rows_buf[g][:, 256:512]
            c = jnp.dot(
                jnp.concatenate([high, low, high], 1), right_tab[...], preferred_element_type=f32
            )
            for m in range(4):
                node = (2 * g + m // 2) * 4 + top + m % 2
                moments(c[160 * m : 160 * m + 160], index, node)

        for m in range(4):
            transform_rows(own, m, rows_buf[0], m)
        for m in range(4):
            transform_rows(own, 4 + m, rows_buf[1], m)
        columns(0)
        columns(1)

    for copy in tables[2:]:
        copy.wait()

    halves = (
        (pl.multiple_of(jnp.where(first_core, SECOND, 0), 16), FIRST, jnp.where(first_core, 2, 0)),
        (pl.multiple_of(jnp.where(first_core, 0, FIRST), 16), SECOND, jnp.where(first_core, 0, 2)),
    )

    def run(half, first, last):
        base, rows, top_patch = halves[half]

        def per_section(s, carry):
            if half == 0 and first == 0:

                @pl.when(s == 0)
                def _():
                    relay(1)

            @pl.when(gz + s < nz)
            def _():
                receive_halos(s, half == 0)

            spectra(s, jnp.where(s == 0, half, 2), base, rows, top_patch)
            if half == 0 and first == 0:

                @pl.when(s == 0)
                def _():
                    far_barrier()
                    send_halos(0, False)

                    @pl.when(gz + 1 < nz)
                    def _():
                        send_halos(1, False)

            if last > 0:

                @pl.when(s > 0)
                def _():
                    correlate(half, s - 1, top_patch)

            return carry

        lax.fori_loop(first, last + 1, per_section, 0)

    run(0, 0, 1)
    relay(2)

    @pl.when(gz + 2 < nz)
    def _():
        send_halos(2, False)

    place_lane = lax.broadcasted_iota(jnp.int32, (16, LANES), 1)
    place_node = lax.broadcasted_iota(jnp.int32, (16, LANES), 0)
    target = lax.rem(place_node, 4) * 16 + place_node // 4

    def flow_row(a):
        parts = [
            jnp.sum(jnp.sum(red[q, a], axis=1), axis=1, keepdims=True) for q in range(3)
        ]
        total = parts[0] + EPSILON
        flow_y = jnp.broadcast_to(parts[1] / total, (16, LANES))
        flow_x = jnp.broadcast_to(parts[2] / total, (16, LANES))
        placed = jnp.where(place_lane == target, flow_y, 0.0) + jnp.where(
            place_lane == target + 64, flow_x, 0.0
        )
        row = jnp.sum(placed, axis=0, keepdims=True)
        return jnp.where(gz + a + 1 < nz, row, 0.0)

    run(1, 0, 1)
    flow_rows = [flow_row(0)]
    early = flow_rows[0] + mask_row
    run(0, 2, 2)
    run(1, 2, 2)
    flow_rows.append(flow_row(1))

    colb[gz] = early + pltpu.roll(flow_rows[1], 4, 1)

    def write(ref, index, row, lane_base):
        for y in range(4):
            start = lane_base + 16 * y
            moved = pltpu.roll(row, (128 - start) % 128, 1) if start % 128 else row
            ref[index, 0, y : y + 1, :] = moved[:, 0:4]

    def col_copy(dz, slot):
        return pltpu.make_async_remote_copy(
            src_ref=colb.at[gz],
            dst_ref=colb.at[slot],
            send_sem=col_send.at[dz - 1],
            recv_sem=col_recv.at[dz - 1],
            device_id={"gz": lax.rem(gz + dz, nz)},
            device_id_type=MESH,
        )

    def plane_copy(d, dz):
        dy, dx = DIRECTIONS[d]
        return pltpu.make_async_remote_copy(
            src_ref=colb.at[gz],
            dst_ref=plane.at[d, gz],
            send_sem=plane_send.at[d],
            recv_sem=plane_recv.at[d],
            device_id={"gz": lax.rem(gz + dz, nz), "gy": gy + dy, "gx": gx + dx},
            device_id_type=MESH,
        )

    def plane_total(d):
        dy, dx = DIRECTIONS[d]
        return pltpu.make_async_remote_copy(
            src_ref=plane.at[d, pl.ds(0, nz)],
            dst_ref=plane.at[d, pl.ds(0, nz)],
            send_sem=plane_send.at[d],
            recv_sem=plane_recv.at[d],
            device_id={"gy": gy + dy, "gx": gx + dx},
            device_id_type=MESH,
        )

    pl.semaphore_wait(wide_sem, nz - 1)
    order = sorted(range(8), key=lambda d: -abs(DIRECTIONS[d][0]) - abs(DIRECTIONS[d][1]))
    for d in order:

        @pl.when(exists(*DIRECTIONS[d]))
        def _():
            for dz in range(nz):
                plane_copy(d, dz).start()

    for dz in range(1, nz):
        col_copy(dz, gz).start()

    for a in range(2):
        for comp in range(2):
            write(flow_ref, 2 * a + comp, flow_rows[a], 64 * comp)

    for dz in range(1, nz):
        col_copy(dz, lax.rem(gz + nz - dz, nz)).wait_recv()

    for d, (dy, dx) in enumerate(DIRECTIONS):

        @pl.when(exists(-dy, -dx))
        def _():
            plane_total(d).wait_recv()

    def block(by, bx):
        if (by, bx) == (0, 0):
            return colb[:, 0, :]
        return plane[DIRECTIONS.index((-by, -bx)), :, 0, :]

    lanes8 = lax.broadcasted_iota(jnp.int32, (8, LANES), 1)
    depth = lax.broadcasted_iota(jnp.int32, (8, LANES), 0)
    x_in = lax.rem(lanes8, 16)
    y_in = lax.rem(lanes8 // 16, 4)
    flow_one, flow_two, masks = [], [], []
    for by in (-1, 0, 1):
        joined = None
        for bx in (-1, 0, 1):
            value = block(by, bx)
            pieces = []
            for q in range(3):
                piece = jnp.where(x_in // 4 == q, value, 0.0)
                moved = (4 * (bx + 1 - q)) % 128
                pieces.append(pltpu.roll(piece, moved, 1) if moved else piece)
            joined = pieces if joined is None else [x + y for x, y in zip(joined, pieces)]
        flow_one.append(joined[0])
        flow_two.append(joined[1])
        masks.append(joined[2])

    not_first_x = (gx > 0).astype(jnp.int32)
    not_last_x = (gx < nx - 1).astype(jnp.int32)
    inside_x = jnp.where(
        x_in < 4, not_first_x, jnp.where(x_in < 8, 1, jnp.where(x_in < 12, not_last_x, 0))
    ).astype(f32)
    row_valid = [(gy > 0).astype(jnp.int32), 1, (gy < ny - 1).astype(jnp.int32)]
    inside = [inside_x * jnp.asarray(v, jnp.int32).astype(f32) for v in row_valid]

    def up(value, steps):
        return pltpu.roll(value, 8 - steps, 0)

    def down(value, steps):
        return pltpu.roll(value, steps, 0)

    steady, weights = [], []
    for b in range(3):
        w1 = jnp.where(depth + 1 < nz, masks[b] * up(masks[b], 1), 0.0)
        w2 = jnp.where(depth + 2 < nz, masks[b] * up(masks[b], 2), 0.0)
        l1, l2 = down(w1, 1), down(w2, 2)
        pull = (
            l1 * down(flow_one[b], 1)
            + l2 * down(flow_two[b], 2)
            - w1 * flow_one[b]
            - w2 * flow_two[b]
        )
        steady.append(pull)
        weights.append((w1, w2, l1, l2, w1 + w2 + l1 + l2))

    u = [STEP_SIZE * steady[b] * inside[b] for b in range(3)]
    for _ in range(RELAX - 1):
        fresh = []
        for b in range(3):
            value = u[b]
            below = pltpu.roll(value, 128 - 16, 1)
            above = pltpu.roll(value, 16, 1)
            edge_below = pltpu.roll(u[b + 1], 48, 1) if b < 2 else jnp.zeros_like(value)
            edge_above = pltpu.roll(u[b - 1], 128 - 48, 1) if b > 0 else jnp.zeros_like(value)
            below = jnp.where(y_in == 3, edge_below, below)
            above = jnp.where(y_in == 0, edge_above, above)
            laplace = (
                below + above + pltpu.roll(value, 1, 1) + pltpu.roll(value, 127, 1) - 4.0 * value
            )
            w1, w2, l1, l2, total = weights[b]
            forces = STIFFNESS * laplace + steady[b] - total * value
            forces = forces + w1 * up(value, 1) + w2 * up(value, 2)
            forces = forces + l1 * down(value, 1) + l2 * down(value, 2)
            fresh.append((value + STEP_SIZE * forces) * inside[b])
        u = fresh

    row = jnp.sum(jnp.where(depth == gz, u[1], 0.0), axis=0, keepdims=True)
    for comp in range(2):
        write(offset_ref, comp, row, 64 * comp + 4)

    for s in range(3):
        for d, (dy, dx) in enumerate(DIRECTIONS):

            @pl.when(exists(dy, dx) & (gz + s < nz))
            def _():
                halo_copy(s, d).wait_send()

    for s in (1, 2):

        @pl.when((gz > 0) & (gz + s - 1 < nz))
        def _():
            tile_copy(s, 1).wait_send()
            tile_copy(s, 2).wait_send()

    for dz in range(1, nz):
        col_copy(dz, gz).wait_send()
    for d, (dy, dx) in enumerate(DIRECTIONS):

        @pl.when(exists(dy, dx))
        def _():
            plane_total(d).wait_send()


def solution(mesh):
    sizes = tuple(mesh.shape[name] for name in ("gz", "gy", "gx"))
    f32, bf16 = jnp.float32, jnp.bfloat16
    column_table = column_tables()
    row_tab, left_tab = parity_tables()
    right_tab = right_inverse()
    constants = (column_table, row_tab, left_tab, right_tab)

    def body(images, tissue_mask):
        vmem = pl.BlockSpec(memory_space=pltpu.VMEM)
        anywhere = pl.BlockSpec(memory_space=pltpu.HBM)
        dma = pltpu.SemaphoreType.DMA
        return pl.pallas_call(
            functools.partial(kernel, sizes),
            out_shape=(
                jax.ShapeDtypeStruct((4, 1, 4, 4), f32),
                jax.ShapeDtypeStruct((2, 1, 4, 4), f32),
            ),
            in_specs=[anywhere] * 6,
            out_specs=(vmem, vmem),
            scratch_shapes=[
                pltpu.VMEM((3, 4, ROWS, LANES), bf16),
                pltpu.VMEM((3, STRIP, LANES), bf16),
                pltpu.VMEM(column_table.shape, bf16),
                pltpu.VMEM(row_tab.shape, bf16),
                pltpu.VMEM(left_tab.shape, bf16),
                pltpu.VMEM(right_tab.shape, bf16),
                pltpu.VMEM((3, 4, ROWS, LANES), f32),
                pltpu.VMEM((3, 4, ROWS, LANES), f32),
                pltpu.VMEM((3, 4, ROWS, LANES), f32),
                pltpu.VMEM((3, 4, ROWS, LANES), f32),
                pltpu.VMEM((4 * PATCH, 512), bf16),
                pltpu.VMEM((4 * PATCH, 512), bf16),
                pltpu.VMEM((3, 8, 176, 256), f32),
                pltpu.VMEM((3, 2, 16, 8, LANES), f32),
                pltpu.VMEM((8, LANES), f32),
                pltpu.VMEM((8, 1, LANES), f32),
                pltpu.VMEM((8, 8, 1, LANES), f32),
                pltpu.VMEM((1, TILE, TILE), bf16),
                pltpu.VMEM((1, 4, 4), jnp.int32),
                dma((6,)),
                dma((3, 8)),
                dma((3, 8)),
                dma((2, 2)),
                dma((2, 2)),
                dma((7,)),
                dma((7,)),
                dma((8,)),
                dma((8,)),
                pltpu.SemaphoreType.REGULAR,
                pltpu.SemaphoreType.REGULAR,
                pltpu.SemaphoreType.REGULAR,
            ],
            compiler_params=pltpu.CompilerParams(
                collective_id=0, has_side_effects=True, vmem_limit_bytes=32 * 1024 * 1024
            ),
        )(*[pltpu.with_memory_space_constraint(x, pltpu.HBM) for x in (images, tissue_mask, *[jnp.asarray(x) for x in constants])])

    return jax.shard_map(
        body,
        mesh=mesh,
        in_specs=(P("gz", "gy", "gx"), P("gz", "gy", "gx")),
        out_specs=(P(None, "gz", "gy", "gx"), P(None, "gz", "gy", "gx")),
        check_vma=False,
    )
```
